32 devices in a mesh: mesh: 8 (over z, y), planes: 4 (over x, core).
Axes of the slice: x: 2, y: 2, z: 4, core: 2. Of those that a mesh axis runs over, the one named last changes fastest.
Arguments:
- velocity: float32 [3, 256, 2496], P(None, 'planes', 'mesh'), may hold values from -1.5 to 1.5
- connect: int32 [49, 64], P(None, 'mesh'), may hold values from 0 to 324, as said below
- right_list: int32 [104], P('mesh'), may hold values from 0 to 311, as said below
- extents: float32 [2, 64], P(None, 'mesh'), may hold values from 0.005 to 0.0375
Outputs:
- new_velocity: float32 [3, 256, 2496], P(None, 'planes', 'mesh')
The draws below stay inside these ranges and needn't reach their ends.
Inputs may be any that keep to these rules, and one draw needn't show every extreme that they name: `connect`: each partition holds a conforming grid of 4 x 2 quadrilaterals of order 6 in a drawn order, with its own nodes numbered 0 to 311 in a drawn order; entry [7 j + i, e] is the local id of node (i, j) of element e; ids 312 + y name the nodes of the partition's first edge, which the previous partition along mesh (cyclically) lists in right_list at position y. `right_list`: part m holds, for y = 0 to 12, the local id of node y of partition m's last edge, shared with partition m + 1 (cyclically).
All inputs are finite; a program needn't handle non-finite values.
Results may differ from the reference program's by a relative error of at most 0.0003.
Values sent between devices are 32-bit elements; how exact they have to be, the bound alone decides.
No kernel may reach another device: no remote copies, remote signals or barrier semaphores. Data moves between devices by JAX's collectives and lax.ppermute only.
A program may use at most 64 MiB of HBM per device.

```python
import math
import jax
import jax.numpy as jnp
import numpy as np
from jax import lax

PLANES = 256
NODES_EL = 49
EX_DEV = 4
NEY = 2
ITERS = 4
MODES_DEV = 64
NB = 13
NO = 312
E_DEV = 8
ELEMS = 64
NODES = 2496
N_MESH = 8
N_PLANES = 4


def mesh_numbering(key):
    device_keys = jax.random.split(key, N_MESH)

    def one_partition(device_key):
        node_key, element_key = jax.random.split(device_key)
        node_order = jax.random.permutation(node_key, NO).astype(jnp.int32)
        element_order = jax.random.permutation(element_key, E_DEV).astype(jnp.int32)
        column_of = element_order // NEY
        row_of = element_order % NEY
        local_index = jnp.arange(NODES_EL, dtype=jnp.int32)
        node_column = 6 * column_of[None, :] + (local_index % 7)[:, None]
        node_row = 6 * row_of[None, :] + (local_index // 7)[:, None]
        structured = jnp.clip((node_column - 1) * NB + node_row, 0, NO - 1)
        node_ids = jnp.where(node_column == 0, NO + node_row, node_order[structured])
        edge_ids = node_order[(6 * EX_DEV - 1) * NB + jnp.arange(NB, dtype=jnp.int32)]
        return (node_ids.astype(jnp.int32), edge_ids.astype(jnp.int32))
    return jax.vmap(one_partition)(device_keys)


def draw_connect(key, part):
    node_ids, edge_ids = mesh_numbering(jax.random.fold_in(key, 17))
    return jnp.transpose(node_ids, (1, 0, 2)).reshape(NODES_EL, N_MESH * E_DEV)


def draw_right_list(key, part):
    node_ids, edge_ids = mesh_numbering(jax.random.fold_in(key, 17))
    return edge_ids.reshape(N_MESH * NB)


def draw_extents(key, part):
    device = (jnp.arange(ELEMS, dtype=jnp.int32) // E_DEV).astype(jnp.float32)
    grade = jnp.exp(device / max(N_MESH - 1, 1) * math.log(3.0))
    factor = jnp.exp(jax.random.uniform(key, (2, ELEMS), jnp.float32, 0.0, math.log(2.5)))
    stretch = jnp.stack([grade, jnp.ones_like(grade)])
    return (0.005 * factor * stretch).astype(jnp.float32)


def steps_of(rng, extent, cuts, low, top_value):
    def one(axis_at, blocks):
        draws = jax.random.uniform(jax.random.fold_in(jax.random.fold_in(rng, 6), axis_at), (blocks,), jnp.float32, low / len(cuts), top_value / len(cuts))
        return jnp.repeat(jnp.exp(draws), extent[axis_at] // blocks).reshape((-1,) + (1,) * (len(extent) - axis_at - 1))

    factor_of = one(*cuts[0])
    for cut in cuts[1:]:
        factor_of = factor_of * one(*cut)
    return factor_of


def gaussian(own_key, dims, deviation, bound, cuts=(), kind=jnp.bfloat16):
    drawn = jax.random.normal(own_key, dims, jnp.float32) * deviation
    if len(cuts) > 0:
        drawn = steps_of(own_key, dims, cuts, -0.22, 0.18) * drawn
    return jnp.clip(drawn, min=-bound, max=bound).astype(kind)


def setup_inputs(seed: int = 0) -> dict:
    key_of = jax.random.split(jax.random.key(seed), 5)
    velocity = gaussian(key_of[0], (3, PLANES, NODES), 0.25, 1.5, ((1, 4), (2, 8)), jnp.float32)
    connect = draw_connect(jax.random.fold_in(key_of[4], 71), 0)
    right_list = draw_right_list(jax.random.fold_in(key_of[4], 71), 0)
    extents = draw_extents(jax.random.fold_in(key_of[4], 71), 0)
    return {"velocity": velocity, "connect": connect, "right_list": right_list, "extents": extents}


highest = lax.Precision.HIGHEST
viscosity = 0.002
time_step = 3e-5
span_wave = 4.0


def legendre_six(points):
    previous = 0.0 * points + 1.0
    current = 1.0 * points
    for order in range(1, 6):
        following = ((2 * order + 1) * points * current - order * previous) / (order + 1)
        previous = current
        current = following
    return current


def gll_tables():
    degree = 6
    points = np.array([-1.0, -0.8302238962785670, -0.4688487934707142, 0.0,
                       0.4688487934707142, 0.8302238962785670, 1.0])
    values = legendre_six(points)
    weights = 2.0 / (degree * (degree + 1) * values ** 2)
    derivative = np.zeros((degree + 1, degree + 1))
    for row_index in range(degree + 1):
        for col_index in range(degree + 1):
            if row_index != col_index:
                derivative[row_index, col_index] = values[row_index] / (values[col_index] * (points[row_index] - points[col_index]))
    derivative[0, 0] = -degree * (degree + 1) / 4.0
    derivative[degree, degree] = degree * (degree + 1) / 4.0
    stiffness = derivative.T @ (weights[:, None] * derivative)
    identity = np.eye(degree + 1)
    weight_matrix = identity * weights[None, :]
    mass_weights = np.kron(weights, weights)
    entries = (np.kron(weight_matrix, stiffness), np.kron(stiffness, weight_matrix),
               mass_weights[:, None] * np.kron(identity, derivative),
               mass_weights[:, None] * np.kron(derivative, identity), mass_weights)
    return tuple(jnp.asarray(entry_table, jnp.float32) for entry_table in entries)


def fourier_tables(planes):
    plane_grid = np.arange(planes)
    synthesis = np.zeros((planes, planes))
    forward = np.zeros((planes, planes))
    synthesis[:, 0] = 1.0
    synthesis[:, 1] = np.cos(np.pi * plane_grid)
    forward[0] = 1.0 / planes
    forward[1] = np.cos(np.pi * plane_grid) / planes
    for wavenumber in range(1, planes // 2):
        phase_angle = 2.0 * np.pi * wavenumber * plane_grid / planes
        synthesis[:, 2 * wavenumber] = np.cos(phase_angle)
        synthesis[:, 2 * wavenumber + 1] = np.sin(phase_angle)
        forward[2 * wavenumber] = 2.0 * np.cos(phase_angle) / planes
        forward[2 * wavenumber + 1] = 2.0 * np.sin(phase_angle) / planes
    return jnp.asarray(synthesis, jnp.float32), jnp.asarray(forward, jnp.float32)


def mode_factors(first_mode, mode_count):
    index_list = first_mode + jnp.arange(mode_count, dtype=jnp.int32)
    wavenumber = jnp.where(index_list == 1, PLANES // 2, index_list // 2).astype(jnp.float32)
    helmholtz = 1.0 / (viscosity * time_step) + (span_wave * wavenumber) ** 2
    pair_waves = span_wave * (first_mode // 2 + jnp.arange(mode_count // 2, dtype=jnp.int32)).astype(jnp.float32)
    return helmholtz, pair_waves


def geometry(extents):
    length_along = extents[0]
    length_across = extents[1]
    return (length_across / length_along, length_along / length_across,
            length_along * length_across / 4.0, length_across / 2.0, length_along / 2.0)


def pair_products(physical):
    along_speed = physical[0]
    across_speed = physical[1]
    span_speed = physical[2]
    return jnp.stack([along_speed * along_speed, along_speed * across_speed, along_speed * span_speed,
                      across_speed * across_speed, across_speed * span_speed, span_speed * span_speed])


def span_derivative(values, pair_waves):
    shaped = values.reshape(values.shape[0], values.shape[1] // 2, 2, values.shape[2], values.shape[3])
    turned = jnp.stack([shaped[:, :, 1], -shaped[:, :, 0]], axis=2) * pair_waves[None, :, None, None, None]
    return turned.reshape(values.shape)


def operator_elements(local_values, tables, shape_terms, helmholtz):
    stiff_along, stiff_across, slope_along, slope_across, mass_weights = tables
    ratio_along, ratio_across, mass_factor, length_along, length_across = shape_terms
    along_part = jnp.einsum('lk,cqke->cqle', stiff_along, local_values, precision=highest)
    across_part = jnp.einsum('lk,cqke->cqle', stiff_across, local_values, precision=highest)
    mass_full = mass_weights[:, None] * mass_factor[None, :]
    return ratio_along * along_part + ratio_across * across_part + helmholtz[None, :, None, None] * mass_full * local_values


def source_elements(speed_values, product_values, tables, shape_terms, helmholtz, pair_waves):
    stiff_along, stiff_across, slope_along, slope_across, mass_weights = tables
    ratio_along, ratio_across, mass_factor, length_along, length_across = shape_terms
    mass_full = mass_weights[:, None] * mass_factor[None, :]
    along_flux = product_values[0:3]
    across_flux = jnp.stack([product_values[1], product_values[3], product_values[4]])
    span_flux = jnp.stack([product_values[2], product_values[4], product_values[5]])
    advection = length_along * jnp.einsum('lk,cqke->cqle', slope_along, along_flux, precision=highest)
    advection = advection + length_across * jnp.einsum('lk,cqke->cqle', slope_across, across_flux, precision=highest)
    advection = advection + mass_full * span_derivative(span_flux, pair_waves)
    inverse_step = 1.0 / (viscosity * time_step)
    return inverse_step * mass_full * speed_values - operator_elements(speed_values, tables, shape_terms, helmholtz) - advection / viscosity


def reference(velocity, connect, right_list, extents):
    tables = gll_tables()
    synthesis, forward = fourier_tables(PLANES)
    shape_terms = geometry(extents)
    element_device = jnp.arange(ELEMS, dtype=jnp.int32) // E_DEV
    previous = (element_device + N_MESH - 1) % N_MESH
    edge_lists = right_list.reshape(N_MESH, NB)
    ghost_row = jnp.clip(connect - NO, 0, NB - 1).astype(jnp.int32)
    previous_full = jnp.broadcast_to(previous[None, :], connect.shape).astype(jnp.int32)
    ghost_ids = previous_full * NO + edge_lists[previous_full, ghost_row]
    global_conn = jnp.where(connect < NO, element_device[None, :] * NO + connect, ghost_ids).astype(jnp.int32)
    flat_conn = global_conn.reshape(-1)

    def transform_block(block_index):
        node_piece = lax.dynamic_slice_in_dim(velocity, (block_index * NO).astype(jnp.int32), NO, 2)
        physical = jnp.einsum('jq,cqn->cjn', synthesis, node_piece, precision=highest)
        return jnp.einsum('qj,fjn->fqn', forward, pair_products(physical), precision=highest)

    product_hat = lax.map(transform_block, jnp.arange(N_MESH, dtype=jnp.int32))

    def assemble(element_terms):
        summed = jnp.zeros((3, MODES_DEV, NODES), jnp.float32)
        return summed.at[:, :, flat_conn].add(element_terms.reshape(3, MODES_DEV, -1))

    def gather_nodes(field):
        return jnp.take(field, flat_conn, axis=2).reshape(field.shape[0], MODES_DEV, NODES_EL, ELEMS)

    results = []
    for plane_block in range(N_PLANES):
        first_mode = plane_block * MODES_DEV
        helmholtz, pair_waves = mode_factors(first_mode, MODES_DEV)
        speeds = velocity[:, first_mode:first_mode + MODES_DEV, :]
        fluxes = jnp.transpose(product_hat[:, :, first_mode:first_mode + MODES_DEV, :], (1, 2, 0, 3)).reshape(6, MODES_DEV, NODES)
        residual = assemble(source_elements(gather_nodes(speeds), gather_nodes(fluxes), tables, shape_terms, helmholtz, pair_waves))
        solution = speeds
        direction = residual
        norm_now = jnp.sum(residual * residual, axis=2)
        for iteration in range(ITERS):
            operated = assemble(operator_elements(gather_nodes(direction), tables, shape_terms, helmholtz))
            step_size = (norm_now / jnp.sum(direction * operated, axis=2))[:, :, None]
            solution = solution + step_size * direction
            residual = residual - step_size * operated
            norm_next = jnp.sum(residual * residual, axis=2)
            direction = residual + (norm_next / norm_now)[:, :, None] * direction
            norm_now = norm_next
        results.append(solution)
    return jnp.concatenate(results, axis=1)
```

```python
import functools

import jax
import jax.numpy as jnp
import numpy as np
from jax import lax
from jax.experimental import pallas as pl
from jax.experimental.pallas import tpu as pltpu
from jax.sharding import PartitionSpec as P

PLANES = 256
ITERS = 4
SIDE = 7
ROWS = 13
COLS = 4
GRID = SIDE * ROWS
EXTRA = GRID
LANES = 128

highest = lax.Precision.HIGHEST
viscosity = 0.002
time_step = 3e-05
span_wave = 4.0
inverse_step = 1.0 / (viscosity * time_step)


def legendre_six(points):
    previous = 0.0 * points + 1.0
    current = 1.0 * points
    for order in range(1, 6):
        following = ((2 * order + 1) * points * current - order * previous) / (order + 1)
        previous = current
        current = following
    return current


def gll_one_d():
    degree = 6
    points = np.array(
        [
            -1.0,
            -0.830223896278567,
            -0.4688487934707142,
            0.0,
            0.4688487934707142,
            0.830223896278567,
            1.0,
        ]
    )
    values = legendre_six(points)
    weights = 2.0 / (degree * (degree + 1) * values**2)
    derivative = np.zeros((degree + 1, degree + 1))
    for row_index in range(degree + 1):
        for col_index in range(degree + 1):
            if row_index != col_index:
                derivative[row_index, col_index] = values[row_index] / (
                    values[col_index] * (points[row_index] - points[col_index])
                )
    derivative[0, 0] = -degree * (degree + 1) / 4.0
    derivative[degree, degree] = degree * (degree + 1) / 4.0
    stiffness = derivative.T @ (weights[:, None] * derivative)
    return weights, derivative, stiffness


def element_tables():
    weights, derivative, stiffness = gll_one_d()
    identity = np.eye(SIDE)
    mass_weights = np.kron(weights, weights)
    return (
        np.kron(np.diag(weights), stiffness),
        np.kron(stiffness, np.diag(weights)),
        mass_weights[:, None] * np.kron(identity, derivative),
        mass_weights[:, None] * np.kron(derivative, identity),
        mass_weights,
    )


def fourier_tables(planes):
    plane_grid = np.arange(planes)
    synthesis = np.zeros((planes, planes))
    forward = np.zeros((planes, planes))
    synthesis[:, 0] = 1.0
    synthesis[:, 1] = np.cos(np.pi * plane_grid)
    forward[0] = 1.0 / planes
    forward[1] = np.cos(np.pi * plane_grid) / planes
    for wavenumber in range(1, planes // 2):
        phase_angle = 2.0 * np.pi * wavenumber * plane_grid / planes
        synthesis[:, 2 * wavenumber] = np.cos(phase_angle)
        synthesis[:, 2 * wavenumber + 1] = np.sin(phase_angle)
        forward[2 * wavenumber] = 2.0 * np.cos(phase_angle) / planes
        forward[2 * wavenumber + 1] = 2.0 * np.sin(phase_angle) / planes
    return synthesis, forward


def span_forward(forward):
    turned = np.zeros_like(forward)
    for wavenumber in range(1, forward.shape[0] // 2):
        turned[2 * wavenumber] = span_wave * wavenumber * forward[2 * wavenumber + 1]
        turned[2 * wavenumber + 1] = -span_wave * wavenumber * forward[2 * wavenumber]
    return turned


def two_parts(table):
    table = np.asarray(table, np.float32)
    high = table.astype(jnp.bfloat16)
    low = (table - high.astype(np.float32)).astype(jnp.bfloat16)
    return high, low


def placement(row, skip_shared):
    table = np.zeros((SIDE * SIDE, LANES))
    for j in range(SIDE):
        if skip_shared and row == 1 and j == 0:
            continue
        for i in range(SIDE):
            table[SIDE * j + i, ROWS * i + 6 * row + j] = 1.0
    return table


def column_tables():
    stiff_along, stiff_across, slope_along, slope_across, mass_weights = element_tables()
    matrices = []
    for table in (slope_along, slope_across, stiff_along, stiff_across):
        for row in range(2):
            place = placement(row, False)
            matrices.append(place.T @ table.T @ place)
    masses = [mass_weights @ placement(row, False) for row in range(2)]
    return np.stack(matrices).astype(np.float32), np.stack(masses).astype(np.float32)


def split_two(value):
    high = value.astype(jnp.bfloat16)
    low = (value - high.astype(jnp.float32)).astype(jnp.bfloat16)
    return high, low


def split_three(value):
    high = value.astype(jnp.bfloat16)
    rest = value - high.astype(jnp.float32)
    middle = rest.astype(jnp.bfloat16)
    low = (rest - middle.astype(jnp.float32)).astype(jnp.bfloat16)
    return high, middle, low


def dot(left, right):
    return jnp.dot(left, right, preferred_element_type=jnp.float32)


def dot_rows(left, right):
    return lax.dot_general(
        left, right, (((1,), (1,)), ((), ())), preferred_element_type=jnp.float32
    )


def dot_split(left, right):
    return dot(left[0], right[0]) + (dot(left[0], right[1]) + dot(left[1], right[0]))


def one_hot(ids_row, count):
    rows = lax.broadcasted_iota(jnp.int32, (count, LANES), 0)
    return jnp.where(rows == ids_row, 1.0, 0.0).astype(jnp.bfloat16)


def gather_kernel(
    plane_ref, velocity_ref, connect_ref, edge_ref, extents_ref, place_ref,
    column_ref, edge_out_ref, ids_ref, extents_out_ref,
):
    own_nodes = velocity_ref.shape[1]
    element_ids = connect_ref[...].astype(jnp.float32)
    first_corner = element_ids[0:1, :]
    last_corner = element_ids[SIDE - 1 : SIDE, :]
    lane = lax.broadcasted_iota(jnp.int32, (1, LANES), 1)
    picked = [
        jnp.where(first_corner == float(own_nodes + 6 * row), 1.0, 0.0) for row in range(2)
    ]
    parts = split_three(velocity_ref[...])
    ids_ref[...] = jnp.full(ids_ref.shape, -1, jnp.int32)
    held = [jnp.zeros((1, 1), jnp.float32) for _ in range(4)]
    plane = plane_ref[0]
    for column in range(COLS):
        ids = jnp.zeros((1, LANES), jnp.float32)
        for row in range(2):
            mine = jnp.sum(element_ids * picked[row], axis=1, keepdims=True)
            ids = ids + jnp.sum(mine * place_ref[row], axis=0, keepdims=True)
            for axis in range(2):
                length = jnp.sum(
                    extents_ref[axis : axis + 1, :] * picked[row], axis=1, keepdims=True
                )
                at = 2 * axis + row
                held[at] = held[at] + jnp.where(plane == column, 1.0, 0.0) * length
            if column < COLS - 1:
                corner = jnp.sum(last_corner * picked[row], axis=1, keepdims=True)
                picked[row] = jnp.where(first_corner == corner, 1.0, 0.0)
        ids = jnp.where(lane < GRID, ids.astype(jnp.int32), -1)
        ids_ref[column : column + 1, :] = jnp.where(lane < ROWS, -1, ids)
        chosen = one_hot(ids, own_nodes)
        column_ref[column] = (dot(parts[2], chosen) + dot(parts[1], chosen)) + dot(parts[0], chosen)
    for at in range(4):
        extents_out_ref[at : at + 1, :] = jnp.broadcast_to(held[at], (1, LANES))
    extents_out_ref[4:8, :] = jnp.zeros((4, LANES), jnp.float32)
    at_edge = edge_ref[...] == lax.broadcasted_iota(jnp.int32, (16, own_nodes), 1)
    chosen = jnp.where(at_edge, 1.0, 0.0).astype(jnp.bfloat16)
    edge_out_ref[...] = (dot_rows(chosen, parts[2]) + dot_rows(chosen, parts[1])) + dot_rows(
        chosen, parts[0]
    )


def residual_kernel(
    modes, column_ref, ghost_a, ghost_b, ghost_c, ghost_d, extents_ref,
    synthesis_ref, forward_ref, plane_ref, mass_ref, out_ref,
):
    planes = PLANES
    groups = planes // modes
    ghosts = [ghost[...].T for ghost in (ghost_a, ghost_b, ghost_c, ghost_d)]
    hx = [extents_ref[0:1, :], extents_ref[1:2, :]]
    hy = [extents_ref[2:3, :], extents_ref[3:4, :]]
    lane = lax.broadcasted_iota(jnp.int32, (1, LANES), 1)
    mass = sum((hx[r] * hy[r] / 4.0) * mass_ref[r : r + 1, :] for r in range(2))
    along = sum((hy[r] / 2.0) * plane_ref[r] for r in range(2))
    across = sum((hx[r] / 2.0) * plane_ref[2 + r] for r in range(2))
    stiff = sum(
        (hy[r] / hx[r]) * plane_ref[4 + r] + (hx[r] / hy[r]) * plane_ref[6 + r] for r in range(2)
    )
    in_plane = split_two(jnp.concatenate([along, across, viscosity * stiff], axis=0))
    synthesis = (synthesis_ref[0], synthesis_ref[1])
    forward = (forward_ref[0], forward_ref[1])
    speeds = []
    fields = []
    for c in range(3):
        pieces = []
        for p in range(groups):
            piece = column_ref[p, c * modes : (c + 1) * modes, :]
            edge = ghosts[p][c * modes : (c + 1) * modes, :]
            edge = jnp.concatenate(
                [edge, jnp.zeros((modes, LANES - edge.shape[1]), jnp.float32)], axis=1
            )
            pieces.append(piece + edge)
        speeds.append(jnp.concatenate(pieces, axis=0))
        fields.append(dot_split(synthesis, split_two(speeds[c])))
    mode = lax.broadcasted_iota(jnp.int32, (planes, LANES), 0)
    wave = span_wave * jnp.where(mode == 1, planes // 2, mode // 2).astype(jnp.float32)
    carried = jnp.zeros((1, LANES), jnp.float32)
    for at, value in enumerate((hx[0], hx[1], hy[0], hy[1])):
        carried = carried + jnp.where(lane == EXTRA + at, value, 0.0)
    blocks = planes // 8
    per_group = modes // 8
    for c in range(3):
        flux = jnp.concatenate([fields[0] * fields[c], fields[1] * fields[c], fields[c]], axis=1)
        divergence = dot_split(split_two(flux), in_plane)
        span = mass * (fields[2] * fields[c])
        stacked = split_two(jnp.concatenate([divergence, span], axis=0))
        result = dot_split(forward, stacked) - (wave * wave) * (mass * speeds[c]) + carried
        for block in range(blocks):
            target = (block % per_group) * groups + block // per_group
            out_ref[target, 8 * c : 8 * c + 8, :] = result[8 * block : 8 * block + 8, :]


def apply_line(stiffness, values):
    even = [values[k] + values[6 - k] for k in range(3)] + [values[3]]
    odd = [values[k] - values[6 - k] for k in range(3)]
    result = [None] * 7
    for i in range(4):
        total = float(stiffness[i, 3]) * even[3]
        for k in range(3):
            total = total + float((stiffness[i, k] + stiffness[i, 6 - k]) / 2) * even[k]
        if i == 3:
            result[3] = total
            continue
        other = float((stiffness[i, 0] - stiffness[i, 6]) / 2) * odd[0]
        for k in range(1, 3):
            other = other + float((stiffness[i, k] - stiffness[i, 6 - k]) / 2) * odd[k]
        result[i] = total + other
        result[6 - i] = total - other
    return result


def cg_kernel(columns, first_ref, in_ref, out_ref, grid_ref, rest_ref, way_ref, image_ref, sum_ref):
    weights, _, stiffness = gll_one_d()
    lane = lax.broadcasted_iota(jnp.int32, (8, LANES), 1)
    at = lane % columns

    def node(i, y):
        start = (ROWS * i + y) * 8
        return slice(start, start + 8)

    def from_next(value):
        return jnp.where(
            at == columns - 1,
            pltpu.roll(value, columns - 1, 1),
            pltpu.roll(value, LANES - 1, 1),
        )

    def from_previous(value):
        return jnp.where(
            at == 0,
            pltpu.roll(value, LANES - columns + 1, 1),
            pltpu.roll(value, 1, 1),
        )

    def over_columns(value):
        step = columns // 2
        while step:
            value = value + jnp.where(
                (lane // step) % 2 == 0,
                pltpu.roll(value, LANES - step, 1),
                pltpu.roll(value, step, 1),
            )
            step //= 2
        return value

    blank = jnp.zeros((LANES - 3 * columns, LANES), jnp.float32)
    for mode in range(8):
        rows = [
            in_ref[pl.ds(8 * c + mode, columns, stride=24), :] for c in range(3)
        ]
        turned = jnp.concatenate(rows + [blank], axis=0).T
        grid_ref[pl.ds(mode, 96, stride=8), :] = turned[:96, :]

    used = lane < 3 * columns

    def extent(which):
        start = (EXTRA + which) * 8
        return jnp.where(used, grid_ref[start : start + 8, :], 1.0)

    hx = [extent(0), extent(1)]
    hy = [extent(2), extent(3)]
    mode = first_ref[0] + lax.broadcasted_iota(jnp.int32, (8, LANES), 0)
    wave = span_wave * jnp.where(mode == 1, PLANES // 2, mode // 2).astype(jnp.float32)
    helmholtz = inverse_step + wave * wave
    ratio_along = [hy[r] / hx[r] for r in range(2)]
    ratio_across = [hx[r] / hy[r] for r in range(2)]
    mass = [helmholtz * (hx[r] * hy[r] / 4.0) for r in range(2)]

    def over_rows(pair, y):
        if y < 6:
            return float(weights[y]) * pair[0]
        if y > 6:
            return float(weights[y - 6]) * pair[1]
        return float(weights[6]) * pair[0] + float(weights[0]) * pair[1]

    def shared(pair):
        return [
            float(weights[0]) * value + float(weights[6]) * from_previous(value) for value in pair
        ]

    mass_shared = shared(mass)
    across_shared = shared(ratio_across)

    total = jnp.zeros((8, LANES), jnp.float32)
    for y in range(ROWS):
        for i in range(6):
            value = grid_ref[node(i, y), :]
            if i == 0:
                value = value + from_previous(grid_ref[node(6, y), :])
            rest_ref[node(i, y), :] = value
            way_ref[node(i, y), :] = value
            sum_ref[node(i, y), :] = jnp.zeros((8, LANES), jnp.float32)
            total = total + value * value
    rest_norm = over_columns(total)

    def apply():
        for y in range(ROWS):
            values = [way_ref[node(i, y), :] for i in range(6)]
            values.append(from_next(values[0]))
            lines = apply_line(stiffness, values)
            along = over_rows(ratio_along, y)
            lines = [along * line for line in lines]
            lines[0] = lines[0] + from_previous(lines[6])
            inner = over_rows(mass, y)
            outer = over_rows(mass_shared, y)
            for i in range(6):
                weight = outer if i == 0 else float(weights[i]) * inner
                image_ref[node(i, y), :] = lines[i] + weight * values[i]
        total = jnp.zeros((8, LANES), jnp.float32)
        for i in range(6):
            values = [way_ref[node(i, y), :] for y in range(ROWS)]
            lower = apply_line(stiffness, values[:7])
            upper = apply_line(stiffness, values[6:])
            if i == 0:
                scale = across_shared
            else:
                scale = [float(weights[i]) * value for value in ratio_across]
            lower = [scale[0] * value for value in lower]
            upper = [scale[1] * value for value in upper]
            lines = lower[:6] + [lower[6] + upper[0]] + upper[1:]
            for y in range(ROWS):
                image = image_ref[node(i, y), :] + lines[y]
                image_ref[node(i, y), :] = image
                total = total + values[y] * image
        return over_columns(total)

    def step(_, rest_norm):
        size = rest_norm / apply()
        total = jnp.zeros((8, LANES), jnp.float32)
        for y in range(ROWS):
            for i in range(6):
                at_node = node(i, y)
                sum_ref[at_node, :] = sum_ref[at_node, :] + size * way_ref[at_node, :]
                rest = rest_ref[at_node, :] - size * image_ref[at_node, :]
                rest_ref[at_node, :] = rest
                total = total + rest * rest
        following = over_columns(total)
        turn = following / rest_norm
        for y in range(ROWS):
            for i in range(6):
                at_node = node(i, y)
                way_ref[at_node, :] = rest_ref[at_node, :] + turn * way_ref[at_node, :]
        return following

    rest_norm = lax.fori_loop(0, ITERS - 1, step, rest_norm)
    size = rest_norm / apply()
    zero = jnp.zeros((8, LANES), jnp.float32)
    for y in range(ROWS):
        grid_ref[node(0, y), :] = zero
        for i in range(6):
            value = sum_ref[node(i, y), :] + size * way_ref[node(i, y), :]
            if i == 0:
                grid_ref[node(6, y), :] = from_next(value)
            else:
                grid_ref[node(i, y), :] = value
    for left in range(GRID, 96):
        grid_ref[left * 8 : left * 8 + 8, :] = zero
    blank = jnp.zeros((LANES - 96, LANES), jnp.float32)
    for mode in range(8):
        turned = jnp.concatenate([grid_ref[pl.ds(mode, 96, stride=8), :], blank], axis=0).T
        for c in range(3):
            out_ref[pl.ds(8 * c + mode, columns, stride=24), :] = turned[
                c * columns : (c + 1) * columns, :
            ]


def scatter_kernel(velocity_ref, change_ref, ids_ref, out_ref):
    own_nodes = velocity_ref.shape[1]
    sources = change_ref.shape[0]
    pieces = []
    chosen = []
    for column in range(COLS):
        start = 24 * column
        pieces.append(
            jnp.concatenate(
                [
                    change_ref[m, start + 8 * c : start + 8 * c + 8, :]
                    for c in range(3)
                    for m in range(sources)
                ],
                axis=0,
            )
        )
        chosen.append(one_hot(ids_ref[column : column + 1, :], own_nodes))
    parts = split_three(jnp.concatenate(pieces, axis=1))
    chosen = jnp.concatenate(chosen, axis=1)
    change = (dot_rows(parts[2], chosen) + dot_rows(parts[1], chosen)) + dot_rows(parts[0], chosen)
    out_ref[...] = velocity_ref[...] + change


def call(kernel, out_shape, scratch=(), scalars=0, operands=0):
    smem = [pl.BlockSpec(memory_space=pltpu.SMEM)] * scalars
    vmem = [pl.BlockSpec(memory_space=pltpu.VMEM)] * operands
    many = isinstance(out_shape, tuple)
    out_spec = pl.BlockSpec(memory_space=pltpu.VMEM)
    return pl.pallas_call(
        kernel,
        out_shape=out_shape,
        in_specs=smem + vmem,
        out_specs=(out_spec,) * len(out_shape) if many else out_spec,
        scratch_shapes=list(scratch),
        compiler_params=pltpu.CompilerParams(vmem_limit_bytes=32 * 2**20),
    )


def transposed(velocity, connect, right_list, extents):
    components, modes, own_nodes = velocity.shape
    groups = lax.axis_size("planes")
    parts = lax.axis_size("mesh")
    plane = lax.axis_index("planes")
    part = lax.axis_index("mesh")
    rows = components * modes
    columns = parts * COLS
    synthesis, forward = fourier_tables(PLANES)
    both = np.concatenate([forward, span_forward(forward)], axis=1) * (-1.0 / viscosity)
    matrices, masses = column_tables()
    place = np.stack([placement(row, True) for row in range(2)]).astype(np.float32)
    flat = velocity.reshape(rows, own_nodes)
    edge_ids = jnp.pad(right_list, (0, 16 - ROWS), constant_values=-1).reshape(16, 1)
    f32 = jnp.float32
    column, edge, ids, column_extents = call(
        gather_kernel,
        (
            jax.ShapeDtypeStruct((COLS, rows, LANES), f32),
            jax.ShapeDtypeStruct((16, rows), f32),
            jax.ShapeDtypeStruct((8, LANES), jnp.int32),
            jax.ShapeDtypeStruct((8, LANES), f32),
        ),
        scalars=1,
        operands=5,
    )(plane.reshape(1), flat, connect, edge_ids, extents, jnp.asarray(place))
    ghosts = [
        lax.ppermute(
            edge,
            ("mesh", "planes"),
            [(m * groups + p, (m + 1) % parts * groups) for m in range(parts)],
        )
        for p in range(groups)
    ]
    column = lax.all_to_all(column, "planes", split_axis=0, concat_axis=0, tiled=True)
    residual = call(
        functools.partial(residual_kernel, modes),
        jax.ShapeDtypeStruct((groups * parts, components * 8, LANES), f32),
        operands=10,
    )(
        column,
        *ghosts,
        column_extents,
        jnp.asarray(np.stack(two_parts(synthesis))),
        jnp.asarray(np.stack(two_parts(both))),
        jnp.asarray(matrices),
        jnp.asarray(masses),
    )
    residual = lax.all_to_all(
        residual, ("mesh", "planes"), split_axis=0, concat_axis=0, tiled=True
    )
    held = pltpu.VMEM((96 * 8, LANES), f32)
    change = call(
        functools.partial(cg_kernel, columns),
        jax.ShapeDtypeStruct((columns * components * 8, LANES), f32),
        scratch=(held,) * 5,
        scalars=1,
        operands=1,
    )((plane * modes + part * 8).reshape(1), residual.reshape(columns * components * 8, LANES))
    change = lax.all_to_all(
        change.reshape(parts, COLS * components * 8, LANES),
        "mesh",
        split_axis=0,
        concat_axis=0,
        tiled=True,
    )
    result = call(
        scatter_kernel,
        jax.ShapeDtypeStruct((rows, own_nodes), f32),
        operands=3,
    )(flat, change, ids)
    return result.reshape(velocity.shape)


def from_behind(value, axis, by):
    peers = lax.axis_size(axis)
    return lax.ppermute(value, axis, [(i, (i + by) % peers) for i in range(peers)])


def partitioned(velocity, connect, right_list, extents):
    components, modes, own_nodes = velocity.shape
    edge_count = right_list.shape[0]
    first_mode = lax.axis_index("planes") * modes
    tables = [jnp.asarray(table, jnp.float32) for table in element_tables()]
    stiff_along, stiff_across, slope_along, slope_across, mass_weights = tables
    synthesis, forward = (jnp.asarray(t, jnp.float32) for t in fourier_tables(PLANES))
    hx, hy = extents[0], extents[1]
    mass_full = mass_weights[:, None] * (hx * hy / 4.0)[None, :]
    index_list = first_mode + jnp.arange(modes, dtype=jnp.int32)
    wave = span_wave * jnp.where(index_list == 1, PLANES // 2, index_list // 2).astype(jnp.float32)
    wave = wave[None, :, None, None]
    helmholtz = inverse_step + wave * wave
    locals_ = jnp.arange(own_nodes + edge_count, dtype=jnp.int32)
    chosen = (locals_[:, None, None] == connect[None]).astype(jnp.float32)
    at_edge = (locals_[:own_nodes, None] == right_list[None]).astype(jnp.float32)

    def contract(spec, *operands):
        return jnp.einsum(spec, *operands, precision=highest)

    physical = contract(
        "jq,cqn->cjn",
        synthesis,
        lax.all_to_all(velocity, "planes", split_axis=2, concat_axis=1, tiled=True),
    )
    pairs = ((0, 0), (0, 1), (0, 2), (1, 1), (1, 2), (2, 2))
    products = jnp.stack([physical[a] * physical[b] for a, b in pairs])
    product_hat = lax.all_to_all(
        contract("qj,fjn->fqn", forward, products), "planes", split_axis=1, concat_axis=2, tiled=True
    )

    def spread(fields):
        ghosts = from_behind(contract("cqn,ny->cqy", fields, at_edge), "mesh", 1)
        return contract("cqn,nke->cqke", jnp.concatenate([fields, ghosts], axis=2), chosen)

    def assemble(terms):
        summed = contract("cqke,nke->cqn", terms, chosen)
        returned = from_behind(summed[:, :, own_nodes:], "mesh", -1)
        return summed[:, :, :own_nodes] + contract("cqy,ny->cqn", returned, at_edge)

    def stiffness(values):
        return (hy / hx) * contract("lk,cqke->cqle", stiff_along, values) + (hx / hy) * contract(
            "lk,cqke->cqle", stiff_across, values
        )

    def dots(left, right):
        return lax.psum(jnp.sum(left * right, axis=2), "mesh")

    values = spread(jnp.concatenate([velocity, product_hat], axis=0))
    speeds, along = values[0:3], values[3:6]
    across = jnp.stack([values[4], values[6], values[7]])
    span = jnp.stack([values[5], values[7], values[8]])
    shaped = span.reshape(span.shape[0], modes // 2, 2, *span.shape[2:])
    turned = jnp.stack([shaped[:, :, 1], -shaped[:, :, 0]], axis=2).reshape(span.shape)
    pair_wave = span_wave * (index_list // 2).astype(jnp.float32)[None, :, None, None]
    advection = (hy / 2.0) * contract("lk,cqke->cqle", slope_along, along)
    advection = advection + (hx / 2.0) * contract("lk,cqke->cqle", slope_across, across)
    advection = advection + mass_full * (pair_wave * turned)
    residual = assemble(
        -(wave * wave) * mass_full * speeds - stiffness(speeds) - advection / viscosity
    )
    solution = velocity
    direction = residual
    norm_now = dots(residual, residual)
    for _ in range(ITERS):
        values = spread(direction)
        operated = assemble(stiffness(values) + helmholtz * mass_full * values)
        step_size = (norm_now / dots(direction, operated))[:, :, None]
        solution = solution + step_size * direction
        residual = residual - step_size * operated
        norm_next = dots(residual, residual)
        direction = residual + (norm_next / norm_now)[:, :, None] * direction
        norm_now = norm_next
    return solution


def on_device(velocity, connect, right_list, extents):
    groups = lax.axis_size("planes")
    parts = lax.axis_size("mesh")
    modes = velocity.shape[1]
    fits = groups == COLS and modes == 8 * parts and 3 * parts * COLS <= LANES
    step = transposed if fits else partitioned
    return step(velocity, connect, right_list, extents)


def solution(mesh):
    placed = (P(None, "planes", "mesh"), P(None, "mesh"), P("mesh"), P(None, "mesh"))
    return jax.shard_map(
        on_device, mesh=mesh, in_specs=placed, out_specs=P(None, "planes", "mesh"), check_vma=False
    )
```

```python
import functools

import jax
import jax.numpy as jnp
import numpy as np
from jax import lax
from jax.experimental import pallas as pl
from jax.experimental.pallas import tpu as pltpu
from jax.sharding import PartitionSpec as P

PLANES = 256
ITERS = 4
SIDE = 7
ROWS = 13
COLS = 4
GRID = SIDE * ROWS
ONWARD_FLUX = GRID
ONWARD_SPEED = GRID + ROWS
EXTRA = GRID + 2 * ROWS
LANES = 128
OWNED = GRID - ROWS
THIRD = OWNED // 3

highest = lax.Precision.HIGHEST
viscosity = 0.002
time_step = 3e-05
span_wave = 4.0
inverse_step = 1.0 / (viscosity * time_step)


def legendre_six(points):
    previous = 0.0 * points + 1.0
    current = 1.0 * points
    for order in range(1, 6):
        following = ((2 * order + 1) * points * current - order * previous) / (order + 1)
        previous = current
        current = following
    return current


def gll_one_d():
    degree = 6
    points = np.array(
        [
            -1.0,
            -0.830223896278567,
            -0.4688487934707142,
            0.0,
            0.4688487934707142,
            0.830223896278567,
            1.0,
        ]
    )
    values = legendre_six(points)
    weights = 2.0 / (degree * (degree + 1) * values**2)
    derivative = np.zeros((degree + 1, degree + 1))
    for row_index in range(degree + 1):
        for col_index in range(degree + 1):
            if row_index != col_index:
                derivative[row_index, col_index] = values[row_index] / (
                    values[col_index] * (points[row_index] - points[col_index])
                )
    derivative[0, 0] = -degree * (degree + 1) / 4.0
    derivative[degree, degree] = degree * (degree + 1) / 4.0
    stiffness = derivative.T @ (weights[:, None] * derivative)
    return weights, derivative, stiffness


def element_tables():
    weights, derivative, stiffness = gll_one_d()
    identity = np.eye(SIDE)
    mass_weights = np.kron(weights, weights)
    return (
        np.kron(np.diag(weights), stiffness),
        np.kron(stiffness, np.diag(weights)),
        mass_weights[:, None] * np.kron(identity, derivative),
        mass_weights[:, None] * np.kron(derivative, identity),
        mass_weights,
    )


def fourier_tables(planes):
    plane_grid = np.arange(planes)
    synthesis = np.zeros((planes, planes))
    forward = np.zeros((planes, planes))
    synthesis[:, 0] = 1.0
    synthesis[:, 1] = np.cos(np.pi * plane_grid)
    forward[0] = 1.0 / planes
    forward[1] = np.cos(np.pi * plane_grid) / planes
    for wavenumber in range(1, planes // 2):
        phase_angle = 2.0 * np.pi * wavenumber * plane_grid / planes
        synthesis[:, 2 * wavenumber] = np.cos(phase_angle)
        synthesis[:, 2 * wavenumber + 1] = np.sin(phase_angle)
        forward[2 * wavenumber] = 2.0 * np.cos(phase_angle) / planes
        forward[2 * wavenumber + 1] = 2.0 * np.sin(phase_angle) / planes
    return synthesis, forward


def span_forward(forward):
    turned = np.zeros_like(forward)
    for wavenumber in range(1, forward.shape[0] // 2):
        turned[2 * wavenumber] = span_wave * wavenumber * forward[2 * wavenumber + 1]
        turned[2 * wavenumber + 1] = -span_wave * wavenumber * forward[2 * wavenumber]
    return turned


def two_parts(table):
    table = np.asarray(table, np.float32)
    high = table.astype(jnp.bfloat16)
    low = (table - high.astype(np.float32)).astype(jnp.bfloat16)
    return high, low


def placement(row, skip_shared):
    table = np.zeros((SIDE * SIDE, LANES))
    for j in range(SIDE):
        if skip_shared and row == 1 and j == 0:
            continue
        for i in range(SIDE):
            table[SIDE * j + i, ROWS * i + 6 * row + j] = 1.0
    return table


def column_tables():
    weights, _, _ = gll_one_d()
    stiff_along, stiff_across, slope_along, slope_across, mass_weights = element_tables()
    owned = np.arange(LANES)
    owned = (owned >= ROWS) & (owned < GRID)
    matrices = []
    for table, onward in (
        (slope_along, ONWARD_FLUX),
        (slope_across, None),
        (stiff_along, ONWARD_SPEED),
        (stiff_across, None),
    ):
        for row in range(2):
            place = placement(row, False)
            matrix = (place.T @ table.T @ place) * owned[:, None]
            if onward is not None:
                for j in range(SIDE):
                    y = 6 * row + j
                    matrix[6 * ROWS + y, onward + y] = weights[j]
            matrices.append(matrix)
    masses = [(mass_weights @ placement(row, False)) * owned for row in range(2)]
    return np.stack(matrices).astype(np.float32), np.stack(masses).astype(np.float32)


def split_two(value):
    high = value.astype(jnp.bfloat16)
    low = (value - high.astype(jnp.float32)).astype(jnp.bfloat16)
    return high, low


def split_three(value):
    high = value.astype(jnp.bfloat16)
    rest = value - high.astype(jnp.float32)
    middle = rest.astype(jnp.bfloat16)
    low = (rest - middle.astype(jnp.float32)).astype(jnp.bfloat16)
    return high, middle, low


def dot(left, right):
    return jnp.dot(left, right, preferred_element_type=jnp.float32)


def dot_rows(left, right):
    return lax.dot_general(
        left, right, (((1,), (1,)), ((), ())), preferred_element_type=jnp.float32
    )


def dot_split(left, right):
    return dot(left[0], right[0]) + (dot(left[0], right[1]) + dot(left[1], right[0]))


def one_hot(ids_row, count):
    rows = lax.broadcasted_iota(jnp.int32, (count, LANES), 0)
    return jnp.where(rows == ids_row, 1.0, 0.0).astype(jnp.bfloat16)


def gather_kernel(
    plane_ref, connect_ref, extents_ref, place_ref, velocity_hbm,
    column_ref, ids_ref, extents_out_ref, velocity_ref, arrived,
):
    copy = pltpu.make_async_copy(velocity_hbm, velocity_ref, arrived)
    copy.start()
    own_nodes = velocity_ref.shape[1]
    modes = velocity_ref.shape[0] // 3
    element_ids = connect_ref[...].astype(jnp.float32)
    elements = element_ids.shape[0]
    first_corner = element_ids[:, 0:1]
    last_corner = element_ids[:, SIDE - 1 : SIDE]
    lane = lax.broadcasted_iota(jnp.int32, (1, LANES), 1)
    ids_parts = split_two(element_ids)
    placed = [dot(ids_parts[0], place_ref[r]) + dot(ids_parts[1], place_ref[r]) for r in range(2)]
    diagonal = lax.broadcasted_iota(jnp.int32, (elements, elements), 0) == lax.broadcasted_iota(
        jnp.int32, (elements, elements), 1
    )
    lengths = [
        jnp.sum(jnp.where(diagonal, extents_ref[axis : axis + 1, :], 0.0), axis=1, keepdims=True)
        for axis in range(2)
    ]
    plane = plane_ref[0]
    held = [jnp.zeros((1, 1), jnp.float32) for _ in range(8)]
    picked = [
        jnp.where(first_corner == float(own_nodes + 6 * row), 1.0, 0.0) for row in range(2)
    ]
    ids_ref[...] = jnp.full(ids_ref.shape, -1, jnp.int32)
    owned = (lane >= ROWS) & (lane < GRID)
    chosen = []
    for column in range(COLS):
        ids = jnp.zeros((1, LANES), jnp.float32)
        own = jnp.where(plane == column, 1.0, 0.0)
        ahead = jnp.where(plane + 1 == column, 1.0, 0.0)
        for row in range(2):
            ids = ids + jnp.sum(placed[row] * picked[row], axis=0, keepdims=True)
            for axis in range(2):
                length = jnp.sum(lengths[axis] * picked[row], axis=0, keepdims=True)
                at = 2 * axis + row
                held[at] = held[at] + own * length
                held[4 + at] = held[4 + at] + ahead * length
            if column < COLS - 1:
                corner = jnp.sum(last_corner * picked[row], axis=0, keepdims=True)
                picked[row] = jnp.where(first_corner == corner, 1.0, 0.0)
        ids = jnp.where(owned, ids.astype(jnp.int32), -1)
        ids_ref[column : column + 1, :] = ids
        chosen.append(one_hot(ids, own_nodes))
    for at in range(8):
        extents_out_ref[at : at + 1, :] = jnp.broadcast_to(held[at], (1, LANES))
    at_end = jnp.where(plane == COLS - 1, 1.0, 0.0)
    extents_out_ref[8:16, :] = jnp.broadcast_to(at_end, (8, LANES))
    copy.wait()
    parts = split_three(velocity_ref[...])
    for column in range(COLS):
        values = dot(parts[2], chosen[column]) + dot(parts[1], chosen[column])
        values = values + dot(parts[0], chosen[column])
        last = values[2 * modes :, :]
        for c in range(2):
            spread = pltpu.roll(last, OWNED - c * (OWNED // 2), 1)
            column_ref[column, :, c * LANES : (c + 1) * LANES] = jnp.where(
                owned, values[c * modes : (c + 1) * modes, :], spread
            )


def three_of(packed):
    lower = packed[:, :LANES]
    upper = packed[:, LANES:]
    lane = lax.broadcasted_iota(jnp.int32, lower.shape, 1)
    last = jnp.where(
        lane < ROWS + OWNED // 2,
        pltpu.roll(lower, LANES - OWNED, 1),
        pltpu.roll(upper, LANES - OWNED // 2, 1),
    )
    return lower, upper, last


def residual_kernel(
    modes, own_nodes, column_ref, extents_ref, behind_ref, fourier_ref, plane_ref, mass_ref, out_ref
):
    planes = PLANES
    groups = planes // modes
    packed = jnp.concatenate([column_ref[p] for p in range(groups)], axis=0)
    synthesis = (fourier_ref[0, :, :planes], fourier_ref[1, :, :planes])
    forward = (fourier_ref[0, :, planes:], fourier_ref[1, :, planes:])
    speeds = three_of(packed)
    fields = three_of(dot_split(synthesis, split_two(packed)))
    lane = lax.broadcasted_iota(jnp.int32, (1, LANES), 1)
    hx = [extents_ref[at : at + 1, :] for at in range(2)]
    hy = [extents_ref[2 + at : 3 + at, :] for at in range(2)]
    at_end = extents_ref[8:9, :]
    ahead = [[], []]
    for axis in range(2):
        for row in range(2):
            match = jnp.where(behind_ref[0:1, :] == float(own_nodes + 6 * row), 1.0, 0.0)
            length = jnp.sum(behind_ref[1 + axis : 2 + axis, :] * match, axis=1, keepdims=True)
            at = 4 + 2 * axis + row
            ahead[axis].append(extents_ref[at : at + 1, :] + at_end * length)
    hx_ahead, hy_ahead = ahead
    shared = (lane >= 6 * ROWS) & (lane < GRID)
    onward = lane >= GRID

    def along_of(own, ahead):
        return jnp.where(onward, ahead, own)

    def across_of(own, ahead):
        return own + jnp.where(shared, ahead, 0.0)

    mass = jnp.zeros((1, LANES), jnp.float32)
    along = jnp.zeros((LANES, LANES), jnp.float32)
    across = jnp.zeros((LANES, LANES), jnp.float32)
    stiff = jnp.zeros((LANES, LANES), jnp.float32)
    for r in range(2):
        own = (hx[r], hy[r])
        ahead = (hx_ahead[r], hy_ahead[r])
        factor = across_of(own[0] * own[1] / 4.0, ahead[0] * ahead[1] / 4.0)
        mass = mass + factor * mass_ref[r : r + 1, :]
        along = along + along_of(own[1] / 2.0, ahead[1] / 2.0) * plane_ref[r]
        across = across + across_of(own[0] / 2.0, ahead[0] / 2.0) * plane_ref[2 + r]
        stiff = stiff + along_of(own[1] / own[0], ahead[1] / ahead[0]) * plane_ref[4 + r]
        stiff = stiff + across_of(own[0] / own[1], ahead[0] / ahead[1]) * plane_ref[6 + r]
    in_plane = split_two(jnp.concatenate([along, across, viscosity * stiff], axis=0))
    mode = lax.broadcasted_iota(jnp.int32, (planes, LANES), 0)
    wave = span_wave * jnp.where(mode == 1, planes // 2, mode // 2).astype(jnp.float32)
    carried = jnp.zeros((1, LANES), jnp.float32)
    for at, value in enumerate((hx[0], hx[1], hy[0], hy[1])):
        carried = carried + jnp.where(lane == EXTRA + at, value, 0.0)
    blocks = planes // 8
    per_group = modes // 8
    for c in range(3):
        flux = jnp.concatenate([fields[0] * fields[c], fields[1] * fields[c], fields[c]], axis=1)
        divergence = dot_split(split_two(flux), in_plane)
        span = mass * (fields[2] * fields[c])
        stacked = split_two(jnp.concatenate([divergence, span], axis=0))
        result = dot_split(forward, stacked) - (wave * wave) * (mass * speeds[c]) + carried
        for block in range(blocks):
            target = (block % per_group) * groups + block // per_group
            out_ref[target, 8 * c : 8 * c + 8, :] = result[8 * block : 8 * block + 8, :]


def apply_line(stiffness, values):
    even = [values[k] + values[6 - k] for k in range(3)] + [values[3]]
    odd = [values[k] - values[6 - k] for k in range(3)]
    result = [None] * 7
    for i in range(4):
        total = float(stiffness[i, 3]) * even[3]
        for k in range(3):
            total = total + float((stiffness[i, k] + stiffness[i, 6 - k]) / 2) * even[k]
        if i == 3:
            result[3] = total
            continue
        other = float((stiffness[i, 0] - stiffness[i, 6]) / 2) * odd[0]
        for k in range(1, 3):
            other = other + float((stiffness[i, k] - stiffness[i, 6 - k]) / 2) * odd[k]
        result[i] = total + other
        result[6 - i] = total - other
    return result


def cg_kernel(
    columns, first_ref, in_ref,
    out_ref, grid_ref, turn_ref, rest_ref, way_ref, image_ref, sum_ref,
):
    weights, derivative, stiffness = gll_one_d()
    lane = lax.broadcasted_iota(jnp.int32, (8, LANES), 1)
    at = lane % columns

    def node(i, y):
        start = (ROWS * i + y) * 8
        return slice(start, start + 8)

    def from_next(value):
        return jnp.where(
            at == columns - 1,
            pltpu.roll(value, columns - 1, 1),
            pltpu.roll(value, LANES - 1, 1),
        )

    def from_previous(value):
        return jnp.where(
            at == 0,
            pltpu.roll(value, LANES - columns + 1, 1),
            pltpu.roll(value, 1, 1),
        )

    def over_columns(value):
        step = columns // 2
        while step:
            value = value + jnp.where(
                (lane // step) % 2 == 0,
                pltpu.roll(value, LANES - step, 1),
                pltpu.roll(value, step, 1),
            )
            step //= 2
        return value

    blank = jnp.zeros((LANES - 3 * columns, LANES), jnp.float32)
    for mode in range(8):
        rows = [
            in_ref[pl.ds(8 * c + mode, columns, stride=24), :] for c in range(3)
        ]
        turned = jnp.concatenate(rows + [blank], axis=0).T
        grid_ref[pl.ds(mode, LANES, stride=8), :] = turned

    used = lane < 3 * columns

    def extent(which):
        start = (EXTRA + which) * 8
        return jnp.where(used, grid_ref[start : start + 8, :], 1.0)

    hx = [extent(0), extent(1)]
    hy = [extent(2), extent(3)]
    mode = first_ref[0] + lax.broadcasted_iota(jnp.int32, (8, LANES), 0)
    wave = span_wave * jnp.where(mode == 1, PLANES // 2, mode // 2).astype(jnp.float32)
    helmholtz = inverse_step + wave * wave
    ratio_along = [hy[r] / hx[r] for r in range(2)]
    ratio_across = [hx[r] / hy[r] for r in range(2)]
    mass = [helmholtz * (hx[r] * hy[r] / 4.0) for r in range(2)]

    def over_rows(pair, y):
        if y < 6:
            return float(weights[y]) * pair[0]
        if y > 6:
            return float(weights[y - 6]) * pair[1]
        return float(weights[6]) * pair[0] + float(weights[0]) * pair[1]

    def shared(pair):
        return [
            float(weights[0]) * value + float(weights[6]) * from_previous(value) for value in pair
        ]

    mass_shared = shared(mass)
    across_shared = shared(ratio_across)

    total = jnp.zeros((8, LANES), jnp.float32)
    for y in range(ROWS):
        flux = from_previous(grid_ref[(ONWARD_FLUX + y) * 8 : (ONWARD_FLUX + y) * 8 + 8, :])
        speed = from_previous(grid_ref[(ONWARD_SPEED + y) * 8 : (ONWARD_SPEED + y) * 8 + 8, :])
        values = [
            grid_ref[node(i, y), :]
            + float(weights[i] * derivative[i, 0]) * flux
            + float(stiffness[i, 0]) * speed
            for i in range(SIDE)
        ]
        values[0] = values[0] + from_previous(values[6])
        for i in range(6):
            value = values[i]
            rest_ref[node(i, y), :] = value
            way_ref[node(i, y), :] = value
            sum_ref[node(i, y), :] = jnp.zeros((8, LANES), jnp.float32)
            total = total + value * value
    rest_norm = over_columns(total)

    def apply():
        for y in range(ROWS):
            values = [way_ref[node(i, y), :] for i in range(6)]
            values.append(from_next(values[0]))
            lines = apply_line(stiffness, values)
            along = over_rows(ratio_along, y)
            lines = [along * line for line in lines]
            lines[0] = lines[0] + from_previous(lines[6])
            inner = over_rows(mass, y)
            outer = over_rows(mass_shared, y)
            for i in range(6):
                weight = outer if i == 0 else float(weights[i]) * inner
                image_ref[node(i, y), :] = lines[i] + weight * values[i]
        total = jnp.zeros((8, LANES), jnp.float32)
        for i in range(6):
            values = [way_ref[node(i, y), :] for y in range(ROWS)]
            lower = apply_line(stiffness, values[:7])
            upper = apply_line(stiffness, values[6:])
            if i == 0:
                scale = across_shared
            else:
                scale = [float(weights[i]) * value for value in ratio_across]
            lower = [scale[0] * value for value in lower]
            upper = [scale[1] * value for value in upper]
            lines = lower[:6] + [lower[6] + upper[0]] + upper[1:]
            for y in range(ROWS):
                image = image_ref[node(i, y), :] + lines[y]
                image_ref[node(i, y), :] = image
                total = total + values[y] * image
        return over_columns(total)

    def step(_, rest_norm):
        size = rest_norm / apply()
        total = jnp.zeros((8, LANES), jnp.float32)
        for y in range(ROWS):
            for i in range(6):
                at_node = node(i, y)
                sum_ref[at_node, :] = sum_ref[at_node, :] + size * way_ref[at_node, :]
                rest = rest_ref[at_node, :] - size * image_ref[at_node, :]
                rest_ref[at_node, :] = rest
                total = total + rest * rest
        following = over_columns(total)
        turn = following / rest_norm
        for y in range(ROWS):
            for i in range(6):
                at_node = node(i, y)
                way_ref[at_node, :] = rest_ref[at_node, :] + turn * way_ref[at_node, :]
        return following

    rest_norm = lax.fori_loop(0, ITERS - 1, step, rest_norm)
    size = rest_norm / apply()
    zero = jnp.zeros((8, LANES), jnp.float32)
    for y in range(ROWS):
        grid_ref[node(0, y), :] = zero
        for i in range(6):
            value = sum_ref[node(i, y), :] + size * way_ref[node(i, y), :]
            if i == 0:
                grid_ref[node(6, y), :] = from_next(value)
            else:
                grid_ref[node(i, y), :] = value
    for left in range(GRID, LANES):
        grid_ref[left * 8 : left * 8 + 8, :] = zero
    parts = columns // COLS
    node_lane = lax.broadcasted_iota(jnp.int32, (3 * parts, LANES), 1)
    owned = (node_lane >= ROWS) & (node_lane < GRID)
    for mode in range(8):
        turn_ref[...] = grid_ref[pl.ds(mode, LANES, stride=8), :].T
        pieces = [turn_ref[pl.ds(k, 3 * parts, stride=COLS), :] for k in range(COLS)]
        for k in range(COLS - 1):
            spread = pltpu.roll(pieces[-1], OWNED - k * THIRD, 1)
            piece = jnp.where(owned, pieces[k], spread)
            for c in range(3):
                out_ref[pl.ds(24 * k + 8 * c + mode, parts, stride=72), :] = piece[
                    c * parts : (c + 1) * parts, :
                ]


def scatter_kernel(velocity_ref, change_ref, ids_ref, out_ref):
    own_nodes = velocity_ref.shape[1]
    sources = change_ref.shape[0]
    pieces = []
    for column in range(COLS - 1):
        start = 24 * column
        pieces.append(
            jnp.concatenate(
                [
                    change_ref[m, start + 8 * c : start + 8 * c + 8, :]
                    for c in range(3)
                    for m in range(sources)
                ],
                axis=0,
            )
        )
    lane = lax.broadcasted_iota(jnp.int32, pieces[0].shape, 1)
    back = [pltpu.roll(pieces[k], LANES - OWNED + k * THIRD, 1) for k in range(COLS - 1)]
    pieces.append(
        jnp.where(
            lane < ROWS + THIRD, back[0], jnp.where(lane < ROWS + 2 * THIRD, back[1], back[2])
        )
    )
    chosen = [one_hot(ids_ref[column : column + 1, :], own_nodes) for column in range(COLS)]
    parts = split_three(jnp.concatenate(pieces, axis=1))
    chosen = jnp.concatenate(chosen, axis=1)
    change = (dot_rows(parts[2], chosen) + dot_rows(parts[1], chosen)) + dot_rows(parts[0], chosen)
    out_ref[...] = velocity_ref[...] + change


def call(kernel, out_shape, scratch=(), spaces=""):
    place = {
        "s": pl.BlockSpec(memory_space=pltpu.SMEM),
        "v": pl.BlockSpec(memory_space=pltpu.VMEM),
        "h": pl.BlockSpec(memory_space=pl.ANY),
    }
    many = isinstance(out_shape, tuple)
    return pl.pallas_call(
        kernel,
        out_shape=out_shape,
        in_specs=[place[space] for space in spaces],
        out_specs=(place["v"],) * len(out_shape) if many else place["v"],
        scratch_shapes=list(scratch),
        compiler_params=pltpu.CompilerParams(vmem_limit_bytes=32 * 2**20),
    )


def transposed(velocity, connect, right_list, extents):
    components, modes, own_nodes = velocity.shape
    groups = lax.axis_size("planes")
    parts = lax.axis_size("mesh")
    plane = lax.axis_index("planes")
    part = lax.axis_index("mesh")
    rows = components * modes
    columns = parts * COLS
    synthesis, forward = fourier_tables(PLANES)
    forward = np.concatenate([forward, span_forward(forward)], axis=1) * (-1.0 / viscosity)
    fourier = np.stack(two_parts(np.concatenate([synthesis, forward], axis=1)))
    matrices, masses = column_tables()
    place = np.stack([placement(row, True) for row in range(2)])
    flat = velocity.reshape(rows, own_nodes)
    f32 = jnp.float32
    corners = jnp.concatenate([connect[0:1].astype(f32), extents], axis=0)
    behind = lax.ppermute(corners, "mesh", [((m + 1) % parts, m) for m in range(parts)])
    column, ids, column_extents = call(
        gather_kernel,
        (
            jax.ShapeDtypeStruct((COLS, modes, 2 * LANES), f32),
            jax.ShapeDtypeStruct((8, LANES), jnp.int32),
            jax.ShapeDtypeStruct((16, LANES), f32),
        ),
        scratch=(pltpu.VMEM((rows, own_nodes), f32), pltpu.SemaphoreType.DMA),
        spaces="svvvh",
    )(plane.reshape(1), connect.T, extents, jnp.asarray(place, jnp.bfloat16), flat)
    column = lax.all_to_all(column, "planes", split_axis=0, concat_axis=0, tiled=True)
    residual = call(
        functools.partial(residual_kernel, modes, own_nodes),
        jax.ShapeDtypeStruct((columns, components * 8, LANES), f32),
        spaces="vvvvvv",
    )(
        column,
        column_extents,
        behind,
        jnp.asarray(fourier),
        jnp.asarray(matrices),
        jnp.asarray(masses),
    )
    residual = lax.all_to_all(
        residual, ("mesh", "planes"), split_axis=0, concat_axis=0, tiled=True
    )
    held = pltpu.VMEM((96 * 8, LANES), f32)
    change = call(
        functools.partial(cg_kernel, columns),
        jax.ShapeDtypeStruct((parts * 72, LANES), f32),
        scratch=(pltpu.VMEM((LANES * 8, LANES), f32), pltpu.VMEM((LANES, LANES), f32))
        + (held,) * 4,
        spaces="sv",
    )((plane * modes + part * 8).reshape(1), residual.reshape(columns * components * 8, LANES))
    change = lax.all_to_all(
        change.reshape(parts, 72, LANES), "mesh", split_axis=0, concat_axis=0, tiled=True
    )
    result = call(scatter_kernel, jax.ShapeDtypeStruct((rows, own_nodes), f32), spaces="vvv")(
        flat, change, ids
    )
    return result.reshape(velocity.shape)


def from_behind(value, axis, by):
    peers = lax.axis_size(axis)
    return lax.ppermute(value, axis, [(i, (i + by) % peers) for i in range(peers)])


def partitioned(velocity, connect, right_list, extents):
    components, modes, own_nodes = velocity.shape
    edge_count = right_list.shape[0]
    first_mode = lax.axis_index("planes") * modes
    tables = [jnp.asarray(table, jnp.float32) for table in element_tables()]
    stiff_along, stiff_across, slope_along, slope_across, mass_weights = tables
    synthesis, forward = (jnp.asarray(t, jnp.float32) for t in fourier_tables(PLANES))
    hx, hy = extents[0], extents[1]
    mass_full = mass_weights[:, None] * (hx * hy / 4.0)[None, :]
    index_list = first_mode + jnp.arange(modes, dtype=jnp.int32)
    wave = span_wave * jnp.where(index_list == 1, PLANES // 2, index_list // 2).astype(jnp.float32)
    wave = wave[None, :, None, None]
    helmholtz = inverse_step + wave * wave
    locals_ = jnp.arange(own_nodes + edge_count, dtype=jnp.int32)
    chosen = (locals_[:, None, None] == connect[None]).astype(jnp.float32)
    at_edge = (locals_[:own_nodes, None] == right_list[None]).astype(jnp.float32)

    def contract(spec, *operands):
        return jnp.einsum(spec, *operands, precision=highest)

    physical = contract(
        "jq,cqn->cjn",
        synthesis,
        lax.all_to_all(velocity, "planes", split_axis=2, concat_axis=1, tiled=True),
    )
    pairs = ((0, 0), (0, 1), (0, 2), (1, 1), (1, 2), (2, 2))
    products = jnp.stack([physical[a] * physical[b] for a, b in pairs])
    product_hat = lax.all_to_all(
        contract("qj,fjn->fqn", forward, products), "planes", split_axis=1, concat_axis=2, tiled=True
    )

    def spread(fields):
        ghosts = from_behind(contract("cqn,ny->cqy", fields, at_edge), "mesh", 1)
        return contract("cqn,nke->cqke", jnp.concatenate([fields, ghosts], axis=2), chosen)

    def assemble(terms):
        summed = contract("cqke,nke->cqn", terms, chosen)
        returned = from_behind(summed[:, :, own_nodes:], "mesh", -1)
        return summed[:, :, :own_nodes] + contract("cqy,ny->cqn", returned, at_edge)

    def stiffness(values):
        return (hy / hx) * contract("lk,cqke->cqle", stiff_along, values) + (hx / hy) * contract(
            "lk,cqke->cqle", stiff_across, values
        )

    def dots(left, right):
        return lax.psum(jnp.sum(left * right, axis=2), "mesh")

    values = spread(jnp.concatenate([velocity, product_hat], axis=0))
    speeds, along = values[0:3], values[3:6]
    across = jnp.stack([values[4], values[6], values[7]])
    span = jnp.stack([values[5], values[7], values[8]])
    shaped = span.reshape(span.shape[0], modes // 2, 2, *span.shape[2:])
    turned = jnp.stack([shaped[:, :, 1], -shaped[:, :, 0]], axis=2).reshape(span.shape)
    pair_wave = span_wave * (index_list // 2).astype(jnp.float32)[None, :, None, None]
    advection = (hy / 2.0) * contract("lk,cqke->cqle", slope_along, along)
    advection = advection + (hx / 2.0) * contract("lk,cqke->cqle", slope_across, across)
    advection = advection + mass_full * (pair_wave * turned)
    residual = assemble(
        -(wave * wave) * mass_full * speeds - stiffness(speeds) - advection / viscosity
    )
    solution = velocity
    direction = residual
    norm_now = dots(residual, residual)
    for _ in range(ITERS):
        values = spread(direction)
        operated = assemble(stiffness(values) + helmholtz * mass_full * values)
        step_size = (norm_now / dots(direction, operated))[:, :, None]
        solution = solution + step_size * direction
        residual = residual - step_size * operated
        norm_next = dots(residual, residual)
        direction = residual + (norm_next / norm_now)[:, :, None] * direction
        norm_now = norm_next
    return solution


def on_device(velocity, connect, right_list, extents):
    groups = lax.axis_size("planes")
    parts = lax.axis_size("mesh")
    modes = velocity.shape[1]
    fits = groups == COLS and modes == 8 * parts and 3 * parts * COLS <= LANES
    step = transposed if fits else partitioned
    return step(velocity, connect, right_list, extents)


def solution(mesh):
    placed = (P(None, "planes", "mesh"), P(None, "mesh"), P("mesh"), P(None, "mesh"))
    return jax.shard_map(
        on_device, mesh=mesh, in_specs=placed, out_specs=P(None, "planes", "mesh"), check_vma=False
    )
```

```python
import functools

import jax
import jax.numpy as jnp
import numpy as np
from jax import lax
from jax.experimental import pallas as pl
from jax.experimental.pallas import tpu as pltpu
from jax.sharding import PartitionSpec as P

PLANES = 256
ITERS = 4
SIDE = 7
ROWS = 13
COLS = 4
GRID = SIDE * ROWS
LANES = 128
SPEED = GRID
FIRST = GRID + ROWS
SECOND = GRID + 2 * ROWS
FITTING = LANES - SECOND
SPILL = 16
CHUNK = 25
OWNED = GRID - ROWS
THIRD = OWNED // 3

highest = lax.Precision.HIGHEST
viscosity = 0.002
time_step = 3e-05
span_wave = 4.0
inverse_step = 1.0 / (viscosity * time_step)


def legendre_six(points):
    previous = 0.0 * points + 1.0
    current = 1.0 * points
    for order in range(1, 6):
        following = ((2 * order + 1) * points * current - order * previous) / (order + 1)
        previous = current
        current = following
    return current


def gll_one_d():
    degree = 6
    points = np.array(
        [
            -1.0,
            -0.830223896278567,
            -0.4688487934707142,
            0.0,
            0.4688487934707142,
            0.830223896278567,
            1.0,
        ]
    )
    values = legendre_six(points)
    weights = 2.0 / (degree * (degree + 1) * values**2)
    derivative = np.zeros((degree + 1, degree + 1))
    for row_index in range(degree + 1):
        for col_index in range(degree + 1):
            if row_index != col_index:
                derivative[row_index, col_index] = values[row_index] / (
                    values[col_index] * (points[row_index] - points[col_index])
                )
    derivative[0, 0] = -degree * (degree + 1) / 4.0
    derivative[degree, degree] = degree * (degree + 1) / 4.0
    stiffness = derivative.T @ (weights[:, None] * derivative)
    return weights, derivative, stiffness


def element_tables():
    weights, derivative, stiffness = gll_one_d()
    identity = np.eye(SIDE)
    mass_weights = np.kron(weights, weights)
    return (
        np.kron(np.diag(weights), stiffness),
        np.kron(stiffness, np.diag(weights)),
        mass_weights[:, None] * np.kron(identity, derivative),
        mass_weights[:, None] * np.kron(derivative, identity),
        mass_weights,
    )


def fourier_tables(planes):
    plane_grid = np.arange(planes)
    synthesis = np.zeros((planes, planes))
    forward = np.zeros((planes, planes))
    synthesis[:, 0] = 1.0
    synthesis[:, 1] = np.cos(np.pi * plane_grid)
    forward[0] = 1.0 / planes
    forward[1] = np.cos(np.pi * plane_grid) / planes
    for wavenumber in range(1, planes // 2):
        phase_angle = 2.0 * np.pi * wavenumber * plane_grid / planes
        synthesis[:, 2 * wavenumber] = np.cos(phase_angle)
        synthesis[:, 2 * wavenumber + 1] = np.sin(phase_angle)
        forward[2 * wavenumber] = 2.0 * np.cos(phase_angle) / planes
        forward[2 * wavenumber + 1] = 2.0 * np.sin(phase_angle) / planes
    return synthesis, forward


def span_forward(forward):
    turned = np.zeros_like(forward)
    for wavenumber in range(1, forward.shape[0] // 2):
        turned[2 * wavenumber] = span_wave * wavenumber * forward[2 * wavenumber + 1]
        turned[2 * wavenumber + 1] = -span_wave * wavenumber * forward[2 * wavenumber]
    return turned


def two_parts(table):
    table = np.asarray(table, np.float32)
    high = table.astype(jnp.bfloat16)
    low = (table - high.astype(np.float32)).astype(jnp.bfloat16)
    return high, low


def placement(row, skip_shared):
    table = np.zeros((SIDE * SIDE, LANES))
    for j in range(SIDE):
        if skip_shared and row == 1 and j == 0:
            continue
        for i in range(SIDE):
            table[SIDE * j + i, ROWS * i + 6 * row + j] = 1.0
    return table


def column_tables():
    stiff_along, stiff_across, slope_along, slope_across, mass_weights = element_tables()
    owned = np.arange(LANES)
    owned = (owned >= ROWS) & (owned < GRID)
    matrices = []
    for table in (slope_along, slope_across, stiff_along, stiff_across):
        for row in range(2):
            place = placement(row, False)
            matrices.append((place.T @ table.T @ place) * owned[:, None])
    for start in (FIRST, SECOND):
        matrix = np.zeros((LANES, LANES))
        for y in range(ROWS):
            if start + y < LANES:
                matrix[6 * ROWS + y, start + y] = 1.0
        matrices.append(matrix)
    masses = [(mass_weights @ placement(row, False)) * owned for row in range(2)]
    return np.stack(matrices).astype(np.float32), np.stack(masses).astype(np.float32)


def split_two(value):
    high = value.astype(jnp.bfloat16)
    low = (value - high.astype(jnp.float32)).astype(jnp.bfloat16)
    return high, low


def split_three(value):
    high = value.astype(jnp.bfloat16)
    rest = value - high.astype(jnp.float32)
    middle = rest.astype(jnp.bfloat16)
    low = (rest - middle.astype(jnp.float32)).astype(jnp.bfloat16)
    return high, middle, low


def dot(left, right):
    return jnp.dot(left, right, preferred_element_type=jnp.float32)


def dot_rows(left, right):
    return lax.dot_general(
        left, right, (((1,), (1,)), ((), ())), preferred_element_type=jnp.float32
    )


def dot_split(left, right):
    return dot(
        jnp.concatenate([left[0], left[1], left[0]], axis=1),
        jnp.concatenate([right[1], right[0], right[0]], axis=0),
    )


def one_hot(ids_row, count):
    rows = lax.broadcasted_iota(jnp.int32, (count, LANES), 0)
    return jnp.where(rows == ids_row, 1.0, 0.0).astype(jnp.bfloat16)


def gather_kernel(
    plane_ref, connect_hbm, extents_hbm, place_hbm, velocity_hbm,
    slot_a, slot_b, slot_c, slot_d, ids_ref, extents_out_ref,
    connect_ref, extents_ref, place_ref, velocity_ref, arrived,
):
    slots = (slot_a, slot_b, slot_c, slot_d)
    sources = (connect_hbm, extents_hbm, place_hbm, velocity_hbm)
    targets = (connect_ref, extents_ref, place_ref, velocity_ref)
    copies = [
        pltpu.make_async_copy(source, target, arrived.at[at])
        for at, (source, target) in enumerate(zip(sources, targets))
    ]
    for copy in copies:
        copy.start()
    for copy in copies[:3]:
        copy.wait()
    own_nodes = velocity_ref.shape[1]
    modes = velocity_ref.shape[0] // 3
    element_ids = connect_ref[...].astype(jnp.float32)
    elements = element_ids.shape[0]
    first_corner = element_ids[:, 0:1]
    last_corner = element_ids[:, SIDE - 1 : SIDE]
    lane = lax.broadcasted_iota(jnp.int32, (1, LANES), 1)
    ids_parts = split_two(element_ids)
    placed = [dot(ids_parts[0], place_ref[r]) + dot(ids_parts[1], place_ref[r]) for r in range(2)]
    diagonal = lax.broadcasted_iota(jnp.int32, (elements, elements), 0) == lax.broadcasted_iota(
        jnp.int32, (elements, elements), 1
    )
    lengths = [
        jnp.sum(jnp.where(diagonal, extents_ref[axis : axis + 1, :], 0.0), axis=1, keepdims=True)
        for axis in range(2)
    ]
    plane = plane_ref[0]
    held = [jnp.zeros((1, 1), jnp.float32) for _ in range(4)]
    picked = [
        jnp.where(first_corner == float(own_nodes + 6 * row), 1.0, 0.0) for row in range(2)
    ]
    ids_ref[...] = jnp.full(ids_ref.shape, -1, jnp.int32)
    owned = (lane >= ROWS) & (lane < GRID)
    for column in range(COLS):
        ids = jnp.zeros((1, LANES), jnp.float32)
        own = jnp.where(plane == column, 1.0, 0.0)
        for row in range(2):
            ids = ids + jnp.sum(placed[row] * picked[row], axis=0, keepdims=True)
            for axis in range(2):
                length = jnp.sum(lengths[axis] * picked[row], axis=0, keepdims=True)
                at = 2 * axis + row
                held[at] = held[at] + own * length
            if column < COLS - 1:
                corner = jnp.sum(last_corner * picked[row], axis=0, keepdims=True)
                picked[row] = jnp.where(first_corner == corner, 1.0, 0.0)
        ids = jnp.where(owned, ids.astype(jnp.int32), -1)
        ids_ref[column : column + 1, :] = ids
    for at in range(4):
        extents_out_ref[at : at + 1, :] = jnp.broadcast_to(held[at], (1, LANES))
    extents_out_ref[4:8, :] = jnp.zeros((4, LANES), jnp.float32)
    chosen = [one_hot(ids_ref[pl.ds(plane ^ slot, 1), :], own_nodes) for slot in range(COLS)]
    copies[3].wait()
    parts = split_three(velocity_ref[...])
    for slot in range(COLS):
        values = dot(parts[2], chosen[slot]) + dot(parts[1], chosen[slot])
        values = values + dot(parts[0], chosen[slot])
        last = values[2 * modes :, :]
        for c in range(2):
            spread = pltpu.roll(last, OWNED - c * (OWNED // 2), 1)
            slots[slot][:, c * LANES : (c + 1) * LANES] = jnp.where(
                owned, values[c * modes : (c + 1) * modes, :], spread
            )


def three_of(packed):
    lower = packed[:, :LANES]
    upper = packed[:, LANES:]
    lane = lax.broadcasted_iota(jnp.int32, lower.shape, 1)
    last = jnp.where(
        lane < ROWS + OWNED // 2,
        pltpu.roll(lower, LANES - OWNED, 1),
        pltpu.roll(upper, LANES - OWNED // 2, 1),
    )
    return lower, upper, last


def setup_kernel(
    extents_ref, fourier_hbm, plane_hbm, mass_ref,
    fourier_ref, in_plane_ref, row_ref, plane_ref, arrived,
):
    copies = [
        pltpu.make_async_copy(plane_hbm, plane_ref, arrived.at[0]),
        pltpu.make_async_copy(fourier_hbm, fourier_ref, arrived.at[1]),
    ]
    for copy in copies:
        copy.start()
    hx = [extents_ref[at : at + 1, :] for at in range(2)]
    hy = [extents_ref[2 + at : 3 + at, :] for at in range(2)]
    lane = lax.broadcasted_iota(jnp.int32, (1, LANES), 1)
    carried = jnp.zeros((1, LANES), jnp.float32)
    for at, value in enumerate((hx[0], hx[1], hy[0], hy[1])):
        carried = carried + jnp.where(lane == at, value, 0.0)
    mass = sum((hx[r] * hy[r] / 4.0) * mass_ref[r : r + 1, :] for r in range(2))
    row_ref[...] = jnp.concatenate([mass, carried, jnp.zeros((6, LANES), jnp.float32)], axis=0)
    copies[0].wait()
    along = sum((hy[r] / 2.0) * plane_ref[r] for r in range(2)) + plane_ref[8]
    across = sum((hx[r] / 2.0) * plane_ref[2 + r] for r in range(2)) + plane_ref[9]
    stiff = sum(
        (hy[r] / hx[r]) * plane_ref[4 + r] + (hx[r] / hy[r]) * plane_ref[6 + r] for r in range(2)
    )
    high, low = split_two(jnp.concatenate([along, across, viscosity * stiff], axis=0))
    in_plane_ref[0] = high
    in_plane_ref[1] = low
    copies[1].wait()


def residual_kernel(
    modes, plane_at, slot_a, slot_b, slot_c, slot_d, fourier_ref, in_plane_ref, row_ref,
    out_ref, packed_ref,
):
    planes = PLANES
    groups = planes // modes
    for slot, slot_ref in enumerate((slot_a, slot_b, slot_c, slot_d)):
        start = pl.multiple_of((plane_at[0] ^ slot) * modes, modes)
        packed_ref[pl.ds(start, modes), :] = slot_ref[...]
    packed = packed_ref[...]
    synthesis = (fourier_ref[0, :, :planes], fourier_ref[1, :, :planes])
    forward = (fourier_ref[0, :, planes:], fourier_ref[1, :, planes:])
    speeds = three_of(packed)
    fields = three_of(dot_split(synthesis, split_two(packed)))
    mass = row_ref[0:1, :]
    carried = row_ref[1:2, :]
    products = [[fields[a] * fields[c] for a in range(3)] for c in range(3)]
    flux = jnp.concatenate(
        [jnp.concatenate([products[c][0], products[c][1], fields[c]], axis=1) for c in range(3)],
        axis=0,
    )
    divergence = dot_split(split_two(flux), (in_plane_ref[0], in_plane_ref[1]))
    divergence = [divergence[c * planes : (c + 1) * planes, :] for c in range(3)]
    lane = lax.broadcasted_iota(jnp.int32, (planes, LANES), 1)
    divergence[1] = jnp.where(
        (lane >= FIRST) & (lane < SECOND),
        pltpu.roll(products[2][2], FIRST - 6 * ROWS, 1),
        divergence[1],
    )
    spill = jnp.zeros((planes, LANES), jnp.float32)
    last = 6 * ROWS + FITTING
    for c in range(3):
        start = SPILL * (c + 1)
        spill = jnp.where(
            (lane >= start) & (lane < start + ROWS - FITTING),
            pltpu.roll(products[c][1], LANES + start - last, 1),
            spill,
        )
    upper = jnp.concatenate(divergence + [spill], axis=1)
    lower = jnp.concatenate([mass * products[c][2] for c in range(3)] + [spill * 0.0], axis=1)
    result = dot_split(forward, split_two(jnp.concatenate([upper, lower], axis=0)))
    mode = lax.broadcasted_iota(jnp.int32, (planes, LANES), 0)
    wave = span_wave * jnp.where(mode == 1, planes // 2, mode // 2).astype(jnp.float32)
    square = wave * wave
    blocks = planes // 8
    per_group = modes // 8
    tiles = []
    for c in range(3):
        tile = result[:, c * LANES : (c + 1) * LANES] - square * (mass * speeds[c])
        handed = pltpu.roll(speeds[c], SPEED - 6 * ROWS, 1)
        tiles.append(jnp.where((lane >= SPEED) & (lane < FIRST), handed, tile))
    spilled = result[:, 3 * LANES :]
    for block in range(blocks):
        start = CHUNK * ((block % per_group) * groups + block // per_group)
        for c in range(3):
            out_ref[start + 8 * c : start + 8 * c + 8, :] = tiles[c][8 * block : 8 * block + 8, :]
        row = pltpu.roll(spilled[8 * block : 8 * block + 8, :], 0, 1, stride=2, stride_axis=0)
        out_ref[start + 24 : start + 25, :] = jnp.sum(row, axis=0, keepdims=True) + carried


def apply_line(stiffness, values):
    even = [values[k] + values[6 - k] for k in range(3)] + [values[3]]
    odd = [values[k] - values[6 - k] for k in range(3)]
    result = [None] * 7
    for i in range(4):
        total = float(stiffness[i, 3]) * even[3]
        for k in range(3):
            total = total + float((stiffness[i, k] + stiffness[i, 6 - k]) / 2) * even[k]
        if i == 3:
            result[3] = total
            continue
        other = float((stiffness[i, 0] - stiffness[i, 6]) / 2) * odd[0]
        for k in range(1, 3):
            other = other + float((stiffness[i, k] - stiffness[i, 6 - k]) / 2) * odd[k]
        result[i] = total + other
        result[6 - i] = total - other
    return result


def cg_kernel(
    columns, first_ref, in_ref,
    out_ref, grid_ref, turn_ref, rest_ref, way_ref, image_ref, sum_ref,
):
    weights, derivative, stiffness = gll_one_d()
    lane = lax.broadcasted_iota(jnp.int32, (8, LANES), 1)
    at = lane % columns

    def node(i, y):
        start = (ROWS * i + y) * 8
        return slice(start, start + 8)

    def from_next(value):
        return jnp.where(
            at == columns - 1,
            pltpu.roll(value, columns - 1, 1),
            pltpu.roll(value, LANES - 1, 1),
        )

    def from_previous(value):
        return jnp.where(
            at == 0,
            pltpu.roll(value, LANES - columns + 1, 1),
            pltpu.roll(value, 1, 1),
        )

    def over_columns(value):
        step = columns // 2
        while step:
            value = value + jnp.where(
                (lane // step) % 2 == 0,
                pltpu.roll(value, LANES - step, 1),
                pltpu.roll(value, step, 1),
            )
            step //= 2
        return value

    blank = jnp.zeros((LANES - 3 * columns, LANES), jnp.float32)
    for mode in range(8):
        rows = [in_ref[pl.ds(8 * c + mode, columns, stride=CHUNK), :] for c in range(3)]
        turned = jnp.concatenate(rows + [blank], axis=0).T
        grid_ref[pl.ds(mode, LANES, stride=8), :] = turned

    extras = in_ref[pl.ds(CHUNK - 1, columns, stride=CHUNK), :]
    turn_ref[...] = jnp.concatenate([extras] * (LANES // columns), axis=0).T
    hx = [jnp.broadcast_to(turn_ref[at : at + 1, :], (8, LANES)) for at in range(2)]
    hy = [jnp.broadcast_to(turn_ref[2 + at : 3 + at, :], (8, LANES)) for at in range(2)]
    mode = first_ref[0] + lax.broadcasted_iota(jnp.int32, (8, LANES), 0)
    wave = span_wave * jnp.where(mode == 1, PLANES // 2, mode // 2).astype(jnp.float32)
    pair_wave = span_wave * (mode // 2).astype(jnp.float32)
    helmholtz = inverse_step + wave * wave
    ratio_along = [hy[r] / hx[r] for r in range(2)]
    ratio_across = [hx[r] / hy[r] for r in range(2)]
    mass = [helmholtz * (hx[r] * hy[r] / 4.0) for r in range(2)]

    def over_rows(pair, y):
        if y < 6:
            return float(weights[y]) * pair[0]
        if y > 6:
            return float(weights[y - 6]) * pair[1]
        return float(weights[6]) * pair[0] + float(weights[0]) * pair[1]

    def shared(pair):
        return [
            float(weights[0]) * value + float(weights[6]) * from_previous(value) for value in pair
        ]

    mass_shared = shared(mass)
    across_shared = shared(ratio_across)

    group = lane // columns

    def handed(start, y):
        return from_previous(grid_ref[(start + y) * 8 : (start + y) * 8 + 8, :])

    def spilled(y):
        rows = [
            turn_ref[pl.ds(SPILL * (c + 1) + y - FITTING, 8, stride=2), :] for c in range(3)
        ]
        return from_previous(
            jnp.where(group == 0, rows[0], jnp.where(group == 1, rows[1], rows[2]))
        )

    first_speed = [handed(SPEED, y) for y in range(ROWS)]
    first = [handed(FIRST, y) for y in range(ROWS)]
    second = [handed(SECOND, y) if y < FITTING else spilled(y) for y in range(ROWS)]
    sloped = weights[:, None] * derivative
    lines = [jnp.zeros((8, LANES), jnp.float32)] * ROWS
    for r in range(2):
        rows = range(6 * r, 6 * r + SIDE)
        curved = apply_line(stiffness, [first_speed[y] for y in rows])
        for j, y in enumerate(rows):
            slope = sum(float(sloped[j, k]) * second[6 * r + k] for k in range(SIDE))
            lines[y] = lines[y] + float(weights[0]) * (
                (0.5 * hx[r]) * slope - ratio_across[r] * curved[j]
            )
    area = [0.25 * hx[r] * hy[r] for r in range(2)]
    half = [0.5 * hy[r] for r in range(2)]
    even = mode % 2 == 0
    total = jnp.zeros((8, LANES), jnp.float32)
    for y in range(ROWS):
        along = jnp.where(group == 1, pltpu.roll(second[y], columns, 1), first[y])
        span = jnp.where(
            group == 0,
            pltpu.roll(first[y], 2 * columns, 1),
            jnp.where(
                group == 1,
                pltpu.roll(second[y], LANES - columns, 1),
                pltpu.roll(first[y], columns, 1),
            ),
        )
        span = jnp.where(even, pltpu.roll(span, 7, 0), -pltpu.roll(span, 1, 0))
        across = lines[y] + float(weights[0]) * over_rows(area, y) * (
            pair_wave * span - (wave * wave) * first_speed[y]
        )
        flux = over_rows(half, y) * along
        speed = over_rows(ratio_along, y) * first_speed[y]
        values = [
            grid_ref[node(i, y), :]
            + float(sloped[i, 0]) * flux
            - float(stiffness[i, 0]) * speed
            for i in range(SIDE)
        ]
        values[0] = values[0] + across + from_previous(values[6])
        for i in range(6):
            value = values[i]
            rest_ref[node(i, y), :] = value
            way_ref[node(i, y), :] = value
            sum_ref[node(i, y), :] = jnp.zeros((8, LANES), jnp.float32)
            total = total + value * value
    rest_norm = over_columns(total)

    def apply():
        for y in range(ROWS):
            values = [way_ref[node(i, y), :] for i in range(6)]
            values.append(from_next(values[0]))
            lines = apply_line(stiffness, values)
            along = over_rows(ratio_along, y)
            lines = [along * line for line in lines]
            lines[0] = lines[0] + from_previous(lines[6])
            inner = over_rows(mass, y)
            outer = over_rows(mass_shared, y)
            for i in range(6):
                weight = outer if i == 0 else float(weights[i]) * inner
                image_ref[node(i, y), :] = lines[i] + weight * values[i]
        total = jnp.zeros((8, LANES), jnp.float32)
        for i in range(6):
            values = [way_ref[node(i, y), :] for y in range(ROWS)]
            lower = apply_line(stiffness, values[:7])
            upper = apply_line(stiffness, values[6:])
            if i == 0:
                scale = across_shared
            else:
                scale = [float(weights[i]) * value for value in ratio_across]
            lower = [scale[0] * value for value in lower]
            upper = [scale[1] * value for value in upper]
            lines = lower[:6] + [lower[6] + upper[0]] + upper[1:]
            for y in range(ROWS):
                image = image_ref[node(i, y), :] + lines[y]
                image_ref[node(i, y), :] = image
                total = total + values[y] * image
        return over_columns(total)

    def step(_, rest_norm):
        size = rest_norm / apply()
        total = jnp.zeros((8, LANES), jnp.float32)
        for y in range(ROWS):
            for i in range(6):
                at_node = node(i, y)
                sum_ref[at_node, :] = sum_ref[at_node, :] + size * way_ref[at_node, :]
                rest = rest_ref[at_node, :] - size * image_ref[at_node, :]
                rest_ref[at_node, :] = rest
                total = total + rest * rest
        following = over_columns(total)
        turn = following / rest_norm
        for y in range(ROWS):
            for i in range(6):
                at_node = node(i, y)
                way_ref[at_node, :] = rest_ref[at_node, :] + turn * way_ref[at_node, :]
        return following

    rest_norm = lax.fori_loop(0, ITERS - 1, step, rest_norm)
    size = rest_norm / apply()
    zero = jnp.zeros((8, LANES), jnp.float32)
    for y in range(ROWS):
        grid_ref[node(0, y), :] = zero
        for i in range(6):
            value = sum_ref[node(i, y), :] + size * way_ref[node(i, y), :]
            if i == 0:
                grid_ref[node(6, y), :] = from_next(value)
            else:
                grid_ref[node(i, y), :] = value
    for left in range(GRID, LANES):
        grid_ref[left * 8 : left * 8 + 8, :] = zero
    parts = columns // COLS
    node_lane = lax.broadcasted_iota(jnp.int32, (3 * parts, LANES), 1)
    owned = (node_lane >= ROWS) & (node_lane < GRID)
    for mode in range(8):
        turn_ref[...] = grid_ref[pl.ds(mode, LANES, stride=8), :].T
        pieces = [turn_ref[pl.ds(k, 3 * parts, stride=COLS), :] for k in range(COLS)]
        for k in range(COLS - 1):
            spread = pltpu.roll(pieces[-1], OWNED - k * THIRD, 1)
            piece = jnp.where(owned, pieces[k], spread)
            for c in range(3):
                out_ref[pl.ds(24 * k + 8 * c + mode, parts, stride=72), :] = piece[
                    c * parts : (c + 1) * parts, :
                ]


def scatter_kernel(velocity_ref, change_ref, ids_ref, out_ref):
    own_nodes = velocity_ref.shape[1]
    sources = change_ref.shape[0]
    pieces = []
    for column in range(COLS - 1):
        start = 24 * column
        pieces.append(
            jnp.concatenate(
                [
                    change_ref[m, start + 8 * c : start + 8 * c + 8, :]
                    for c in range(3)
                    for m in range(sources)
                ],
                axis=0,
            )
        )
    lane = lax.broadcasted_iota(jnp.int32, pieces[0].shape, 1)
    back = [pltpu.roll(pieces[k], LANES - OWNED + k * THIRD, 1) for k in range(COLS - 1)]
    pieces.append(
        jnp.where(
            lane < ROWS + THIRD, back[0], jnp.where(lane < ROWS + 2 * THIRD, back[1], back[2])
        )
    )
    chosen = [one_hot(ids_ref[column : column + 1, :], own_nodes) for column in range(COLS)]
    parts = split_three(jnp.concatenate(pieces, axis=1))
    chosen = jnp.concatenate(chosen, axis=1)
    change = (dot_rows(parts[2], chosen) + dot_rows(parts[1], chosen)) + dot_rows(parts[0], chosen)
    out_ref[...] = velocity_ref[...] + change


def call(kernel, out_shape, scratch=(), spaces="", cost=None):
    place = {
        "s": pl.BlockSpec(memory_space=pltpu.SMEM),
        "v": pl.BlockSpec(memory_space=pltpu.VMEM),
        "h": pl.BlockSpec(memory_space=pltpu.HBM),
    }
    many = isinstance(out_shape, tuple)
    run = pl.pallas_call(
        kernel,
        out_shape=out_shape,
        in_specs=[place[space] for space in spaces],
        out_specs=(place["v"],) * len(out_shape) if many else place["v"],
        scratch_shapes=list(scratch),
        cost_estimate=cost,
        compiler_params=pltpu.CompilerParams(vmem_limit_bytes=16 * 2**20),
    )

    def with_spaces(*operands):
        return run(
            *(
                pltpu.with_memory_space_constraint(operand, pltpu.HBM) if space == "h" else operand
                for space, operand in zip(spaces, operands)
            )
        )

    return with_spaces


def transposed(velocity, connect, right_list, extents):
    components, modes, own_nodes = velocity.shape
    groups = lax.axis_size("planes")
    parts = lax.axis_size("mesh")
    plane = lax.axis_index("planes")
    part = lax.axis_index("mesh")
    rows = components * modes
    columns = parts * COLS
    synthesis, forward = fourier_tables(PLANES)
    forward = np.concatenate([forward, span_forward(forward)], axis=1) * (-1.0 / viscosity)
    fourier = np.stack(two_parts(np.concatenate([synthesis, forward], axis=1)))
    matrices, masses = column_tables()
    place = np.stack([placement(row, True) for row in range(2)])
    flat = velocity.reshape(rows, own_nodes)
    f32 = jnp.float32
    slot_shape = jax.ShapeDtypeStruct((modes, 2 * LANES), f32)
    *slots, ids, column_extents = call(
        gather_kernel,
        (slot_shape,) * COLS
        + (
            jax.ShapeDtypeStruct((8, LANES), jnp.int32),
            jax.ShapeDtypeStruct((8, LANES), f32),
        ),
        scratch=(
            pltpu.VMEM(connect.shape[::-1], jnp.int32),
            pltpu.VMEM(extents.shape, f32),
            pltpu.VMEM(place.shape, jnp.bfloat16),
            pltpu.VMEM((rows, own_nodes), f32),
            pltpu.SemaphoreType.DMA((4,)),
        ),
        spaces="shhhh",
    )(plane.reshape(1), connect.T, extents, jnp.asarray(place, jnp.bfloat16), flat)
    slots = [slots[0]] + [
        lax.ppermute(slots[s], "planes", [(p, p ^ s) for p in range(groups)])
        for s in range(1, groups)
    ]
    tables = call(
        setup_kernel,
        (
            jax.ShapeDtypeStruct(fourier.shape, jnp.bfloat16),
            jax.ShapeDtypeStruct((2, 3 * LANES, LANES), jnp.bfloat16),
            jax.ShapeDtypeStruct((8, LANES), f32),
        ),
        scratch=(pltpu.VMEM(matrices.shape, f32), pltpu.SemaphoreType.DMA((2,))),
        spaces="vhhv",
        cost=pl.CostEstimate(flops=10**6, bytes_accessed=3 * 10**6, transcendentals=0),
    )(column_extents, jnp.asarray(fourier), jnp.asarray(matrices), jnp.asarray(masses))
    residual = call(
        functools.partial(residual_kernel, modes),
        jax.ShapeDtypeStruct((columns * CHUNK, LANES), f32),
        scratch=(pltpu.VMEM((PLANES, 2 * LANES), f32),),
        spaces="svvvvvvv",
    )(plane.reshape(1), *slots, *tables)
    residual = lax.all_to_all(
        residual.reshape(columns * CHUNK, 1, LANES),
        ("mesh", "planes"),
        split_axis=0,
        concat_axis=0,
        tiled=True,
    )
    held = pltpu.VMEM((96 * 8, LANES), f32)
    change = call(
        functools.partial(cg_kernel, columns),
        jax.ShapeDtypeStruct((parts * 72, LANES), f32),
        scratch=(pltpu.VMEM((LANES * 8, LANES), f32), pltpu.VMEM((LANES, LANES), f32))
        + (held,) * 4,
        spaces="sv",
    )((plane * modes + part * 8).reshape(1), residual.reshape(columns * CHUNK, LANES))
    change = lax.all_to_all(
        change.reshape(parts, 72, LANES), "mesh", split_axis=0, concat_axis=0, tiled=True
    )
    result = call(scatter_kernel, jax.ShapeDtypeStruct((rows, own_nodes), f32), spaces="vvv")(
        flat, change, ids
    )
    return result.reshape(velocity.shape)


def from_behind(value, axis, by):
    peers = lax.axis_size(axis)
    return lax.ppermute(value, axis, [(i, (i + by) % peers) for i in range(peers)])


def partitioned(velocity, connect, right_list, extents):
    components, modes, own_nodes = velocity.shape
    edge_count = right_list.shape[0]
    first_mode = lax.axis_index("planes") * modes
    tables = [jnp.asarray(table, jnp.float32) for table in element_tables()]
    stiff_along, stiff_across, slope_along, slope_across, mass_weights = tables
    synthesis, forward = (jnp.asarray(t, jnp.float32) for t in fourier_tables(PLANES))
    hx, hy = extents[0], extents[1]
    mass_full = mass_weights[:, None] * (hx * hy / 4.0)[None, :]
    index_list = first_mode + jnp.arange(modes, dtype=jnp.int32)
    wave = span_wave * jnp.where(index_list == 1, PLANES // 2, index_list // 2).astype(jnp.float32)
    wave = wave[None, :, None, None]
    helmholtz = inverse_step + wave * wave
    locals_ = jnp.arange(own_nodes + edge_count, dtype=jnp.int32)
    chosen = (locals_[:, None, None] == connect[None]).astype(jnp.float32)
    at_edge = (locals_[:own_nodes, None] == right_list[None]).astype(jnp.float32)

    def contract(spec, *operands):
        return jnp.einsum(spec, *operands, precision=highest)

    physical = contract(
        "jq,cqn->cjn",
        synthesis,
        lax.all_to_all(velocity, "planes", split_axis=2, concat_axis=1, tiled=True),
    )
    pairs = ((0, 0), (0, 1), (0, 2), (1, 1), (1, 2), (2, 2))
    products = jnp.stack([physical[a] * physical[b] for a, b in pairs])
    product_hat = lax.all_to_all(
        contract("qj,fjn->fqn", forward, products), "planes", split_axis=1, concat_axis=2, tiled=True
    )

    def spread(fields):
        ghosts = from_behind(contract("cqn,ny->cqy", fields, at_edge), "mesh", 1)
        return contract("cqn,nke->cqke", jnp.concatenate([fields, ghosts], axis=2), chosen)

    def assemble(terms):
        summed = contract("cqke,nke->cqn", terms, chosen)
        returned = from_behind(summed[:, :, own_nodes:], "mesh", -1)
        return summed[:, :, :own_nodes] + contract("cqy,ny->cqn", returned, at_edge)

    def stiffness(values):
        return (hy / hx) * contract("lk,cqke->cqle", stiff_along, values) + (hx / hy) * contract(
            "lk,cqke->cqle", stiff_across, values
        )

    def dots(left, right):
        return lax.psum(jnp.sum(left * right, axis=2), "mesh")

    values = spread(jnp.concatenate([velocity, product_hat], axis=0))
    speeds, along = values[0:3], values[3:6]
    across = jnp.stack([values[4], values[6], values[7]])
    span = jnp.stack([values[5], values[7], values[8]])
    shaped = span.reshape(span.shape[0], modes // 2, 2, *span.shape[2:])
    turned = jnp.stack([shaped[:, :, 1], -shaped[:, :, 0]], axis=2).reshape(span.shape)
    pair_wave = span_wave * (index_list // 2).astype(jnp.float32)[None, :, None, None]
    advection = (hy / 2.0) * contract("lk,cqke->cqle", slope_along, along)
    advection = advection + (hx / 2.0) * contract("lk,cqke->cqle", slope_across, across)
    advection = advection + mass_full * (pair_wave * turned)
    residual = assemble(
        -(wave * wave) * mass_full * speeds - stiffness(speeds) - advection / viscosity
    )
    solution = velocity
    direction = residual
    norm_now = dots(residual, residual)
    for _ in range(ITERS):
        values = spread(direction)
        operated = assemble(stiffness(values) + helmholtz * mass_full * values)
        step_size = (norm_now / dots(direction, operated))[:, :, None]
        solution = solution + step_size * direction
        residual = residual - step_size * operated
        norm_next = dots(residual, residual)
        direction = residual + (norm_next / norm_now)[:, :, None] * direction
        norm_now = norm_next
    return solution


def on_device(velocity, connect, right_list, extents):
    groups = lax.axis_size("planes")
    parts = lax.axis_size("mesh")
    modes = velocity.shape[1]
    fits = groups == COLS and modes == 8 * parts and 3 * parts * COLS <= LANES
    step = transposed if fits else partitioned
    return step(velocity, connect, right_list, extents)


def solution(mesh):
    placed = (P(None, "planes", "mesh"), P(None, "mesh"), P("mesh"), P(None, "mesh"))
    return jax.shard_map(
        on_device, mesh=mesh, in_specs=placed, out_specs=P(None, "planes", "mesh"), check_vma=False
    )
```

```python
import functools

import jax
import jax.numpy as jnp
import numpy as np
from jax import lax
from jax.experimental import pallas as pl
from jax.experimental.pallas import tpu as pltpu
from jax.sharding import PartitionSpec as P

PLANES = 256
ITERS = 4
SIDE = 7
ROWS = 13
COLS = 4
GRID = SIDE * ROWS
LANES = 128
SPEED = GRID
FIRST = GRID + ROWS
SECOND = GRID + 2 * ROWS
FITTING = LANES - SECOND
SPILL = 16
CHUNK = 25
OWNED = GRID - ROWS
THIRD = OWNED // 3

highest = lax.Precision.HIGHEST
viscosity = 0.002
time_step = 3e-05
span_wave = 4.0
inverse_step = 1.0 / (viscosity * time_step)


def legendre_six(points):
    previous = 0.0 * points + 1.0
    current = 1.0 * points
    for order in range(1, 6):
        following = ((2 * order + 1) * points * current - order * previous) / (order + 1)
        previous = current
        current = following
    return current


def gll_one_d():
    degree = 6
    points = np.array(
        [
            -1.0,
            -0.830223896278567,
            -0.4688487934707142,
            0.0,
            0.4688487934707142,
            0.830223896278567,
            1.0,
        ]
    )
    values = legendre_six(points)
    weights = 2.0 / (degree * (degree + 1) * values**2)
    derivative = np.zeros((degree + 1, degree + 1))
    for row_index in range(degree + 1):
        for col_index in range(degree + 1):
            if row_index != col_index:
                derivative[row_index, col_index] = values[row_index] / (
                    values[col_index] * (points[row_index] - points[col_index])
                )
    derivative[0, 0] = -degree * (degree + 1) / 4.0
    derivative[degree, degree] = degree * (degree + 1) / 4.0
    stiffness = derivative.T @ (weights[:, None] * derivative)
    return weights, derivative, stiffness


def element_tables():
    weights, derivative, stiffness = gll_one_d()
    identity = np.eye(SIDE)
    mass_weights = np.kron(weights, weights)
    return (
        np.kron(np.diag(weights), stiffness),
        np.kron(stiffness, np.diag(weights)),
        mass_weights[:, None] * np.kron(identity, derivative),
        mass_weights[:, None] * np.kron(derivative, identity),
        mass_weights,
    )


def fourier_tables(planes):
    plane_grid = np.arange(planes)
    synthesis = np.zeros((planes, planes))
    forward = np.zeros((planes, planes))
    synthesis[:, 0] = 1.0
    synthesis[:, 1] = np.cos(np.pi * plane_grid)
    forward[0] = 1.0 / planes
    forward[1] = np.cos(np.pi * plane_grid) / planes
    for wavenumber in range(1, planes // 2):
        phase_angle = 2.0 * np.pi * wavenumber * plane_grid / planes
        synthesis[:, 2 * wavenumber] = np.cos(phase_angle)
        synthesis[:, 2 * wavenumber + 1] = np.sin(phase_angle)
        forward[2 * wavenumber] = 2.0 * np.cos(phase_angle) / planes
        forward[2 * wavenumber + 1] = 2.0 * np.sin(phase_angle) / planes
    return synthesis, forward


def span_forward(forward):
    turned = np.zeros_like(forward)
    for wavenumber in range(1, forward.shape[0] // 2):
        turned[2 * wavenumber] = span_wave * wavenumber * forward[2 * wavenumber + 1]
        turned[2 * wavenumber + 1] = -span_wave * wavenumber * forward[2 * wavenumber]
    return turned


def two_parts(table):
    table = np.asarray(table, np.float32)
    high = table.astype(jnp.bfloat16)
    low = (table - high.astype(np.float32)).astype(jnp.bfloat16)
    return high, low


def placement(row, skip_shared):
    table = np.zeros((SIDE * SIDE, LANES))
    for j in range(SIDE):
        if skip_shared and row == 1 and j == 0:
            continue
        for i in range(SIDE):
            table[SIDE * j + i, ROWS * i + 6 * row + j] = 1.0
    return table


def column_tables():
    stiff_along, stiff_across, slope_along, slope_across, mass_weights = element_tables()
    owned = np.arange(LANES)
    owned = (owned >= ROWS) & (owned < GRID)
    matrices = []
    for table in (slope_along, slope_across, stiff_along, stiff_across):
        for row in range(2):
            place = placement(row, False)
            matrices.append((place.T @ table.T @ place) * owned[:, None])
    for start in (FIRST, SECOND):
        matrix = np.zeros((LANES, LANES))
        for y in range(ROWS):
            if start + y < LANES:
                matrix[6 * ROWS + y, start + y] = 1.0
        matrices.append(matrix)
    masses = [(mass_weights @ placement(row, False)) * owned for row in range(2)]
    return np.stack(matrices).astype(np.float32), np.stack(masses).astype(np.float32)


def split_two(value):
    high = value.astype(jnp.bfloat16)
    low = (value - high.astype(jnp.float32)).astype(jnp.bfloat16)
    return high, low


def split_three(value):
    high = value.astype(jnp.bfloat16)
    rest = value - high.astype(jnp.float32)
    middle = rest.astype(jnp.bfloat16)
    low = (rest - middle.astype(jnp.float32)).astype(jnp.bfloat16)
    return high, middle, low


def dot(left, right):
    return jnp.dot(left, right, preferred_element_type=jnp.float32)


def dot_split(left, right):
    return dot(
        jnp.concatenate([left[0], left[1], left[0]], axis=1),
        jnp.concatenate([right[1], right[0], right[0]], axis=0),
    )


def one_hot(ids_row, count):
    rows = lax.broadcasted_iota(jnp.int32, (count, LANES), 0)
    return jnp.where(rows == ids_row, 1.0, 0.0).astype(jnp.bfloat16)


def gather_kernel(
    plane_ref, connect_hbm, extents_hbm, place_hbm, velocity_hbm,
    slot_a, slot_b, slot_c, slot_d, ids_ref, extents_out_ref,
    connect_ref, extents_ref, place_ref, velocity_ref, arrived,
):
    slots = (slot_a, slot_b, slot_c, slot_d)
    sources = (connect_hbm, extents_hbm, place_hbm, velocity_hbm)
    targets = (connect_ref, extents_ref, place_ref, velocity_ref)
    copies = [
        pltpu.make_async_copy(source, target, arrived.at[at])
        for at, (source, target) in enumerate(zip(sources, targets))
    ]
    for copy in copies:
        copy.start()
    for copy in copies[:3]:
        copy.wait()
    own_nodes = velocity_ref.shape[1]
    modes = velocity_ref.shape[0] // 3
    element_ids = connect_ref[...].astype(jnp.float32)
    elements = element_ids.shape[0]
    first_corner = element_ids[:, 0:1]
    last_corner = element_ids[:, SIDE - 1 : SIDE]
    lane = lax.broadcasted_iota(jnp.int32, (1, LANES), 1)
    ids_parts = split_two(element_ids)
    placed = [dot(ids_parts[0], place_ref[r]) + dot(ids_parts[1], place_ref[r]) for r in range(2)]
    diagonal = lax.broadcasted_iota(jnp.int32, (elements, elements), 0) == lax.broadcasted_iota(
        jnp.int32, (elements, elements), 1
    )
    lengths = [
        jnp.sum(jnp.where(diagonal, extents_ref[axis : axis + 1, :], 0.0), axis=1, keepdims=True)
        for axis in range(2)
    ]
    plane = plane_ref[0]
    held = [jnp.zeros((1, 1), jnp.float32) for _ in range(4)]
    picked = [
        jnp.where(first_corner == float(own_nodes + 6 * row), 1.0, 0.0) for row in range(2)
    ]
    ids_ref[...] = jnp.full(ids_ref.shape, -1, jnp.int32)
    owned = (lane >= ROWS) & (lane < GRID)
    for column in range(COLS):
        ids = jnp.zeros((1, LANES), jnp.float32)
        own = jnp.where(plane == column, 1.0, 0.0)
        for row in range(2):
            ids = ids + jnp.sum(placed[row] * picked[row], axis=0, keepdims=True)
            for axis in range(2):
                length = jnp.sum(lengths[axis] * picked[row], axis=0, keepdims=True)
                at = 2 * axis + row
                held[at] = held[at] + own * length
            if column < COLS - 1:
                corner = jnp.sum(last_corner * picked[row], axis=0, keepdims=True)
                picked[row] = jnp.where(first_corner == corner, 1.0, 0.0)
        ids = jnp.where(owned, ids.astype(jnp.int32), -1)
        ids_ref[column : column + 1, :] = ids
    for at in range(4):
        extents_out_ref[at : at + 1, :] = jnp.broadcast_to(held[at], (1, LANES))
    extents_out_ref[4:8, :] = jnp.zeros((4, LANES), jnp.float32)
    chosen = jnp.concatenate(
        [one_hot(ids_ref[pl.ds(plane ^ slot, 1), :], own_nodes) for slot in range(COLS)], axis=1
    )
    copies[3].wait()
    both = dot(jnp.concatenate(split_two(velocity_ref[...]), axis=0), chosen)
    both = both[: 3 * modes, :] + both[3 * modes :, :]
    for slot in range(COLS):
        values = both[:, slot * LANES : (slot + 1) * LANES]
        last = values[2 * modes :, :]
        for c in range(2):
            spread = pltpu.roll(last, OWNED - c * (OWNED // 2), 1)
            slots[slot][:, c * LANES : (c + 1) * LANES] = jnp.where(
                owned, values[c * modes : (c + 1) * modes, :], spread
            )


def three_of(packed):
    lower = packed[:, :LANES]
    upper = packed[:, LANES:]
    lane = lax.broadcasted_iota(jnp.int32, lower.shape, 1)
    last = jnp.where(
        lane < ROWS + OWNED // 2,
        pltpu.roll(lower, LANES - OWNED, 1),
        pltpu.roll(upper, LANES - OWNED // 2, 1),
    )
    return lower, upper, last


def setup_kernel(
    extents_ref, fourier_hbm, plane_hbm, mass_hbm,
    fourier_ref, in_plane_ref, row_ref, plane_ref, mass_ref, arrived,
):
    copies = [
        pltpu.make_async_copy(mass_hbm, mass_ref, arrived.at[0]),
        pltpu.make_async_copy(plane_hbm, plane_ref, arrived.at[1]),
        pltpu.make_async_copy(fourier_hbm, fourier_ref, arrived.at[2]),
    ]
    for copy in copies:
        copy.start()
    hx = [extents_ref[at : at + 1, :] for at in range(2)]
    hy = [extents_ref[2 + at : 3 + at, :] for at in range(2)]
    lane = lax.broadcasted_iota(jnp.int32, (1, LANES), 1)
    carried = jnp.zeros((1, LANES), jnp.float32)
    for at, value in enumerate((hx[0], hx[1], hy[0], hy[1])):
        carried = carried + jnp.where(lane == at, value, 0.0)
    copies[0].wait()
    mass = sum((hx[r] * hy[r] / 4.0) * mass_ref[r : r + 1, :] for r in range(2))
    row_ref[...] = jnp.concatenate([mass, carried, jnp.zeros((6, LANES), jnp.float32)], axis=0)
    copies[1].wait()
    along = sum((hy[r] / 2.0) * plane_ref[r] for r in range(2)) + plane_ref[8]
    across = sum((hx[r] / 2.0) * plane_ref[2 + r] for r in range(2)) + plane_ref[9]
    stiff = sum(
        (hy[r] / hx[r]) * plane_ref[4 + r] + (hx[r] / hy[r]) * plane_ref[6 + r] for r in range(2)
    )
    high, low = split_two(jnp.concatenate([along, across, viscosity * stiff], axis=0))
    in_plane_ref[0] = high
    in_plane_ref[1] = low
    copies[2].wait()


def residual_kernel(
    modes, plane_at, slot_a, slot_b, slot_c, slot_d, fourier_ref, in_plane_ref, row_ref,
    out_ref, packed_ref,
):
    planes = PLANES
    groups = planes // modes
    for slot, slot_ref in enumerate((slot_a, slot_b, slot_c, slot_d)):
        start = pl.multiple_of((plane_at[0] ^ slot) * modes, modes)
        packed_ref[pl.ds(start, modes), :] = slot_ref[...]
    packed = packed_ref[...]
    synthesis = (fourier_ref[0, :, :planes], fourier_ref[1, :, :planes])
    forward = (fourier_ref[0, :, planes:], fourier_ref[1, :, planes:])
    speeds = three_of(packed)
    fields = three_of(dot_split(synthesis, split_two(packed)))
    mass = row_ref[0:1, :]
    carried = row_ref[1:2, :]
    products = [[fields[a] * fields[c] for a in range(3)] for c in range(3)]
    flux = jnp.concatenate(
        [jnp.concatenate([products[c][0], products[c][1], fields[c]], axis=1) for c in range(3)],
        axis=0,
    )
    divergence = dot_split(split_two(flux), (in_plane_ref[0], in_plane_ref[1]))
    divergence = [divergence[c * planes : (c + 1) * planes, :] for c in range(3)]
    lane = lax.broadcasted_iota(jnp.int32, (planes, LANES), 1)
    divergence[1] = jnp.where(
        (lane >= FIRST) & (lane < SECOND),
        pltpu.roll(products[2][2], FIRST - 6 * ROWS, 1),
        divergence[1],
    )
    spill = jnp.zeros((planes, LANES), jnp.float32)
    last = 6 * ROWS + FITTING
    for c in range(3):
        start = SPILL * (c + 1)
        spill = jnp.where(
            (lane >= start) & (lane < start + ROWS - FITTING),
            pltpu.roll(products[c][1], LANES + start - last, 1),
            spill,
        )
    upper = jnp.concatenate(divergence + [spill], axis=1)
    lower = jnp.concatenate([mass * products[c][2] for c in range(3)] + [spill * 0.0], axis=1)
    result = dot_split(forward, split_two(jnp.concatenate([upper, lower], axis=0)))
    mode = lax.broadcasted_iota(jnp.int32, (planes, LANES), 0)
    wave = span_wave * jnp.where(mode == 1, planes // 2, mode // 2).astype(jnp.float32)
    square = wave * wave
    blocks = planes // 8
    per_group = modes // 8
    tiles = []
    for c in range(3):
        tile = result[:, c * LANES : (c + 1) * LANES] - square * (mass * speeds[c])
        handed = pltpu.roll(speeds[c], SPEED - 6 * ROWS, 1)
        tiles.append(jnp.where((lane >= SPEED) & (lane < FIRST), handed, tile))
    spilled = result[:, 3 * LANES :]
    for block in range(blocks):
        start = CHUNK * ((block % per_group) * groups + block // per_group)
        for c in range(3):
            out_ref[start + 8 * c : start + 8 * c + 8, :] = tiles[c][8 * block : 8 * block + 8, :]
        row = pltpu.roll(spilled[8 * block : 8 * block + 8, :], 0, 1, stride=2, stride_axis=0)
        out_ref[start + 24 : start + 25, :] = jnp.sum(row, axis=0, keepdims=True) + carried


def apply_line(stiffness, values):
    even = [values[k] + values[6 - k] for k in range(3)] + [values[3]]
    odd = [values[k] - values[6 - k] for k in range(3)]
    result = [None] * 7
    for i in range(4):
        total = float(stiffness[i, 3]) * even[3]
        for k in range(3):
            total = total + float((stiffness[i, k] + stiffness[i, 6 - k]) / 2) * even[k]
        if i == 3:
            result[3] = total
            continue
        other = float((stiffness[i, 0] - stiffness[i, 6]) / 2) * odd[0]
        for k in range(1, 3):
            other = other + float((stiffness[i, k] - stiffness[i, 6 - k]) / 2) * odd[k]
        result[i] = total + other
        result[6 - i] = total - other
    return result


def cg_kernel(
    columns, first_ref, in_ref,
    out_ref, grid_ref, turn_ref, rest_ref, way_ref, image_ref, sum_ref,
):
    weights, derivative, stiffness = gll_one_d()
    lane = lax.broadcasted_iota(jnp.int32, (8, LANES), 1)
    at = lane % columns

    def node(i, y):
        start = (ROWS * i + y) * 8
        return slice(start, start + 8)

    def from_next(value):
        return jnp.where(
            at == columns - 1,
            pltpu.roll(value, columns - 1, 1),
            pltpu.roll(value, LANES - 1, 1),
        )

    def from_previous(value):
        return jnp.where(
            at == 0,
            pltpu.roll(value, LANES - columns + 1, 1),
            pltpu.roll(value, 1, 1),
        )

    same = (
        lax.broadcasted_iota(jnp.int32, (LANES, LANES), 0) // columns
        == lax.broadcasted_iota(jnp.int32, (LANES, LANES), 1) // columns
    )
    ones = jnp.where(same, 1.0, 0.0).astype(jnp.bfloat16)
    ones = jnp.concatenate([ones, ones, ones], axis=0)

    def over_columns(value):
        return dot(jnp.concatenate(split_three(value), axis=1), ones)

    blank = jnp.zeros((LANES - 3 * columns, LANES), jnp.float32)
    for mode in range(8):
        rows = [in_ref[pl.ds(8 * c + mode, columns, stride=CHUNK), :] for c in range(3)]
        turned = jnp.concatenate(rows + [blank], axis=0).T
        grid_ref[pl.ds(mode, LANES, stride=8), :] = turned

    extras = in_ref[pl.ds(CHUNK - 1, columns, stride=CHUNK), :]
    turn_ref[...] = jnp.concatenate([extras] * (LANES // columns), axis=0).T
    hx = [jnp.broadcast_to(turn_ref[at : at + 1, :], (8, LANES)) for at in range(2)]
    hy = [jnp.broadcast_to(turn_ref[2 + at : 3 + at, :], (8, LANES)) for at in range(2)]
    mode = first_ref[0] + lax.broadcasted_iota(jnp.int32, (8, LANES), 0)
    wave = span_wave * jnp.where(mode == 1, PLANES // 2, mode // 2).astype(jnp.float32)
    pair_wave = span_wave * (mode // 2).astype(jnp.float32)
    helmholtz = inverse_step + wave * wave
    ratio_along = [hy[r] / hx[r] for r in range(2)]
    ratio_across = [hx[r] / hy[r] for r in range(2)]
    mass = [helmholtz * (hx[r] * hy[r] / 4.0) for r in range(2)]

    def over_rows(pair, y):
        if y < 6:
            return float(weights[y]) * pair[0]
        if y > 6:
            return float(weights[y - 6]) * pair[1]
        return float(weights[6]) * pair[0] + float(weights[0]) * pair[1]

    def shared(pair):
        return [
            float(weights[0]) * value + float(weights[6]) * from_previous(value) for value in pair
        ]

    mass_shared = shared(mass)
    across_shared = shared(ratio_across)

    group = lane // columns

    def handed(start, y):
        return from_previous(grid_ref[(start + y) * 8 : (start + y) * 8 + 8, :])

    def spilled(y):
        rows = [
            turn_ref[pl.ds(SPILL * (c + 1) + y - FITTING, 8, stride=2), :] for c in range(3)
        ]
        return from_previous(
            jnp.where(group == 0, rows[0], jnp.where(group == 1, rows[1], rows[2]))
        )

    first_speed = [handed(SPEED, y) for y in range(ROWS)]
    first = [handed(FIRST, y) for y in range(ROWS)]
    second = [handed(SECOND, y) if y < FITTING else spilled(y) for y in range(ROWS)]
    sloped = weights[:, None] * derivative
    lines = [jnp.zeros((8, LANES), jnp.float32)] * ROWS
    for r in range(2):
        rows = range(6 * r, 6 * r + SIDE)
        curved = apply_line(stiffness, [first_speed[y] for y in rows])
        for j, y in enumerate(rows):
            slope = sum(float(sloped[j, k]) * second[6 * r + k] for k in range(SIDE))
            lines[y] = lines[y] + float(weights[0]) * (
                (0.5 * hx[r]) * slope - ratio_across[r] * curved[j]
            )
    area = [0.25 * hx[r] * hy[r] for r in range(2)]
    half = [0.5 * hy[r] for r in range(2)]
    even = mode % 2 == 0
    total = jnp.zeros((8, LANES), jnp.float32)
    for y in range(ROWS):
        along = jnp.where(group == 1, pltpu.roll(second[y], columns, 1), first[y])
        span = jnp.where(
            group == 0,
            pltpu.roll(first[y], 2 * columns, 1),
            jnp.where(
                group == 1,
                pltpu.roll(second[y], LANES - columns, 1),
                pltpu.roll(first[y], columns, 1),
            ),
        )
        span = jnp.where(even, pltpu.roll(span, 7, 0), -pltpu.roll(span, 1, 0))
        across = lines[y] + float(weights[0]) * over_rows(area, y) * (
            pair_wave * span - (wave * wave) * first_speed[y]
        )
        flux = over_rows(half, y) * along
        speed = over_rows(ratio_along, y) * first_speed[y]
        values = [
            grid_ref[node(i, y), :]
            + float(sloped[i, 0]) * flux
            - float(stiffness[i, 0]) * speed
            for i in range(SIDE)
        ]
        values[0] = values[0] + across + from_previous(values[6])
        for i in range(6):
            value = values[i]
            rest_ref[node(i, y), :] = value
            total = total + value * value
    rest_norm = over_columns(total)

    first_turn = None

    def apply(size, turn):
        for y in range(ROWS):
            values = []
            for i in range(6):
                value = rest_ref[node(i, y), :]
                if turn is not None:
                    before = way_ref[node(i, y), :]
                    moved = size * before
                    if turn is not first_turn:
                        moved = sum_ref[node(i, y), :] + moved
                    sum_ref[node(i, y), :] = moved
                    value = value + turn * before
                way_ref[node(i, y), :] = value
                values.append(value)
            values.append(from_next(values[0]))
            lines = apply_line(stiffness, values)
            along = over_rows(ratio_along, y)
            lines = [along * line for line in lines]
            lines[0] = lines[0] + from_previous(lines[6])
            inner = over_rows(mass, y)
            inner = [None] + [float(weights[i]) * inner for i in range(1, 4)]
            inner = [over_rows(mass_shared, y)] + inner[1:] + [inner[2], inner[1]]
            for i in range(6):
                image_ref[node(i, y), :] = lines[i] + inner[i] * values[i]
        total = jnp.zeros((8, LANES), jnp.float32)
        for i in range(6):
            values = [way_ref[node(i, y), :] for y in range(ROWS)]
            lower = apply_line(stiffness, values[:7])
            upper = apply_line(stiffness, values[6:])
            if i == 0:
                scale = across_shared
            else:
                scale = [float(weights[i]) * value for value in ratio_across]
            lower = [scale[0] * value for value in lower]
            upper = [scale[1] * value for value in upper]
            lines = lower[:6] + [lower[6] + upper[0]] + upper[1:]
            for y in range(ROWS):
                image = image_ref[node(i, y), :] + lines[y]
                image_ref[node(i, y), :] = image
                total = total + values[y] * image
        return over_columns(total)

    size = turn = None
    for iteration in range(ITERS):
        if iteration == 1:
            first_turn = turn
        size = rest_norm / apply(size, turn)
        if iteration == ITERS - 1:
            break
        total = jnp.zeros((8, LANES), jnp.float32)
        for y in range(ROWS):
            for i in range(6):
                rest = rest_ref[node(i, y), :] - size * image_ref[node(i, y), :]
                rest_ref[node(i, y), :] = rest
                total = total + rest * rest
        following = over_columns(total)
        turn = following / rest_norm
        rest_norm = following
    zero = jnp.zeros((8, LANES), jnp.float32)
    for y in range(ROWS):
        grid_ref[node(0, y), :] = zero
        for i in range(6):
            value = sum_ref[node(i, y), :] + size * way_ref[node(i, y), :]
            if i == 0:
                grid_ref[node(6, y), :] = from_next(value)
            else:
                grid_ref[node(i, y), :] = value
    for left in range(GRID, LANES):
        grid_ref[left * 8 : left * 8 + 8, :] = zero
    parts = columns // COLS
    node_lane = lax.broadcasted_iota(jnp.int32, (3 * parts, LANES), 1)
    owned = (node_lane >= ROWS) & (node_lane < GRID)
    for mode in range(8):
        turn_ref[...] = grid_ref[pl.ds(mode, LANES, stride=8), :].T
        pieces = [turn_ref[pl.ds(k, 3 * parts, stride=COLS), :] for k in range(COLS)]
        for k in range(COLS - 1):
            spread = pltpu.roll(pieces[-1], OWNED - k * THIRD, 1)
            piece = jnp.where(owned, pieces[k], spread)
            for c in range(3):
                out_ref[pl.ds(24 * k + 8 * c + mode, parts, stride=72), :] = piece[
                    c * parts : (c + 1) * parts, :
                ]


def choice_kernel(ids_ref, out_ref):
    nodes = lax.broadcasted_iota(jnp.int32, (LANES, out_ref.shape[1]), 1)
    for column in range(COLS):
        ids = jnp.broadcast_to(ids_ref[column : column + 1, :].astype(jnp.float32), (LANES, LANES))
        ids = ids.T[:, 0:1].astype(jnp.int32)
        out_ref[column * LANES : (column + 1) * LANES, :] = jnp.where(
            nodes == ids, 1.0, 0.0
        ).astype(jnp.bfloat16)


def scatter_kernel(velocity_ref, change_ref, chosen_ref, out_ref):
    rows = velocity_ref.shape[0]
    sources = change_ref.shape[0]
    pieces = []
    for column in range(COLS - 1):
        start = 24 * column
        pieces.append(
            jnp.concatenate(
                [
                    change_ref[m, start + 8 * c : start + 8 * c + 8, :]
                    for c in range(3)
                    for m in range(sources)
                ],
                axis=0,
            )
        )
    lane = lax.broadcasted_iota(jnp.int32, pieces[0].shape, 1)
    back = [pltpu.roll(pieces[k], LANES - OWNED + k * THIRD, 1) for k in range(COLS - 1)]
    pieces.append(
        jnp.where(
            lane < ROWS + THIRD, back[0], jnp.where(lane < ROWS + 2 * THIRD, back[1], back[2])
        )
    )
    parts = jnp.concatenate(split_two(jnp.concatenate(pieces, axis=1)), axis=0)
    change = dot(parts, chosen_ref[...])
    out_ref[...] = velocity_ref[...] + (change[:rows, :] + change[rows:, :])


def call(kernel, out_shape, scratch=(), spaces="", cost=None):
    place = {
        "s": pl.BlockSpec(memory_space=pltpu.SMEM),
        "v": pl.BlockSpec(memory_space=pltpu.VMEM),
        "h": pl.BlockSpec(memory_space=pltpu.HBM),
    }
    many = isinstance(out_shape, tuple)
    run = pl.pallas_call(
        kernel,
        out_shape=out_shape,
        in_specs=[place[space] for space in spaces],
        out_specs=(place["v"],) * len(out_shape) if many else place["v"],
        scratch_shapes=list(scratch),
        cost_estimate=cost,
        compiler_params=pltpu.CompilerParams(vmem_limit_bytes=16 * 2**20),
    )

    def with_spaces(*operands):
        return run(
            *(
                pltpu.with_memory_space_constraint(operand, pltpu.HBM) if space == "h" else operand
                for space, operand in zip(spaces, operands)
            )
        )

    return with_spaces


def transposed(velocity, connect, right_list, extents):
    components, modes, own_nodes = velocity.shape
    groups = lax.axis_size("planes")
    parts = lax.axis_size("mesh")
    plane = lax.axis_index("planes")
    part = lax.axis_index("mesh")
    rows = components * modes
    columns = parts * COLS
    synthesis, forward = fourier_tables(PLANES)
    forward = np.concatenate([forward, span_forward(forward)], axis=1) * (-1.0 / viscosity)
    fourier = np.stack(two_parts(np.concatenate([synthesis, forward], axis=1)))
    matrices, masses = column_tables()
    place = np.stack([placement(row, True) for row in range(2)])
    flat = velocity.reshape(rows, own_nodes)
    f32 = jnp.float32
    slot_shape = jax.ShapeDtypeStruct((modes, 2 * LANES), f32)
    *slots, ids, column_extents = call(
        gather_kernel,
        (slot_shape,) * COLS
        + (
            jax.ShapeDtypeStruct((8, LANES), jnp.int32),
            jax.ShapeDtypeStruct((8, LANES), f32),
        ),
        scratch=(
            pltpu.VMEM(connect.shape[::-1], jnp.int32),
            pltpu.VMEM(extents.shape, f32),
            pltpu.VMEM(place.shape, jnp.bfloat16),
            pltpu.VMEM((rows, own_nodes), f32),
            pltpu.SemaphoreType.DMA((4,)),
        ),
        spaces="shhhh",
    )(plane.reshape(1), connect.T, extents, jnp.asarray(place, jnp.bfloat16), flat)
    slots = [slots[0]] + [
        lax.ppermute(slots[s], "planes", [(p, p ^ s) for p in range(groups)])
        for s in range(1, groups)
    ]
    tables = call(
        setup_kernel,
        (
            jax.ShapeDtypeStruct(fourier.shape, jnp.bfloat16),
            jax.ShapeDtypeStruct((2, 3 * LANES, LANES), jnp.bfloat16),
            jax.ShapeDtypeStruct((8, LANES), f32),
        ),
        scratch=(
            pltpu.VMEM(matrices.shape, f32),
            pltpu.VMEM(masses.shape, f32),
            pltpu.SemaphoreType.DMA((3,)),
        ),
        spaces="vhhh",
        cost=pl.CostEstimate(flops=10**6, bytes_accessed=3 * 10**6, transcendentals=0),
    )(column_extents, jnp.asarray(fourier), jnp.asarray(matrices), jnp.asarray(masses))
    residual = call(
        functools.partial(residual_kernel, modes),
        jax.ShapeDtypeStruct((columns * CHUNK, LANES), f32),
        scratch=(pltpu.VMEM((PLANES, 2 * LANES), f32),),
        spaces="svvvvvvv",
    )(plane.reshape(1), *slots, *tables)
    residual = lax.all_to_all(
        residual.reshape(columns * CHUNK, 1, LANES),
        ("mesh", "planes"),
        split_axis=0,
        concat_axis=0,
        tiled=True,
    )
    chosen = call(
        choice_kernel,
        jax.ShapeDtypeStruct((COLS * LANES, own_nodes), jnp.bfloat16),
        spaces="v",
        cost=pl.CostEstimate(flops=10**6, bytes_accessed=10**6, transcendentals=0),
    )(ids)
    held = pltpu.VMEM((96 * 8, LANES), f32)
    change = call(
        functools.partial(cg_kernel, columns),
        jax.ShapeDtypeStruct((parts * 72, LANES), f32),
        scratch=(pltpu.VMEM((LANES * 8, LANES), f32), pltpu.VMEM((LANES, LANES), f32))
        + (held,) * 4,
        spaces="sv",
    )((plane * modes + part * 8).reshape(1), residual.reshape(columns * CHUNK, LANES))
    change = lax.all_to_all(
        change.reshape(parts, 72, LANES), "mesh", split_axis=0, concat_axis=0, tiled=True
    )
    result = call(scatter_kernel, jax.ShapeDtypeStruct((rows, own_nodes), f32), spaces="vvv")(
        flat, change, chosen
    )
    return result.reshape(velocity.shape)


def from_behind(value, axis, by):
    peers = lax.axis_size(axis)
    return lax.ppermute(value, axis, [(i, (i + by) % peers) for i in range(peers)])


def partitioned(velocity, connect, right_list, extents):
    components, modes, own_nodes = velocity.shape
    edge_count = right_list.shape[0]
    first_mode = lax.axis_index("planes") * modes
    tables = [jnp.asarray(table, jnp.float32) for table in element_tables()]
    stiff_along, stiff_across, slope_along, slope_across, mass_weights = tables
    synthesis, forward = (jnp.asarray(t, jnp.float32) for t in fourier_tables(PLANES))
    hx, hy = extents[0], extents[1]
    mass_full = mass_weights[:, None] * (hx * hy / 4.0)[None, :]
    index_list = first_mode + jnp.arange(modes, dtype=jnp.int32)
    wave = span_wave * jnp.where(index_list == 1, PLANES // 2, index_list // 2).astype(jnp.float32)
    wave = wave[None, :, None, None]
    helmholtz = inverse_step + wave * wave
    locals_ = jnp.arange(own_nodes + edge_count, dtype=jnp.int32)
    chosen = (locals_[:, None, None] == connect[None]).astype(jnp.float32)
    at_edge = (locals_[:own_nodes, None] == right_list[None]).astype(jnp.float32)

    def contract(spec, *operands):
        return jnp.einsum(spec, *operands, precision=highest)

    physical = contract(
        "jq,cqn->cjn",
        synthesis,
        lax.all_to_all(velocity, "planes", split_axis=2, concat_axis=1, tiled=True),
    )
    pairs = ((0, 0), (0, 1), (0, 2), (1, 1), (1, 2), (2, 2))
    products = jnp.stack([physical[a] * physical[b] for a, b in pairs])
    product_hat = lax.all_to_all(
        contract("qj,fjn->fqn", forward, products), "planes", split_axis=1, concat_axis=2, tiled=True
    )

    def spread(fields):
        ghosts = from_behind(contract("cqn,ny->cqy", fields, at_edge), "mesh", 1)
        return contract("cqn,nke->cqke", jnp.concatenate([fields, ghosts], axis=2), chosen)

    def assemble(terms):
        summed = contract("cqke,nke->cqn", terms, chosen)
        returned = from_behind(summed[:, :, own_nodes:], "mesh", -1)
        return summed[:, :, :own_nodes] + contract("cqy,ny->cqn", returned, at_edge)

    def stiffness(values):
        return (hy / hx) * contract("lk,cqke->cqle", stiff_along, values) + (hx / hy) * contract(
            "lk,cqke->cqle", stiff_across, values
        )

    def dots(left, right):
        return lax.psum(jnp.sum(left * right, axis=2), "mesh")

    values = spread(jnp.concatenate([velocity, product_hat], axis=0))
    speeds, along = values[0:3], values[3:6]
    across = jnp.stack([values[4], values[6], values[7]])
    span = jnp.stack([values[5], values[7], values[8]])
    shaped = span.reshape(span.shape[0], modes // 2, 2, *span.shape[2:])
    turned = jnp.stack([shaped[:, :, 1], -shaped[:, :, 0]], axis=2).reshape(span.shape)
    pair_wave = span_wave * (index_list // 2).astype(jnp.float32)[None, :, None, None]
    advection = (hy / 2.0) * contract("lk,cqke->cqle", slope_along, along)
    advection = advection + (hx / 2.0) * contract("lk,cqke->cqle", slope_across, across)
    advection = advection + mass_full * (pair_wave * turned)
    residual = assemble(
        -(wave * wave) * mass_full * speeds - stiffness(speeds) - advection / viscosity
    )
    solution = velocity
    direction = residual
    norm_now = dots(residual, residual)
    for _ in range(ITERS):
        values = spread(direction)
        operated = assemble(stiffness(values) + helmholtz * mass_full * values)
        step_size = (norm_now / dots(direction, operated))[:, :, None]
        solution = solution + step_size * direction
        residual = residual - step_size * operated
        norm_next = dots(residual, residual)
        direction = residual + (norm_next / norm_now)[:, :, None] * direction
        norm_now = norm_next
    return solution


def on_device(velocity, connect, right_list, extents):
    groups = lax.axis_size("planes")
    parts = lax.axis_size("mesh")
    modes = velocity.shape[1]
    fits = groups == COLS and modes == 8 * parts and 3 * parts * COLS <= LANES
    step = transposed if fits else partitioned
    return step(velocity, connect, right_list, extents)


def solution(mesh):
    placed = (P(None, "planes", "mesh"), P(None, "mesh"), P("mesh"), P(None, "mesh"))
    return jax.shard_map(
        on_device, mesh=mesh, in_specs=placed, out_specs=P(None, "planes", "mesh"), check_vma=False
    )
```

```python
import functools

import jax
import jax.numpy as jnp
import numpy as np
from jax import lax
from jax.experimental import pallas as pl
from jax.experimental.pallas import tpu as pltpu
from jax.sharding import PartitionSpec as P

PLANES = 256
ITERS = 4
SIDE = 7
ROWS = 13
COLS = 4
GRID = SIDE * ROWS
LANES = 128
SPEED = GRID
FIRST = GRID + ROWS
SECOND = GRID + 2 * ROWS
FITTING = LANES - SECOND
SPILL = 16
CHUNK = 25
OWNED = GRID - ROWS
HALF = OWNED // 2
THIRD = OWNED // 3

highest = lax.Precision.HIGHEST
viscosity = 0.002
time_step = 3e-05
span_wave = 4.0
inverse_step = 1.0 / (viscosity * time_step)


def legendre_six(points):
    previous = 0.0 * points + 1.0
    current = 1.0 * points
    for order in range(1, 6):
        following = ((2 * order + 1) * points * current - order * previous) / (order + 1)
        previous = current
        current = following
    return current


def gll_one_d():
    degree = 6
    points = np.array(
        [
            -1.0,
            -0.830223896278567,
            -0.4688487934707142,
            0.0,
            0.4688487934707142,
            0.830223896278567,
            1.0,
        ]
    )
    values = legendre_six(points)
    weights = 2.0 / (degree * (degree + 1) * values**2)
    derivative = np.zeros((degree + 1, degree + 1))
    for row_index in range(degree + 1):
        for col_index in range(degree + 1):
            if row_index != col_index:
                derivative[row_index, col_index] = values[row_index] / (
                    values[col_index] * (points[row_index] - points[col_index])
                )
    derivative[0, 0] = -degree * (degree + 1) / 4.0
    derivative[degree, degree] = degree * (degree + 1) / 4.0
    stiffness = derivative.T @ (weights[:, None] * derivative)
    return weights, derivative, stiffness


def element_tables():
    weights, derivative, stiffness = gll_one_d()
    identity = np.eye(SIDE)
    mass_weights = np.kron(weights, weights)
    return (
        np.kron(np.diag(weights), stiffness),
        np.kron(stiffness, np.diag(weights)),
        mass_weights[:, None] * np.kron(identity, derivative),
        mass_weights[:, None] * np.kron(derivative, identity),
        mass_weights,
    )


def fourier_tables(planes):
    plane_grid = np.arange(planes)
    synthesis = np.zeros((planes, planes))
    forward = np.zeros((planes, planes))
    synthesis[:, 0] = 1.0
    synthesis[:, 1] = np.cos(np.pi * plane_grid)
    forward[0] = 1.0 / planes
    forward[1] = np.cos(np.pi * plane_grid) / planes
    for wavenumber in range(1, planes // 2):
        phase_angle = 2.0 * np.pi * wavenumber * plane_grid / planes
        synthesis[:, 2 * wavenumber] = np.cos(phase_angle)
        synthesis[:, 2 * wavenumber + 1] = np.sin(phase_angle)
        forward[2 * wavenumber] = 2.0 * np.cos(phase_angle) / planes
        forward[2 * wavenumber + 1] = 2.0 * np.sin(phase_angle) / planes
    return synthesis, forward


def span_forward(forward):
    turned = np.zeros_like(forward)
    for wavenumber in range(1, forward.shape[0] // 2):
        turned[2 * wavenumber] = span_wave * wavenumber * forward[2 * wavenumber + 1]
        turned[2 * wavenumber + 1] = -span_wave * wavenumber * forward[2 * wavenumber]
    return turned


def two_parts(table):
    table = np.asarray(table, np.float32)
    high = table.astype(jnp.bfloat16)
    low = (table - high.astype(np.float32)).astype(jnp.bfloat16)
    return high, low


def placement(row, skip_shared):
    table = np.zeros((SIDE * SIDE, LANES))
    for j in range(SIDE):
        if skip_shared and row == 1 and j == 0:
            continue
        for i in range(SIDE):
            table[SIDE * j + i, ROWS * i + 6 * row + j] = 1.0
    return table


def column_tables():
    stiff_along, stiff_across, slope_along, slope_across, mass_weights = element_tables()
    owned = np.arange(LANES)
    owned = (owned >= ROWS) & (owned < GRID)
    matrices = []
    for table in (slope_along, slope_across, stiff_along, stiff_across):
        for row in range(2):
            place = placement(row, False)
            matrices.append((place.T @ table.T @ place) * owned[:, None])
    for start in (FIRST, SECOND):
        matrix = np.zeros((LANES, LANES))
        for y in range(ROWS):
            if start + y < LANES:
                matrix[6 * ROWS + y, start + y] = 1.0
        matrices.append(matrix)
    masses = [(mass_weights @ placement(row, False)) * owned for row in range(2)]
    return np.stack(matrices).astype(np.float32), np.stack(masses).astype(np.float32)


def split_two(value):
    high = value.astype(jnp.bfloat16)
    low = (value - high.astype(jnp.float32)).astype(jnp.bfloat16)
    return high, low


def split_three(value):
    high = value.astype(jnp.bfloat16)
    rest = value - high.astype(jnp.float32)
    middle = rest.astype(jnp.bfloat16)
    low = (rest - middle.astype(jnp.float32)).astype(jnp.bfloat16)
    return high, middle, low


def dot(left, right):
    return jnp.dot(left, right, preferred_element_type=jnp.float32)


def dot_split(left, right):
    return dot(left[0], right[0]) + (dot(left[0], right[1]) + dot(left[1], right[0]))


def one_hot(ids_row, count):
    rows = lax.broadcasted_iota(jnp.int32, (count, LANES), 0)
    return jnp.where(rows == ids_row, 1.0, 0.0).astype(jnp.bfloat16)


def element_order(element_ids, own_nodes):
    wide = (element_ids.shape[0], LANES)
    first_corner = jnp.broadcast_to(element_ids[:, 0:1], wide)
    last_corner = jnp.broadcast_to(element_ids[:, SIDE - 1 : SIDE], wide)
    picked = [
        jnp.where(first_corner == float(own_nodes + 6 * row), 1.0, 0.0) for row in range(2)
    ]
    order = [picked]
    for _ in range(COLS - 1):
        corners = [jnp.sum(last_corner * mask, axis=0, keepdims=True) for mask in picked]
        picked = [jnp.where(first_corner == corner, 1.0, 0.0) for corner in corners]
        order.append(picked)
    return order


def gather_kernel(
    plane_ref, connect_hbm, place_hbm, velocity_hbm,
    slot_a, slot_b, slot_c, slot_d, ids_ref,
    connect_ref, place_ref, velocity_ref, arrived,
):
    slots = (slot_a, slot_b, slot_c, slot_d)
    sources = (connect_hbm, place_hbm, velocity_hbm)
    targets = (connect_ref, place_ref, velocity_ref)
    copies = [
        pltpu.make_async_copy(source, target, arrived.at[at])
        for at, (source, target) in enumerate(zip(sources, targets))
    ]
    for copy in copies:
        copy.start()
    own_nodes = velocity_ref.shape[1]
    modes = velocity_ref.shape[0] // 3
    lane = lax.broadcasted_iota(jnp.int32, (1, LANES), 1)
    owned = (lane >= ROWS) & (lane < GRID)
    plane = plane_ref[0]
    copies[0].wait()
    element_ids = connect_ref[...].astype(jnp.float32)
    order = element_order(element_ids, own_nodes)
    ids_parts = split_two(element_ids)
    copies[1].wait()
    placed = [dot(ids_parts[0], place_ref[r]) + dot(ids_parts[1], place_ref[r]) for r in range(2)]
    rows = []
    for column in range(COLS):
        picked = order[column]
        ids = jnp.sum(placed[0] * picked[0] + placed[1] * picked[1], axis=0, keepdims=True)
        rows.append(jnp.where(owned, ids.astype(jnp.int32), -1))
    ids_ref[...] = jnp.concatenate(rows + [jnp.full((8 - COLS, LANES), -1, jnp.int32)], axis=0)
    chosen = []
    for slot in range(COLS):
        ids = rows[0]
        for column in range(1, COLS):
            ids = jnp.where((plane ^ slot) == column, rows[column], ids)
        chosen.append(one_hot(ids, own_nodes))
    copies[2].wait()
    both = dot(
        jnp.concatenate(split_two(velocity_ref[...]), axis=0), jnp.concatenate(chosen, axis=1)
    )
    both = both[: 3 * modes, :] + both[3 * modes :, :]
    for slot in range(COLS):
        values = both[:, slot * LANES : (slot + 1) * LANES]
        last = values[2 * modes :, :]
        for c in range(2):
            spread = pltpu.roll(last, OWNED - c * HALF, 1)
            slots[slot][:, c * LANES : (c + 1) * LANES] = jnp.where(
                owned, values[c * modes : (c + 1) * modes, :], spread
            )


def three_of(packed):
    lower = packed[:, :LANES]
    upper = packed[:, LANES:]
    lane = lax.broadcasted_iota(jnp.int32, lower.shape, 1)
    last = jnp.where(
        lane < ROWS + HALF,
        pltpu.roll(lower, LANES - OWNED, 1),
        pltpu.roll(upper, LANES - HALF, 1),
    )
    return lower, upper, last


def setup_kernel(
    own_nodes, plane_at, connect_hbm, extents_hbm, fourier_hbm, plane_hbm, mass_hbm,
    fourier_ref, in_plane_ref, row_ref,
    connect_ref, extents_ref, plane_ref, mass_ref, arrived,
):
    sources = (connect_hbm, extents_hbm, mass_hbm, plane_hbm, fourier_hbm)
    targets = (connect_ref, extents_ref, mass_ref, plane_ref, fourier_ref)
    copies = [
        pltpu.make_async_copy(source, target, arrived.at[at])
        for at, (source, target) in enumerate(zip(sources, targets))
    ]
    for copy in copies:
        copy.start()
    for copy in copies[:3]:
        copy.wait()
    element_ids = connect_ref[...].astype(jnp.float32)
    elements = element_ids.shape[0]
    order = element_order(element_ids, own_nodes)
    lane = lax.broadcasted_iota(jnp.int32, (1, LANES), 1)
    diagonal = lax.broadcasted_iota(jnp.int32, (elements, elements), 0) == lax.broadcasted_iota(
        jnp.int32, (elements, elements), 1
    )
    held = []
    for axis in range(2):
        lengths = jnp.sum(
            jnp.where(diagonal, extents_ref[axis : axis + 1, :], 0.0), axis=1, keepdims=True
        )
        for row in range(2):
            mask = order[0][row]
            for column in range(1, COLS):
                mask = jnp.where(plane_at[0] == column, order[column][row], mask)
            held.append(jnp.sum(lengths * mask, axis=0, keepdims=True))
    hx, hy = held[:2], held[2:]
    carried = jnp.zeros((1, LANES), jnp.float32)
    for at, value in enumerate(held):
        carried = carried + jnp.where(lane == at, value, 0.0)
    mass = sum((hx[r] * hy[r] / 4.0) * mass_ref[r : r + 1, :] for r in range(2))
    row_ref[...] = jnp.concatenate([mass, carried, jnp.zeros((6, LANES), jnp.float32)], axis=0)
    copies[3].wait()
    along = sum((hy[r] / 2.0) * plane_ref[r] for r in range(2)) + plane_ref[8]
    across = sum((hx[r] / 2.0) * plane_ref[2 + r] for r in range(2)) + plane_ref[9]
    stiff = viscosity * sum(
        (hy[r] / hx[r]) * plane_ref[4 + r] + (hx[r] / hy[r]) * plane_ref[6 + r] for r in range(2)
    )
    at_row = lax.broadcasted_iota(jnp.int32, (LANES, LANES), 0)
    middle = ROWS + HALF
    lower = jnp.where(at_row < middle, stiff, 0.0)
    upper = jnp.where(at_row >= middle, stiff, 0.0)
    high, low = split_two(
        jnp.concatenate(
            [along + pltpu.roll(lower, OWNED, 0), across + pltpu.roll(upper, OWNED - HALF, 0)],
            axis=0,
        )
    )
    in_plane_ref[0] = high
    in_plane_ref[1] = low
    copies[4].wait()


def residual_kernel(
    modes, plane_at, slot_a, slot_b, slot_c, slot_d, fourier_ref, in_plane_ref, row_ref,
    out_ref, packed_ref,
):
    planes = PLANES
    groups = planes // modes
    for slot, slot_ref in enumerate((slot_a, slot_b, slot_c, slot_d)):
        start = pl.multiple_of((plane_at[0] ^ slot) * modes, modes)
        packed_ref[pl.ds(start, modes), :] = slot_ref[...]
    packed = packed_ref[...]
    synthesis = (fourier_ref[0, :, :planes], fourier_ref[1, :, :planes])
    forward = (fourier_ref[0, :, planes:], fourier_ref[1, :, planes:])
    speeds = three_of(packed)
    physical = dot_split(synthesis, split_two(packed))
    fields = three_of(physical)
    mass = row_ref[0:1, :]
    carried = row_ref[1:2, :]
    products = [[fields[a] * fields[c] for a in range(3)] for c in range(3)]
    lane = lax.broadcasted_iota(jnp.int32, (planes, LANES), 1)
    owned = (lane >= ROWS) & (lane < GRID)
    flux = []
    for c in range(3):
        for half in range(2):
            if c == 2:
                spread = physical[:, half * LANES : (half + 1) * LANES]
            else:
                spread = pltpu.roll(fields[c], OWNED - half * HALF, 1)
            flux.append(jnp.where(owned, products[c][half], spread))
    flux = jnp.concatenate(
        [jnp.concatenate(flux[2 * c : 2 * c + 2], axis=1) for c in range(3)], axis=0
    )
    divergence = [
        dot_split(split_two(flux[c * planes : (c + 1) * planes, :]), (in_plane_ref[0], in_plane_ref[1]))
        for c in range(3)
    ]
    divergence[1] = jnp.where(
        (lane >= FIRST) & (lane < SECOND),
        pltpu.roll(products[2][2], FIRST - 6 * ROWS, 1),
        divergence[1],
    )
    spill = jnp.zeros((planes, LANES), jnp.float32)
    last = 6 * ROWS + FITTING
    for c in range(3):
        start = SPILL * (c + 1)
        spill = jnp.where(
            (lane >= start) & (lane < start + ROWS - FITTING),
            pltpu.roll(products[c][1], LANES + start - last, 1),
            spill,
        )
    upper = jnp.concatenate(divergence + [spill], axis=1)
    lower = jnp.concatenate([mass * products[c][2] for c in range(3)] + [spill * 0.0], axis=1)
    upper_parts, lower_parts = split_two(upper), split_two(lower[:, : 3 * LANES])
    from_upper = dot_split((forward[0][:, :planes], forward[1][:, :planes]), upper_parts)
    from_lower = dot_split((forward[0][:, planes:], forward[1][:, planes:]), lower_parts)
    result = jnp.concatenate([from_upper[:, : 3 * LANES] + from_lower, from_upper[:, 3 * LANES :]], axis=1)
    mode = lax.broadcasted_iota(jnp.int32, (planes, LANES), 0)
    wave = span_wave * jnp.where(mode == 1, planes // 2, mode // 2).astype(jnp.float32)
    square = wave * wave
    blocks = planes // 8
    per_group = modes // 8
    tiles = []
    for c in range(3):
        tile = result[:, c * LANES : (c + 1) * LANES] - square * (mass * speeds[c])
        handed = pltpu.roll(speeds[c], SPEED - 6 * ROWS, 1)
        tiles.append(jnp.where((lane >= SPEED) & (lane < FIRST), handed, tile))
    spilled = result[:, 3 * LANES :]
    for block in range(blocks):
        start = CHUNK * ((block % per_group) * groups + block // per_group)
        for c in range(3):
            out_ref[start + 8 * c : start + 8 * c + 8, :] = tiles[c][8 * block : 8 * block + 8, :]
        row = pltpu.roll(spilled[8 * block : 8 * block + 8, :], 0, 1, stride=2, stride_axis=0)
        out_ref[start + 24 : start + 25, :] = jnp.sum(row, axis=0, keepdims=True) + carried


def apply_line(stiffness, values):
    even = [values[k] + values[6 - k] for k in range(3)] + [values[3]]
    odd = [values[k] - values[6 - k] for k in range(3)]
    result = [None] * 7
    for i in range(4):
        total = float(stiffness[i, 3]) * even[3]
        for k in range(3):
            total = total + float((stiffness[i, k] + stiffness[i, 6 - k]) / 2) * even[k]
        if i == 3:
            result[3] = total
            continue
        other = float((stiffness[i, 0] - stiffness[i, 6]) / 2) * odd[0]
        for k in range(1, 3):
            other = other + float((stiffness[i, k] - stiffness[i, 6 - k]) / 2) * odd[k]
        result[i] = total + other
        result[6 - i] = total - other
    return result


def cg_kernel(
    columns, first_ref, in_ref,
    out_ref, grid_ref, turn_ref, rest_ref, image_ref, way_ref,
):
    weights, derivative, stiffness = gll_one_d()
    lane = lax.broadcasted_iota(jnp.int32, (8, LANES), 1)
    at = lane % columns

    def node(i, y):
        start = (ROWS * i + y) * 8
        return slice(start, start + 8)

    def from_next(value):
        return jnp.where(
            at == columns - 1,
            pltpu.roll(value, columns - 1, 1),
            pltpu.roll(value, LANES - 1, 1),
        )

    def from_previous(value):
        return jnp.where(
            at == 0,
            pltpu.roll(value, LANES - columns + 1, 1),
            pltpu.roll(value, 1, 1),
        )

    same = (
        lax.broadcasted_iota(jnp.int32, (LANES, LANES), 0) // columns
        == lax.broadcasted_iota(jnp.int32, (LANES, LANES), 1) // columns
    )
    ones = jnp.where(same, 1.0, 0.0).astype(jnp.bfloat16)
    ones = jnp.concatenate([ones, ones, ones], axis=0)

    def tree(values):
        return (values[0] + values[1]) + (values[2] + values[3]) + (values[4] + values[5])

    def over_columns(value):
        return dot(jnp.concatenate(split_three(value), axis=1), ones)

    blank = jnp.zeros((LANES - 3 * columns, LANES), jnp.float32)
    for mode in range(8):
        rows = [in_ref[pl.ds(8 * c + mode, columns, stride=CHUNK), :] for c in range(3)]
        turned = jnp.concatenate(rows + [blank], axis=0).T
        grid_ref[pl.ds(mode, LANES, stride=8), :] = turned

    extras = in_ref[pl.ds(CHUNK - 1, columns, stride=CHUNK), :]
    turn_ref[...] = jnp.concatenate([extras] * (LANES // columns), axis=0).T
    hx = [jnp.broadcast_to(turn_ref[at : at + 1, :], (8, LANES)) for at in range(2)]
    hy = [jnp.broadcast_to(turn_ref[2 + at : 3 + at, :], (8, LANES)) for at in range(2)]
    mode = first_ref[0] + lax.broadcasted_iota(jnp.int32, (8, LANES), 0)
    wave = span_wave * jnp.where(mode == 1, PLANES // 2, mode // 2).astype(jnp.float32)
    pair_wave = span_wave * (mode // 2).astype(jnp.float32)
    helmholtz = inverse_step + wave * wave
    ratio_along = [hy[r] / hx[r] for r in range(2)]
    ratio_across = [hx[r] / hy[r] for r in range(2)]
    mass = [helmholtz * (hx[r] * hy[r] / 4.0) for r in range(2)]

    def over_rows(pair, y):
        if y < 6:
            return float(weights[y]) * pair[0]
        if y > 6:
            return float(weights[y - 6]) * pair[1]
        return float(weights[6]) * pair[0] + float(weights[0]) * pair[1]

    def shared(pair):
        return [
            float(weights[0]) * value + float(weights[6]) * from_previous(value) for value in pair
        ]

    mass_shared = shared(mass)
    across_shared = shared(ratio_across)

    group = lane // columns

    def handed(start, y):
        return from_previous(grid_ref[(start + y) * 8 : (start + y) * 8 + 8, :])

    def spilled(y):
        rows = [
            turn_ref[pl.ds(SPILL * (c + 1) + y - FITTING, 8, stride=2), :] for c in range(3)
        ]
        return from_previous(
            jnp.where(group == 0, rows[0], jnp.where(group == 1, rows[1], rows[2]))
        )

    first_speed = [handed(SPEED, y) for y in range(ROWS)]
    first = [handed(FIRST, y) for y in range(ROWS)]
    second = [handed(SECOND, y) if y < FITTING else spilled(y) for y in range(ROWS)]
    sloped = weights[:, None] * derivative
    lines = [jnp.zeros((8, LANES), jnp.float32)] * ROWS
    for r in range(2):
        rows = range(6 * r, 6 * r + SIDE)
        curved = apply_line(stiffness, [first_speed[y] for y in rows])
        for j, y in enumerate(rows):
            slope = sum(float(sloped[j, k]) * second[6 * r + k] for k in range(SIDE))
            lines[y] = lines[y] + float(weights[0]) * (
                (0.5 * hx[r]) * slope - ratio_across[r] * curved[j]
            )
    area = [0.25 * hx[r] * hy[r] for r in range(2)]
    half = [0.5 * hy[r] for r in range(2)]
    even = mode % 2 == 0
    total = jnp.zeros((8, LANES), jnp.float32)
    for y in range(ROWS):
        along = jnp.where(group == 1, pltpu.roll(second[y], columns, 1), first[y])
        span = jnp.where(
            group == 0,
            pltpu.roll(first[y], 2 * columns, 1),
            jnp.where(
                group == 1,
                pltpu.roll(second[y], LANES - columns, 1),
                pltpu.roll(first[y], columns, 1),
            ),
        )
        span = jnp.where(even, pltpu.roll(span, 7, 0), -pltpu.roll(span, 1, 0))
        across = lines[y] + float(weights[0]) * over_rows(area, y) * (
            pair_wave * span - (wave * wave) * first_speed[y]
        )
        flux = over_rows(half, y) * along
        speed = over_rows(ratio_along, y) * first_speed[y]
        values = [
            grid_ref[node(i, y), :]
            + float(sloped[i, 0]) * flux
            - float(stiffness[i, 0]) * speed
            for i in range(SIDE)
        ]
        values[0] = values[0] + across + from_previous(values[6])
        for i in range(6):
            value = values[i]
            rest_ref[node(i, y), :] = value
            way_ref[0, node(i, y), :] = value
            total = total + value * value
    rest_norm = over_columns(total)

    def apply(iteration, turn):
        for y in range(ROWS):
            values = []
            for i in range(6):
                value = rest_ref[node(i, y), :]
                if iteration:
                    value = value + turn * way_ref[iteration - 1, node(i, y), :]
                    way_ref[iteration, node(i, y), :] = value
                values.append(value)
            values.append(from_next(values[0]))
            lines = apply_line(stiffness, values)
            along = over_rows(ratio_along, y)
            lines = [along * line for line in lines]
            lines[0] = lines[0] + from_previous(lines[6])
            inner = over_rows(mass, y)
            inner = [None] + [float(weights[i]) * inner for i in range(1, 4)]
            inner = [over_rows(mass_shared, y)] + inner[1:] + [inner[2], inner[1]]
            for i in range(6):
                image_ref[node(i, y), :] = lines[i] + inner[i] * values[i]
        totals = [jnp.zeros((8, LANES), jnp.float32)] * 6
        for i in range(6):
            values = [way_ref[iteration, node(i, y), :] for y in range(ROWS)]
            lower = apply_line(stiffness, values[:7])
            upper = apply_line(stiffness, values[6:])
            if i == 0:
                scale = across_shared
            else:
                scale = [float(weights[i]) * value for value in ratio_across]
            lower = [scale[0] * value for value in lower]
            upper = [scale[1] * value for value in upper]
            lines = lower[:6] + [lower[6] + upper[0]] + upper[1:]
            for y in range(ROWS):
                image = image_ref[node(i, y), :] + lines[y]
                image_ref[node(i, y), :] = image
                totals[y % 6] = totals[y % 6] + values[y] * image
        return over_columns(tree(totals))

    turn = None
    sizes = []
    for iteration in range(ITERS):
        size = rest_norm / apply(iteration, turn)
        sizes.append(size)
        if iteration == ITERS - 1:
            break
        totals = [jnp.zeros((8, LANES), jnp.float32)] * 6
        for y in range(ROWS):
            for i in range(6):
                rest = rest_ref[node(i, y), :] - size * image_ref[node(i, y), :]
                rest_ref[node(i, y), :] = rest
                totals[i] = totals[i] + rest * rest
        following = over_columns(tree(totals))
        turn = following / rest_norm
        rest_norm = following
    zero = jnp.zeros((8, LANES), jnp.float32)
    for y in range(ROWS):
        grid_ref[node(0, y), :] = zero
        for i in range(6):
            value = sizes[0] * way_ref[0, node(i, y), :]
            for step in range(1, ITERS):
                value = value + sizes[step] * way_ref[step, node(i, y), :]
            if i == 0:
                grid_ref[node(6, y), :] = from_next(value)
            else:
                grid_ref[node(i, y), :] = value
    for left in range(GRID, LANES):
        grid_ref[left * 8 : left * 8 + 8, :] = zero
    parts = columns // COLS
    node_lane = lax.broadcasted_iota(jnp.int32, (3 * parts, LANES), 1)
    owned = (node_lane >= ROWS) & (node_lane < GRID)
    for mode in range(8):
        turn_ref[...] = grid_ref[pl.ds(mode, LANES, stride=8), :].T
        pieces = [turn_ref[pl.ds(k, 3 * parts, stride=COLS), :] for k in range(COLS)]
        for k in range(COLS - 1):
            spread = pltpu.roll(pieces[-1], OWNED - k * THIRD, 1)
            piece = jnp.where(owned, pieces[k], spread)
            for c in range(3):
                out_ref[pl.ds(24 * k + 8 * c + mode, parts, stride=72), :] = piece[
                    c * parts : (c + 1) * parts, :
                ]


def choice_kernel(ids_ref, out_ref):
    nodes = lax.broadcasted_iota(jnp.int32, (LANES, out_ref.shape[1]), 1)
    for column in range(COLS):
        ids = jnp.broadcast_to(ids_ref[column : column + 1, :].astype(jnp.float32), (LANES, LANES))
        ids = ids.T[:, 0:1].astype(jnp.int32)
        out_ref[column * LANES : (column + 1) * LANES, :] = jnp.where(
            nodes == ids, 1.0, 0.0
        ).astype(jnp.bfloat16)


def scatter_kernel(velocity_ref, change_ref, chosen_ref, out_ref):
    rows = velocity_ref.shape[0]
    sources = change_ref.shape[0]
    pieces = []
    for column in range(COLS - 1):
        start = 24 * column
        pieces.append(
            jnp.concatenate(
                [
                    change_ref[m, start + 8 * c : start + 8 * c + 8, :]
                    for c in range(3)
                    for m in range(sources)
                ],
                axis=0,
            )
        )
    lane = lax.broadcasted_iota(jnp.int32, pieces[0].shape, 1)
    back = [pltpu.roll(pieces[k], LANES - OWNED + k * THIRD, 1) for k in range(COLS - 1)]
    pieces.append(
        jnp.where(
            lane < ROWS + THIRD, back[0], jnp.where(lane < ROWS + 2 * THIRD, back[1], back[2])
        )
    )
    parts = jnp.concatenate(split_two(jnp.concatenate(pieces, axis=1)), axis=0)
    change = dot(parts, chosen_ref[...])
    out_ref[...] = velocity_ref[...] + (change[:rows, :] + change[rows:, :])


def call(kernel, out_shape, scratch=(), spaces="", cost=None):
    place = {
        "s": pl.BlockSpec(memory_space=pltpu.SMEM),
        "v": pl.BlockSpec(memory_space=pltpu.VMEM),
        "h": pl.BlockSpec(memory_space=pltpu.HBM),
    }
    many = isinstance(out_shape, tuple)
    run = pl.pallas_call(
        kernel,
        out_shape=out_shape,
        in_specs=[place[space] for space in spaces],
        out_specs=(place["v"],) * len(out_shape) if many else place["v"],
        scratch_shapes=list(scratch),
        cost_estimate=cost,
        compiler_params=pltpu.CompilerParams(vmem_limit_bytes=16 * 2**20),
    )

    def with_spaces(*operands):
        return run(
            *(
                pltpu.with_memory_space_constraint(operand, pltpu.HBM) if space == "h" else operand
                for space, operand in zip(spaces, operands)
            )
        )

    return with_spaces


def transposed(velocity, connect, right_list, extents):
    components, modes, own_nodes = velocity.shape
    groups = lax.axis_size("planes")
    parts = lax.axis_size("mesh")
    plane = lax.axis_index("planes")
    part = lax.axis_index("mesh")
    rows = components * modes
    columns = parts * COLS
    synthesis, forward = fourier_tables(PLANES)
    forward = np.concatenate([forward, span_forward(forward)], axis=1) * (-1.0 / viscosity)
    fourier = np.stack(two_parts(np.concatenate([synthesis, forward], axis=1)))
    matrices, masses = column_tables()
    place = np.stack([placement(row, True) for row in range(2)])
    flat = velocity.reshape(rows, own_nodes)
    f32 = jnp.float32
    slot_shape = jax.ShapeDtypeStruct((modes, 2 * LANES), f32)
    *slots, ids = call(
        gather_kernel,
        (slot_shape,) * COLS + (jax.ShapeDtypeStruct((8, LANES), jnp.int32),),
        scratch=(
            pltpu.VMEM(connect.shape[::-1], jnp.int32),
            pltpu.VMEM(place.shape, jnp.bfloat16),
            pltpu.VMEM((rows, own_nodes), f32),
            pltpu.SemaphoreType.DMA((3,)),
        ),
        spaces="shhh",
    )(plane.reshape(1), connect.T, jnp.asarray(place, jnp.bfloat16), flat)
    for s in reversed(range(1, groups)):
        slots[s] = lax.ppermute(slots[s], "planes", [(p, p ^ s) for p in range(groups)])
    tables = call(
        functools.partial(setup_kernel, own_nodes),
        (
            jax.ShapeDtypeStruct(fourier.shape, jnp.bfloat16),
            jax.ShapeDtypeStruct((2, 2 * LANES, LANES), jnp.bfloat16),
            jax.ShapeDtypeStruct((8, LANES), f32),
        ),
        scratch=(
            pltpu.VMEM(connect.shape[::-1], jnp.int32),
            pltpu.VMEM(extents.shape, f32),
            pltpu.VMEM(matrices.shape, f32),
            pltpu.VMEM(masses.shape, f32),
            pltpu.SemaphoreType.DMA((5,)),
        ),
        spaces="shhhhh",
        cost=pl.CostEstimate(flops=10**6, bytes_accessed=3 * 10**6, transcendentals=0),
    )(
        plane.reshape(1), connect.T, extents,
        jnp.asarray(fourier), jnp.asarray(matrices), jnp.asarray(masses),
    )
    residual = call(
        functools.partial(residual_kernel, modes),
        jax.ShapeDtypeStruct((columns * CHUNK, LANES), f32),
        scratch=(pltpu.VMEM((PLANES, 2 * LANES), f32),),
        spaces="svvvvvvv",
    )(plane.reshape(1), *slots, *tables)
    residual = lax.all_to_all(
        residual.reshape(columns * CHUNK, 1, LANES),
        ("mesh", "planes"),
        split_axis=0,
        concat_axis=0,
        tiled=True,
    )
    chosen = call(
        choice_kernel,
        jax.ShapeDtypeStruct((COLS * LANES, own_nodes), jnp.bfloat16),
        spaces="v",
        cost=pl.CostEstimate(flops=10**6, bytes_accessed=10**6, transcendentals=0),
    )(ids)
    held = pltpu.VMEM((96 * 8, LANES), f32)
    change = call(
        functools.partial(cg_kernel, columns),
        jax.ShapeDtypeStruct((parts * 72, LANES), f32),
        scratch=(pltpu.VMEM((LANES * 8, LANES), f32), pltpu.VMEM((LANES, LANES), f32))
        + (held, held, pltpu.VMEM((ITERS, 6 * ROWS * 8, LANES), f32)),
        spaces="sv",
    )((plane * modes + part * 8).reshape(1), residual.reshape(columns * CHUNK, LANES))
    change = lax.all_to_all(
        change.reshape(parts, 72, LANES), "mesh", split_axis=0, concat_axis=0, tiled=True
    )
    result = call(scatter_kernel, jax.ShapeDtypeStruct((rows, own_nodes), f32), spaces="vvv")(
        flat, change, chosen
    )
    return result.reshape(velocity.shape)


def from_behind(value, axis, by):
    peers = lax.axis_size(axis)
    return lax.ppermute(value, axis, [(i, (i + by) % peers) for i in range(peers)])


def partitioned(velocity, connect, right_list, extents):
    components, modes, own_nodes = velocity.shape
    edge_count = right_list.shape[0]
    first_mode = lax.axis_index("planes") * modes
    tables = [jnp.asarray(table, jnp.float32) for table in element_tables()]
    stiff_along, stiff_across, slope_along, slope_across, mass_weights = tables
    synthesis, forward = (jnp.asarray(t, jnp.float32) for t in fourier_tables(PLANES))
    hx, hy = extents[0], extents[1]
    mass_full = mass_weights[:, None] * (hx * hy / 4.0)[None, :]
    index_list = first_mode + jnp.arange(modes, dtype=jnp.int32)
    wave = span_wave * jnp.where(index_list == 1, PLANES // 2, index_list // 2).astype(jnp.float32)
    wave = wave[None, :, None, None]
    helmholtz = inverse_step + wave * wave
    locals_ = jnp.arange(own_nodes + edge_count, dtype=jnp.int32)
    chosen = (locals_[:, None, None] == connect[None]).astype(jnp.float32)
    at_edge = (locals_[:own_nodes, None] == right_list[None]).astype(jnp.float32)

    def contract(spec, *operands):
        return jnp.einsum(spec, *operands, precision=highest)

    physical = contract(
        "jq,cqn->cjn",
        synthesis,
        lax.all_to_all(velocity, "planes", split_axis=2, concat_axis=1, tiled=True),
    )
    pairs = ((0, 0), (0, 1), (0, 2), (1, 1), (1, 2), (2, 2))
    products = jnp.stack([physical[a] * physical[b] for a, b in pairs])
    product_hat = lax.all_to_all(
        contract("qj,fjn->fqn", forward, products), "planes", split_axis=1, concat_axis=2, tiled=True
    )

    def spread(fields):
        ghosts = from_behind(contract("cqn,ny->cqy", fields, at_edge), "mesh", 1)
        return contract("cqn,nke->cqke", jnp.concatenate([fields, ghosts], axis=2), chosen)

    def assemble(terms):
        summed = contract("cqke,nke->cqn", terms, chosen)
        returned = from_behind(summed[:, :, own_nodes:], "mesh", -1)
        return summed[:, :, :own_nodes] + contract("cqy,ny->cqn", returned, at_edge)

    def stiffness(values):
        return (hy / hx) * contract("lk,cqke->cqle", stiff_along, values) + (hx / hy) * contract(
            "lk,cqke->cqle", stiff_across, values
        )

    def dots(left, right):
        return lax.psum(jnp.sum(left * right, axis=2), "mesh")

    values = spread(jnp.concatenate([velocity, product_hat], axis=0))
    speeds, along = values[0:3], values[3:6]
    across = jnp.stack([values[4], values[6], values[7]])
    span = jnp.stack([values[5], values[7], values[8]])
    shaped = span.reshape(span.shape[0], modes // 2, 2, *span.shape[2:])
    turned = jnp.stack([shaped[:, :, 1], -shaped[:, :, 0]], axis=2).reshape(span.shape)
    pair_wave = span_wave * (index_list // 2).astype(jnp.float32)[None, :, None, None]
    advection = (hy / 2.0) * contract("lk,cqke->cqle", slope_along, along)
    advection = advection + (hx / 2.0) * contract("lk,cqke->cqle", slope_across, across)
    advection = advection + mass_full * (pair_wave * turned)
    residual = assemble(
        -(wave * wave) * mass_full * speeds - stiffness(speeds) - advection / viscosity
    )
    solution = velocity
    direction = residual
    norm_now = dots(residual, residual)
    for _ in range(ITERS):
        values = spread(direction)
        operated = assemble(stiffness(values) + helmholtz * mass_full * values)
        step_size = (norm_now / dots(direction, operated))[:, :, None]
        solution = solution + step_size * direction
        residual = residual - step_size * operated
        norm_next = dots(residual, residual)
        direction = residual + (norm_next / norm_now)[:, :, None] * direction
        norm_now = norm_next
    return solution


def on_device(velocity, connect, right_list, extents):
    groups = lax.axis_size("planes")
    parts = lax.axis_size("mesh")
    modes = velocity.shape[1]
    fits = groups == COLS and modes == 8 * parts and 3 * parts * COLS <= LANES
    step = transposed if fits else partitioned
    return step(velocity, connect, right_list, extents)


def solution(mesh):
    placed = (P(None, "planes", "mesh"), P(None, "mesh"), P("mesh"), P(None, "mesh"))
    return jax.shard_map(
        on_device, mesh=mesh, in_specs=placed, out_specs=P(None, "planes", "mesh"), check_vma=False
    )
```

```python
import functools

import jax
import jax.numpy as jnp
import numpy as np
from jax import lax
from jax.experimental import pallas as pl
from jax.experimental.pallas import tpu as pltpu
from jax.sharding import PartitionSpec as P

PLANES = 256
ITERS = 4
SIDE = 7
ROWS = 13
COLS = 4
GRID = SIDE * ROWS
LANES = 128
SPEED = GRID
FIRST = GRID + ROWS
SECOND = GRID + 2 * ROWS
FITTING = LANES - SECOND
SPILL = 16
CHUNK = 25
OWNED = GRID - ROWS
HALF = OWNED // 2
SPARE = LANES - OWNED
REST = OWNED - SPARE

highest = lax.Precision.HIGHEST
viscosity = 0.002
time_step = 3e-05
span_wave = 4.0
inverse_step = 1.0 / (viscosity * time_step)


def legendre_six(points):
    previous = 0.0 * points + 1.0
    current = 1.0 * points
    for order in range(1, 6):
        following = ((2 * order + 1) * points * current - order * previous) / (order + 1)
        previous = current
        current = following
    return current


def gll_one_d():
    degree = 6
    points = np.array(
        [
            -1.0,
            -0.830223896278567,
            -0.4688487934707142,
            0.0,
            0.4688487934707142,
            0.830223896278567,
            1.0,
        ]
    )
    values = legendre_six(points)
    weights = 2.0 / (degree * (degree + 1) * values**2)
    derivative = np.zeros((degree + 1, degree + 1))
    for row_index in range(degree + 1):
        for col_index in range(degree + 1):
            if row_index != col_index:
                derivative[row_index, col_index] = values[row_index] / (
                    values[col_index] * (points[row_index] - points[col_index])
                )
    derivative[0, 0] = -degree * (degree + 1) / 4.0
    derivative[degree, degree] = degree * (degree + 1) / 4.0
    stiffness = derivative.T @ (weights[:, None] * derivative)
    return weights, derivative, stiffness


def element_tables():
    weights, derivative, stiffness = gll_one_d()
    identity = np.eye(SIDE)
    mass_weights = np.kron(weights, weights)
    return (
        np.kron(np.diag(weights), stiffness),
        np.kron(stiffness, np.diag(weights)),
        mass_weights[:, None] * np.kron(identity, derivative),
        mass_weights[:, None] * np.kron(derivative, identity),
        mass_weights,
    )


def fourier_tables(planes):
    plane_grid = np.arange(planes)
    synthesis = np.zeros((planes, planes))
    forward = np.zeros((planes, planes))
    synthesis[:, 0] = 1.0
    synthesis[:, 1] = np.cos(np.pi * plane_grid)
    forward[0] = 1.0 / planes
    forward[1] = np.cos(np.pi * plane_grid) / planes
    for wavenumber in range(1, planes // 2):
        phase_angle = 2.0 * np.pi * wavenumber * plane_grid / planes
        synthesis[:, 2 * wavenumber] = np.cos(phase_angle)
        synthesis[:, 2 * wavenumber + 1] = np.sin(phase_angle)
        forward[2 * wavenumber] = 2.0 * np.cos(phase_angle) / planes
        forward[2 * wavenumber + 1] = 2.0 * np.sin(phase_angle) / planes
    return synthesis, forward


def span_forward(forward):
    turned = np.zeros_like(forward)
    for wavenumber in range(1, forward.shape[0] // 2):
        turned[2 * wavenumber] = span_wave * wavenumber * forward[2 * wavenumber + 1]
        turned[2 * wavenumber + 1] = -span_wave * wavenumber * forward[2 * wavenumber]
    return turned


def two_parts(table):
    table = np.asarray(table, np.float32)
    high = table.astype(jnp.bfloat16)
    low = (table - high.astype(np.float32)).astype(jnp.bfloat16)
    return high, low


def placement(row, skip_shared):
    table = np.zeros((SIDE * SIDE, LANES))
    for j in range(SIDE):
        if skip_shared and row == 1 and j == 0:
            continue
        for i in range(SIDE):
            table[SIDE * j + i, ROWS * i + 6 * row + j] = 1.0
    return table


def column_tables():
    stiff_along, stiff_across, slope_along, slope_across, mass_weights = element_tables()
    owned = np.arange(LANES)
    owned = (owned >= ROWS) & (owned < GRID)
    matrices = []
    for table in (slope_along, slope_across, stiff_along, stiff_across):
        for row in range(2):
            place = placement(row, False)
            matrices.append((place.T @ table.T @ place) * owned[:, None])
    for start in (FIRST, SECOND):
        matrix = np.zeros((LANES, LANES))
        for y in range(ROWS):
            if start + y < LANES:
                matrix[6 * ROWS + y, start + y] = 1.0
        matrices.append(matrix)
    masses = [(mass_weights @ placement(row, False)) * owned for row in range(2)]
    return np.stack(matrices).astype(np.float32), np.stack(masses).astype(np.float32)


def split_two(value):
    high = value.astype(jnp.bfloat16)
    low = (value - high.astype(jnp.float32)).astype(jnp.bfloat16)
    return high, low


def split_three(value):
    high = value.astype(jnp.bfloat16)
    rest = value - high.astype(jnp.float32)
    middle = rest.astype(jnp.bfloat16)
    low = (rest - middle.astype(jnp.float32)).astype(jnp.bfloat16)
    return high, middle, low


def dot(left, right):
    return jnp.dot(left, right, preferred_element_type=jnp.float32)


def dot_split(left, right):
    return dot(left[0], right[0]) + (dot(left[0], right[1]) + dot(left[1], right[0]))


def one_hot(ids_row, count):
    rows = lax.broadcasted_iota(jnp.int32, (count, LANES), 0)
    return jnp.where(rows == ids_row, 1.0, 0.0).astype(jnp.bfloat16)


def element_order(element_ids, own_nodes):
    wide = (element_ids.shape[0], LANES)
    first_corner = jnp.broadcast_to(element_ids[:, 0:1], wide)
    last_corner = jnp.broadcast_to(element_ids[:, SIDE - 1 : SIDE], wide)
    picked = [
        jnp.where(first_corner == float(own_nodes + 6 * row), 1.0, 0.0) for row in range(2)
    ]
    order = [picked]
    for _ in range(COLS - 1):
        corners = [jnp.sum(last_corner * mask, axis=0, keepdims=True) for mask in picked]
        picked = [jnp.where(first_corner == corner, 1.0, 0.0) for corner in corners]
        order.append(picked)
    return order


def gather_kernel(
    plane_ref, connect_hbm, place_hbm, velocity_hbm,
    slot_a, slot_b, slot_c, slot_d, ids_ref,
    connect_ref, place_ref, velocity_ref, arrived,
):
    slots = (slot_a, slot_b, slot_c, slot_d)
    sources = (connect_hbm, place_hbm, velocity_hbm)
    targets = (connect_ref, place_ref, velocity_ref)
    copies = [
        pltpu.make_async_copy(source, target, arrived.at[at])
        for at, (source, target) in enumerate(zip(sources, targets))
    ]
    for copy in copies:
        copy.start()
    own_nodes = velocity_ref.shape[1]
    modes = velocity_ref.shape[0] // 3
    lane = lax.broadcasted_iota(jnp.int32, (1, LANES), 1)
    owned = (lane >= ROWS) & (lane < GRID)
    plane = plane_ref[0]
    copies[0].wait()
    element_ids = connect_ref[...].astype(jnp.float32)
    order = element_order(element_ids, own_nodes)
    ids_parts = split_two(element_ids)
    copies[1].wait()
    placed = [dot(ids_parts[0], place_ref[r]) + dot(ids_parts[1], place_ref[r]) for r in range(2)]
    rows = []
    for column in range(COLS):
        picked = order[column]
        ids = jnp.sum(placed[0] * picked[0] + placed[1] * picked[1], axis=0, keepdims=True)
        rows.append(jnp.where(owned, ids.astype(jnp.int32), -1))
    ids_ref[...] = jnp.concatenate(rows + [jnp.full((8 - COLS, LANES), -1, jnp.int32)], axis=0)
    chosen = []
    for slot in range(COLS):
        ids = rows[0]
        for column in range(1, COLS):
            ids = jnp.where((plane ^ slot) == column, rows[column], ids)
        chosen.append(one_hot(ids, own_nodes))
    copies[2].wait()
    both = dot(
        jnp.concatenate(split_two(velocity_ref[...]), axis=0), jnp.concatenate(chosen, axis=1)
    )
    both = both[: 3 * modes, :] + both[3 * modes :, :]
    for slot in range(COLS):
        values = both[:, slot * LANES : (slot + 1) * LANES]
        last = values[2 * modes :, :]
        for c in range(2):
            spread = pltpu.roll(last, OWNED - c * HALF, 1)
            slots[slot][:, c * LANES : (c + 1) * LANES] = jnp.where(
                owned, values[c * modes : (c + 1) * modes, :], spread
            )


def three_of(packed):
    lower = packed[:, :LANES]
    upper = packed[:, LANES:]
    lane = lax.broadcasted_iota(jnp.int32, lower.shape, 1)
    last = jnp.where(
        lane < ROWS + HALF,
        pltpu.roll(lower, LANES - OWNED, 1),
        pltpu.roll(upper, LANES - HALF, 1),
    )
    return lower, upper, last


def setup_kernel(
    own_nodes, plane_at, connect_hbm, extents_hbm, fourier_hbm, plane_hbm, mass_hbm,
    fourier_ref, in_plane_ref, row_ref,
    connect_ref, extents_ref, plane_ref, mass_ref, arrived,
):
    sources = (connect_hbm, extents_hbm, mass_hbm, plane_hbm, fourier_hbm)
    targets = (connect_ref, extents_ref, mass_ref, plane_ref, fourier_ref)
    copies = [
        pltpu.make_async_copy(source, target, arrived.at[at])
        for at, (source, target) in enumerate(zip(sources, targets))
    ]
    for copy in copies:
        copy.start()
    for copy in copies[:3]:
        copy.wait()
    element_ids = connect_ref[...].astype(jnp.float32)
    elements = element_ids.shape[0]
    order = element_order(element_ids, own_nodes)
    lane = lax.broadcasted_iota(jnp.int32, (1, LANES), 1)
    diagonal = lax.broadcasted_iota(jnp.int32, (elements, elements), 0) == lax.broadcasted_iota(
        jnp.int32, (elements, elements), 1
    )
    held = []
    for axis in range(2):
        lengths = jnp.sum(
            jnp.where(diagonal, extents_ref[axis : axis + 1, :], 0.0), axis=1, keepdims=True
        )
        for row in range(2):
            mask = order[0][row]
            for column in range(1, COLS):
                mask = jnp.where(plane_at[0] == column, order[column][row], mask)
            held.append(jnp.sum(lengths * mask, axis=0, keepdims=True))
    hx, hy = held[:2], held[2:]
    carried = jnp.zeros((1, LANES), jnp.float32)
    for at, value in enumerate(held):
        carried = carried + jnp.where(lane == at, value, 0.0)
    mass = sum((hx[r] * hy[r] / 4.0) * mass_ref[r : r + 1, :] for r in range(2))
    row_ref[...] = jnp.concatenate([mass, carried, jnp.zeros((6, LANES), jnp.float32)], axis=0)
    copies[3].wait()
    along = sum((hy[r] / 2.0) * plane_ref[r] for r in range(2)) + plane_ref[8]
    across = sum((hx[r] / 2.0) * plane_ref[2 + r] for r in range(2)) + plane_ref[9]
    stiff = viscosity * sum(
        (hy[r] / hx[r]) * plane_ref[4 + r] + (hx[r] / hy[r]) * plane_ref[6 + r] for r in range(2)
    )
    at_row = lax.broadcasted_iota(jnp.int32, (LANES, LANES), 0)
    middle = ROWS + HALF
    lower = jnp.where(at_row < middle, stiff, 0.0)
    upper = jnp.where(at_row >= middle, stiff, 0.0)
    high, low = split_two(
        jnp.concatenate(
            [along + pltpu.roll(lower, OWNED, 0), across + pltpu.roll(upper, OWNED - HALF, 0)],
            axis=0,
        )
    )
    in_plane_ref[0] = high
    in_plane_ref[1] = low
    copies[4].wait()


def residual_kernel(
    modes, plane_at, slot_a, slot_b, slot_c, slot_d, fourier_ref, in_plane_ref, row_ref,
    out_ref, packed_ref,
):
    planes = PLANES
    groups = planes // modes
    for slot, slot_ref in enumerate((slot_a, slot_b, slot_c, slot_d)):
        start = pl.multiple_of((plane_at[0] ^ slot) * modes, modes)
        packed_ref[pl.ds(start, modes), :] = slot_ref[...]
    packed = packed_ref[...]
    synthesis = (fourier_ref[0, :, :planes], fourier_ref[1, :, :planes])
    forward = (fourier_ref[0, :, planes:], fourier_ref[1, :, planes:])
    speeds = three_of(packed)
    physical = dot_split(synthesis, split_two(packed))
    fields = three_of(physical)
    mass = row_ref[0:1, :]
    carried = row_ref[1:2, :]
    products = [[fields[a] * fields[c] for a in range(3)] for c in range(3)]
    lane = lax.broadcasted_iota(jnp.int32, (planes, LANES), 1)
    owned = (lane >= ROWS) & (lane < GRID)
    flux = []
    for c in range(3):
        for half in range(2):
            if c == 2:
                spread = physical[:, half * LANES : (half + 1) * LANES]
            else:
                spread = pltpu.roll(fields[c], OWNED - half * HALF, 1)
            flux.append(jnp.where(owned, products[c][half], spread))
    flux = jnp.concatenate(
        [jnp.concatenate(flux[2 * c : 2 * c + 2], axis=1) for c in range(3)], axis=0
    )
    divergence = [
        dot_split(split_two(flux[c * planes : (c + 1) * planes, :]), (in_plane_ref[0], in_plane_ref[1]))
        for c in range(3)
    ]
    divergence[1] = jnp.where(
        (lane >= FIRST) & (lane < SECOND),
        pltpu.roll(products[2][2], FIRST - 6 * ROWS, 1),
        divergence[1],
    )
    spill = jnp.zeros((planes, LANES), jnp.float32)
    last = 6 * ROWS + FITTING
    for c in range(3):
        start = SPILL * (c + 1)
        spill = jnp.where(
            (lane >= start) & (lane < start + ROWS - FITTING),
            pltpu.roll(products[c][1], LANES + start - last, 1),
            spill,
        )
    upper = jnp.concatenate(divergence + [spill], axis=1)
    lower = jnp.concatenate([mass * products[c][2] for c in range(3)] + [spill * 0.0], axis=1)
    upper_parts, lower_parts = split_two(upper), split_two(lower[:, : 3 * LANES])
    from_upper = dot_split((forward[0][:, :planes], forward[1][:, :planes]), upper_parts)
    from_lower = dot_split((forward[0][:, planes:], forward[1][:, planes:]), lower_parts)
    result = jnp.concatenate([from_upper[:, : 3 * LANES] + from_lower, from_upper[:, 3 * LANES :]], axis=1)
    mode = lax.broadcasted_iota(jnp.int32, (planes, LANES), 0)
    wave = span_wave * jnp.where(mode == 1, planes // 2, mode // 2).astype(jnp.float32)
    square = wave * wave
    blocks = planes // 8
    per_group = modes // 8
    tiles = []
    for c in range(3):
        tile = result[:, c * LANES : (c + 1) * LANES] - square * (mass * speeds[c])
        handed = pltpu.roll(speeds[c], SPEED - 6 * ROWS, 1)
        tiles.append(jnp.where((lane >= SPEED) & (lane < FIRST), handed, tile))
    spilled = result[:, 3 * LANES :]
    for block in range(blocks):
        start = CHUNK * ((block % per_group) * groups + block // per_group)
        for c in range(3):
            out_ref[start + 8 * c : start + 8 * c + 8, :] = tiles[c][8 * block : 8 * block + 8, :]
        row = pltpu.roll(spilled[8 * block : 8 * block + 8, :], 0, 1, stride=2, stride_axis=0)
        out_ref[start + 24 : start + 25, :] = jnp.sum(row, axis=0, keepdims=True) + carried


def apply_line(stiffness, values):
    even = [values[k] + values[6 - k] for k in range(3)] + [values[3]]
    odd = [values[k] - values[6 - k] for k in range(3)]
    result = [None] * 7
    for i in range(4):
        total = float(stiffness[i, 3]) * even[3]
        for k in range(3):
            total = total + float((stiffness[i, k] + stiffness[i, 6 - k]) / 2) * even[k]
        if i == 3:
            result[3] = total
            continue
        other = float((stiffness[i, 0] - stiffness[i, 6]) / 2) * odd[0]
        for k in range(1, 3):
            other = other + float((stiffness[i, k] - stiffness[i, 6 - k]) / 2) * odd[k]
        result[i] = total + other
        result[6 - i] = total - other
    return result


def cg_kernel(
    columns, first_ref, in_ref,
    out_ref, grid_ref, turn_ref, rest_ref, image_ref, way_ref,
):
    weights, derivative, stiffness = gll_one_d()
    lane = lax.broadcasted_iota(jnp.int32, (8, LANES), 1)
    at = lane % columns

    def node(i, y):
        start = (ROWS * i + y) * 8
        return slice(start, start + 8)

    def from_next(value):
        return jnp.where(
            at == columns - 1,
            pltpu.roll(value, columns - 1, 1),
            pltpu.roll(value, LANES - 1, 1),
        )

    def from_previous(value):
        return jnp.where(
            at == 0,
            pltpu.roll(value, LANES - columns + 1, 1),
            pltpu.roll(value, 1, 1),
        )

    same = (
        lax.broadcasted_iota(jnp.int32, (LANES, LANES), 0) // columns
        == lax.broadcasted_iota(jnp.int32, (LANES, LANES), 1) // columns
    )
    ones = jnp.where(same, 1.0, 0.0).astype(jnp.bfloat16)
    ones = jnp.concatenate([ones, ones, ones], axis=0)

    def tree(values):
        return (values[0] + values[1]) + (values[2] + values[3]) + (values[4] + values[5])

    def over_columns(value):
        return dot(jnp.concatenate(split_three(value), axis=1), ones)

    blank = jnp.zeros((LANES - 3 * columns, LANES), jnp.float32)
    for mode in range(8):
        rows = [in_ref[pl.ds(8 * c + mode, columns, stride=CHUNK), :] for c in range(3)]
        turned = jnp.concatenate(rows + [blank], axis=0).T
        grid_ref[pl.ds(mode, LANES, stride=8), :] = turned

    extras = in_ref[pl.ds(CHUNK - 1, columns, stride=CHUNK), :]
    turn_ref[...] = jnp.concatenate([extras] * (LANES // columns), axis=0).T
    hx = [jnp.broadcast_to(turn_ref[at : at + 1, :], (8, LANES)) for at in range(2)]
    hy = [jnp.broadcast_to(turn_ref[2 + at : 3 + at, :], (8, LANES)) for at in range(2)]
    mode = first_ref[0] + lax.broadcasted_iota(jnp.int32, (8, LANES), 0)
    wave = span_wave * jnp.where(mode == 1, PLANES // 2, mode // 2).astype(jnp.float32)
    pair_wave = span_wave * (mode // 2).astype(jnp.float32)
    helmholtz = inverse_step + wave * wave
    ratio_along = [hy[r] / hx[r] for r in range(2)]
    ratio_across = [hx[r] / hy[r] for r in range(2)]
    mass = [helmholtz * (hx[r] * hy[r] / 4.0) for r in range(2)]

    def over_rows(pair, y):
        if y < 6:
            return float(weights[y]) * pair[0]
        if y > 6:
            return float(weights[y - 6]) * pair[1]
        return float(weights[6]) * pair[0] + float(weights[0]) * pair[1]

    def shared(pair):
        return [
            float(weights[0]) * value + float(weights[6]) * from_previous(value) for value in pair
        ]

    mass_shared = shared(mass)
    across_shared = shared(ratio_across)

    group = lane // columns

    def handed(start, y):
        return from_previous(grid_ref[(start + y) * 8 : (start + y) * 8 + 8, :])

    def spilled(y):
        rows = [
            turn_ref[pl.ds(SPILL * (c + 1) + y - FITTING, 8, stride=2), :] for c in range(3)
        ]
        return from_previous(
            jnp.where(group == 0, rows[0], jnp.where(group == 1, rows[1], rows[2]))
        )

    first_speed = [handed(SPEED, y) for y in range(ROWS)]
    first = [handed(FIRST, y) for y in range(ROWS)]
    second = [handed(SECOND, y) if y < FITTING else spilled(y) for y in range(ROWS)]
    sloped = weights[:, None] * derivative
    lines = [jnp.zeros((8, LANES), jnp.float32)] * ROWS
    for r in range(2):
        rows = range(6 * r, 6 * r + SIDE)
        curved = apply_line(stiffness, [first_speed[y] for y in rows])
        for j, y in enumerate(rows):
            slope = sum(float(sloped[j, k]) * second[6 * r + k] for k in range(SIDE))
            lines[y] = lines[y] + float(weights[0]) * (
                (0.5 * hx[r]) * slope - ratio_across[r] * curved[j]
            )
    area = [0.25 * hx[r] * hy[r] for r in range(2)]
    half = [0.5 * hy[r] for r in range(2)]
    even = mode % 2 == 0
    total = jnp.zeros((8, LANES), jnp.float32)
    for y in range(ROWS):
        along = jnp.where(group == 1, pltpu.roll(second[y], columns, 1), first[y])
        span = jnp.where(
            group == 0,
            pltpu.roll(first[y], 2 * columns, 1),
            jnp.where(
                group == 1,
                pltpu.roll(second[y], LANES - columns, 1),
                pltpu.roll(first[y], columns, 1),
            ),
        )
        span = jnp.where(even, pltpu.roll(span, 7, 0), -pltpu.roll(span, 1, 0))
        across = lines[y] + float(weights[0]) * over_rows(area, y) * (
            pair_wave * span - (wave * wave) * first_speed[y]
        )
        flux = over_rows(half, y) * along
        speed = over_rows(ratio_along, y) * first_speed[y]
        values = [
            grid_ref[node(i, y), :]
            + float(sloped[i, 0]) * flux
            - float(stiffness[i, 0]) * speed
            for i in range(SIDE)
        ]
        values[0] = values[0] + across + from_previous(values[6])
        for i in range(6):
            value = values[i]
            rest_ref[node(i, y), :] = value
            way_ref[0, node(i, y), :] = value
            total = total + value * value
    rest_norm = over_columns(total)

    def apply(iteration, turn):
        for y in range(ROWS):
            values = []
            for i in range(6):
                value = rest_ref[node(i, y), :]
                if iteration:
                    value = value + turn * way_ref[iteration - 1, node(i, y), :]
                    way_ref[iteration, node(i, y), :] = value
                values.append(value)
            values.append(from_next(values[0]))
            lines = apply_line(stiffness, values)
            along = over_rows(ratio_along, y)
            lines = [along * line for line in lines]
            lines[0] = lines[0] + from_previous(lines[6])
            inner = over_rows(mass, y)
            inner = [None] + [float(weights[i]) * inner for i in range(1, 4)]
            inner = [over_rows(mass_shared, y)] + inner[1:] + [inner[2], inner[1]]
            for i in range(6):
                image_ref[node(i, y), :] = lines[i] + inner[i] * values[i]
        totals = [jnp.zeros((8, LANES), jnp.float32)] * 6
        for i in range(6):
            values = [way_ref[iteration, node(i, y), :] for y in range(ROWS)]
            lower = apply_line(stiffness, values[:7])
            upper = apply_line(stiffness, values[6:])
            if i == 0:
                scale = across_shared
            else:
                scale = [float(weights[i]) * value for value in ratio_across]
            lower = [scale[0] * value for value in lower]
            upper = [scale[1] * value for value in upper]
            lines = lower[:6] + [lower[6] + upper[0]] + upper[1:]
            for y in range(ROWS):
                image = image_ref[node(i, y), :] + lines[y]
                image_ref[node(i, y), :] = image
                totals[y % 6] = totals[y % 6] + values[y] * image
        return over_columns(tree(totals))

    turn = None
    sizes = []
    for iteration in range(ITERS):
        size = rest_norm / apply(iteration, turn)
        sizes.append(size)
        if iteration == ITERS - 1:
            break
        totals = [jnp.zeros((8, LANES), jnp.float32)] * 6
        for y in range(ROWS):
            for i in range(6):
                rest = rest_ref[node(i, y), :] - size * image_ref[node(i, y), :]
                rest_ref[node(i, y), :] = rest
                totals[i] = totals[i] + rest * rest
        following = over_columns(tree(totals))
        turn = following / rest_norm
        rest_norm = following
    zero = jnp.zeros((8, LANES), jnp.float32)
    for y in range(ROWS):
        grid_ref[node(0, y), :] = zero
        for i in range(6):
            value = sizes[0] * way_ref[0, node(i, y), :]
            for step in range(1, ITERS):
                value = value + sizes[step] * way_ref[step, node(i, y), :]
            if i == 0:
                grid_ref[node(6, y), :] = from_next(value)
            else:
                grid_ref[node(i, y), :] = value
    for left in range(GRID, LANES):
        grid_ref[left * 8 : left * 8 + 8, :] = zero
    parts = columns // COLS
    node_lane = lax.broadcasted_iota(jnp.int32, (3 * parts, LANES), 1)
    owned = (node_lane >= ROWS) & (node_lane < GRID)
    rest_from = LANES - ROWS - SPARE
    for mode in range(8):
        turn_ref[...] = grid_ref[pl.ds(mode, LANES, stride=8), :].T
        pieces = [turn_ref[pl.ds(k, 3 * parts, stride=COLS), :] for k in range(COLS)]
        for k in range(2):
            tile = jnp.where(owned, pieces[k], pltpu.roll(pieces[k + 2], OWNED, 1))
            for c in range(3):
                out_ref[pl.ds(24 * k + 8 * c + mode, parts, stride=64), :] = tile[
                    c * parts : (c + 1) * parts, :
                ]
        rest = jnp.where(
            node_lane < REST,
            pltpu.roll(pieces[2], rest_from, 1),
            pltpu.roll(pieces[3], rest_from + REST, 1),
        )
        rest = [rest[c * parts : (c + 1) * parts, :] for c in range(3)]
        both = jnp.where(
            node_lane[:parts, :] < LANES // 2, rest[0], pltpu.roll(rest[1], LANES // 2, 1)
        )
        out_ref[pl.ds(48 + mode, parts, stride=64), :] = both
        out_ref[pl.ds(56 + mode, parts, stride=64), :] = rest[2]


def choice_kernel(ids_ref, out_ref):
    nodes = lax.broadcasted_iota(jnp.int32, (LANES, out_ref.shape[1]), 1)
    for column in range(COLS):
        ids = jnp.broadcast_to(ids_ref[column : column + 1, :].astype(jnp.float32), (LANES, LANES))
        ids = ids.T[:, 0:1].astype(jnp.int32)
        out_ref[column * LANES : (column + 1) * LANES, :] = jnp.where(
            nodes == ids, 1.0, 0.0
        ).astype(jnp.bfloat16)


def scatter_kernel(velocity_ref, change_ref, chosen_ref, out_ref):
    rows = velocity_ref.shape[0]
    sources = change_ref.shape[0]
    def tiles(start):
        return jnp.concatenate(
            [change_ref[m, start : start + 8, :] for m in range(sources)], axis=0
        )

    lane = lax.broadcasted_iota(jnp.int32, (8 * sources, LANES), 1)
    pieces = []
    shared, single = tiles(48), tiles(56)
    for c in range(3):
        held = [tiles(24 * k + 8 * c) for k in range(2)]
        rest, skip = (single, 0) if c == 2 else (shared, c * (LANES // 2))
        for k in range(2):
            moved = pltpu.roll(rest, (ROWS + SPARE - k * REST - skip) % LANES, 1)
            held.append(jnp.where(lane < ROWS + SPARE, pltpu.roll(held[k], SPARE, 1), moved))
        pieces.append(jnp.concatenate(held, axis=1))
    parts = jnp.concatenate(split_two(jnp.concatenate(pieces, axis=0)), axis=0)
    change = dot(parts, chosen_ref[...])
    out_ref[...] = velocity_ref[...] + (change[:rows, :] + change[rows:, :])


def call(kernel, out_shape, scratch=(), spaces="", cost=None):
    place = {
        "s": pl.BlockSpec(memory_space=pltpu.SMEM),
        "v": pl.BlockSpec(memory_space=pltpu.VMEM),
        "h": pl.BlockSpec(memory_space=pltpu.HBM),
    }
    many = isinstance(out_shape, tuple)
    run = pl.pallas_call(
        kernel,
        out_shape=out_shape,
        in_specs=[place[space] for space in spaces],
        out_specs=(place["v"],) * len(out_shape) if many else place["v"],
        scratch_shapes=list(scratch),
        cost_estimate=cost,
        compiler_params=pltpu.CompilerParams(vmem_limit_bytes=16 * 2**20),
    )

    def with_spaces(*operands):
        return run(
            *(
                pltpu.with_memory_space_constraint(operand, pltpu.HBM) if space == "h" else operand
                for space, operand in zip(spaces, operands)
            )
        )

    return with_spaces


def transposed(velocity, connect, right_list, extents):
    components, modes, own_nodes = velocity.shape
    groups = lax.axis_size("planes")
    parts = lax.axis_size("mesh")
    plane = lax.axis_index("planes")
    part = lax.axis_index("mesh")
    rows = components * modes
    columns = parts * COLS
    synthesis, forward = fourier_tables(PLANES)
    forward = np.concatenate([forward, span_forward(forward)], axis=1) * (-1.0 / viscosity)
    fourier = np.stack(two_parts(np.concatenate([synthesis, forward], axis=1)))
    matrices, masses = column_tables()
    place = np.stack([placement(row, True) for row in range(2)])
    flat = velocity.reshape(rows, own_nodes)
    f32 = jnp.float32
    slot_shape = jax.ShapeDtypeStruct((modes, 2 * LANES), f32)
    *slots, ids = call(
        gather_kernel,
        (slot_shape,) * COLS + (jax.ShapeDtypeStruct((8, LANES), jnp.int32),),
        scratch=(
            pltpu.VMEM(connect.shape[::-1], jnp.int32),
            pltpu.VMEM(place.shape, jnp.bfloat16),
            pltpu.VMEM((rows, own_nodes), f32),
            pltpu.SemaphoreType.DMA((3,)),
        ),
        spaces="shhh",
    )(plane.reshape(1), connect.T, jnp.asarray(place, jnp.bfloat16), flat)
    for s in reversed(range(1, groups)):
        slots[s] = lax.ppermute(slots[s], "planes", [(p, p ^ s) for p in range(groups)])
    tables = call(
        functools.partial(setup_kernel, own_nodes),
        (
            jax.ShapeDtypeStruct(fourier.shape, jnp.bfloat16),
            jax.ShapeDtypeStruct((2, 2 * LANES, LANES), jnp.bfloat16),
            jax.ShapeDtypeStruct((8, LANES), f32),
        ),
        scratch=(
            pltpu.VMEM(connect.shape[::-1], jnp.int32),
            pltpu.VMEM(extents.shape, f32),
            pltpu.VMEM(matrices.shape, f32),
            pltpu.VMEM(masses.shape, f32),
            pltpu.SemaphoreType.DMA((5,)),
        ),
        spaces="shhhhh",
        cost=pl.CostEstimate(flops=10**6, bytes_accessed=3 * 10**6, transcendentals=0),
    )(
        plane.reshape(1), connect.T, extents,
        jnp.asarray(fourier), jnp.asarray(matrices), jnp.asarray(masses),
    )
    residual = call(
        functools.partial(residual_kernel, modes),
        jax.ShapeDtypeStruct((columns * CHUNK, LANES), f32),
        scratch=(pltpu.VMEM((PLANES, 2 * LANES), f32),),
        spaces="svvvvvvv",
    )(plane.reshape(1), *slots, *tables)
    residual = lax.all_to_all(
        residual.reshape(columns * CHUNK, 1, LANES),
        ("mesh", "planes"),
        split_axis=0,
        concat_axis=0,
        tiled=True,
    )
    chosen = call(
        choice_kernel,
        jax.ShapeDtypeStruct((COLS * LANES, own_nodes), jnp.bfloat16),
        spaces="v",
        cost=pl.CostEstimate(flops=10**6, bytes_accessed=10**6, transcendentals=0),
    )(ids)
    held = pltpu.VMEM((96 * 8, LANES), f32)
    change = call(
        functools.partial(cg_kernel, columns),
        jax.ShapeDtypeStruct((parts * 64, LANES), f32),
        scratch=(pltpu.VMEM((LANES * 8, LANES), f32), pltpu.VMEM((LANES, LANES), f32))
        + (held, held, pltpu.VMEM((ITERS, 6 * ROWS * 8, LANES), f32)),
        spaces="sv",
    )((plane * modes + part * 8).reshape(1), residual.reshape(columns * CHUNK, LANES))
    change = lax.all_to_all(
        change.reshape(parts, 64, LANES), "mesh", split_axis=0, concat_axis=0, tiled=True
    )
    result = call(scatter_kernel, jax.ShapeDtypeStruct((rows, own_nodes), f32), spaces="vvv")(
        flat, change, chosen
    )
    return result.reshape(velocity.shape)


def from_behind(value, axis, by):
    peers = lax.axis_size(axis)
    return lax.ppermute(value, axis, [(i, (i + by) % peers) for i in range(peers)])


def partitioned(velocity, connect, right_list, extents):
    components, modes, own_nodes = velocity.shape
    edge_count = right_list.shape[0]
    first_mode = lax.axis_index("planes") * modes
    tables = [jnp.asarray(table, jnp.float32) for table in element_tables()]
    stiff_along, stiff_across, slope_along, slope_across, mass_weights = tables
    synthesis, forward = (jnp.asarray(t, jnp.float32) for t in fourier_tables(PLANES))
    hx, hy = extents[0], extents[1]
    mass_full = mass_weights[:, None] * (hx * hy / 4.0)[None, :]
    index_list = first_mode + jnp.arange(modes, dtype=jnp.int32)
    wave = span_wave * jnp.where(index_list == 1, PLANES // 2, index_list // 2).astype(jnp.float32)
    wave = wave[None, :, None, None]
    helmholtz = inverse_step + wave * wave
    locals_ = jnp.arange(own_nodes + edge_count, dtype=jnp.int32)
    chosen = (locals_[:, None, None] == connect[None]).astype(jnp.float32)
    at_edge = (locals_[:own_nodes, None] == right_list[None]).astype(jnp.float32)

    def contract(spec, *operands):
        return jnp.einsum(spec, *operands, precision=highest)

    physical = contract(
        "jq,cqn->cjn",
        synthesis,
        lax.all_to_all(velocity, "planes", split_axis=2, concat_axis=1, tiled=True),
    )
    pairs = ((0, 0), (0, 1), (0, 2), (1, 1), (1, 2), (2, 2))
    products = jnp.stack([physical[a] * physical[b] for a, b in pairs])
    product_hat = lax.all_to_all(
        contract("qj,fjn->fqn", forward, products), "planes", split_axis=1, concat_axis=2, tiled=True
    )

    def spread(fields):
        ghosts = from_behind(contract("cqn,ny->cqy", fields, at_edge), "mesh", 1)
        return contract("cqn,nke->cqke", jnp.concatenate([fields, ghosts], axis=2), chosen)

    def assemble(terms):
        summed = contract("cqke,nke->cqn", terms, chosen)
        returned = from_behind(summed[:, :, own_nodes:], "mesh", -1)
        return summed[:, :, :own_nodes] + contract("cqy,ny->cqn", returned, at_edge)

    def stiffness(values):
        return (hy / hx) * contract("lk,cqke->cqle", stiff_along, values) + (hx / hy) * contract(
            "lk,cqke->cqle", stiff_across, values
        )

    def dots(left, right):
        return lax.psum(jnp.sum(left * right, axis=2), "mesh")

    values = spread(jnp.concatenate([velocity, product_hat], axis=0))
    speeds, along = values[0:3], values[3:6]
    across = jnp.stack([values[4], values[6], values[7]])
    span = jnp.stack([values[5], values[7], values[8]])
    shaped = span.reshape(span.shape[0], modes // 2, 2, *span.shape[2:])
    turned = jnp.stack([shaped[:, :, 1], -shaped[:, :, 0]], axis=2).reshape(span.shape)
    pair_wave = span_wave * (index_list // 2).astype(jnp.float32)[None, :, None, None]
    advection = (hy / 2.0) * contract("lk,cqke->cqle", slope_along, along)
    advection = advection + (hx / 2.0) * contract("lk,cqke->cqle", slope_across, across)
    advection = advection + mass_full * (pair_wave * turned)
    residual = assemble(
        -(wave * wave) * mass_full * speeds - stiffness(speeds) - advection / viscosity
    )
    solution = velocity
    direction = residual
    norm_now = dots(residual, residual)
    for _ in range(ITERS):
        values = spread(direction)
        operated = assemble(stiffness(values) + helmholtz * mass_full * values)
        step_size = (norm_now / dots(direction, operated))[:, :, None]
        solution = solution + step_size * direction
        residual = residual - step_size * operated
        norm_next = dots(residual, residual)
        direction = residual + (norm_next / norm_now)[:, :, None] * direction
        norm_now = norm_next
    return solution


def on_device(velocity, connect, right_list, extents):
    groups = lax.axis_size("planes")
    parts = lax.axis_size("mesh")
    modes = velocity.shape[1]
    fits = groups == COLS and modes == 8 * parts and 3 * parts * COLS <= LANES
    step = transposed if fits else partitioned
    return step(velocity, connect, right_list, extents)


def solution(mesh):
    placed = (P(None, "planes", "mesh"), P(None, "mesh"), P("mesh"), P(None, "mesh"))
    return jax.shard_map(
        on_device, mesh=mesh, in_specs=placed, out_specs=P(None, "planes", "mesh"), check_vma=False
    )
```

```python
import functools

import jax
import jax.numpy as jnp
import numpy as np
from jax import lax
from jax.experimental import pallas as pl
from jax.experimental.pallas import tpu as pltpu
from jax.sharding import PartitionSpec as P

PLANES = 256
ITERS = 4
SIDE = 7
ROWS = 13
COLS = 4
GRID = SIDE * ROWS
LANES = 128
SHARE = 4
SPEED = GRID
FIRST = GRID + SHARE
SECOND = GRID + 2 * SHARE
KEPT = GRID + 3 * SHARE
SPLIT = LANES - KEPT
WHOLE = KEPT - 2 * SPLIT
TAKEN = GRID + SHARE
ROOM = LANES - TAKEN
QUARTER = LANES // 4
CHUNK = 20
OWNED = GRID - ROWS
SPARE = LANES - OWNED
REST = OWNED - SPARE

highest = lax.Precision.HIGHEST
viscosity = 0.002
time_step = 3e-05
span_wave = 4.0
inverse_step = 1.0 / (viscosity * time_step)


def legendre_six(points):
    previous = 0.0 * points + 1.0
    current = 1.0 * points
    for order in range(1, 6):
        following = ((2 * order + 1) * points * current - order * previous) / (order + 1)
        previous = current
        current = following
    return current


def gll_one_d():
    degree = 6
    points = np.array(
        [
            -1.0,
            -0.830223896278567,
            -0.4688487934707142,
            0.0,
            0.4688487934707142,
            0.830223896278567,
            1.0,
        ]
    )
    values = legendre_six(points)
    weights = 2.0 / (degree * (degree + 1) * values**2)
    derivative = np.zeros((degree + 1, degree + 1))
    for row_index in range(degree + 1):
        for col_index in range(degree + 1):
            if row_index != col_index:
                derivative[row_index, col_index] = values[row_index] / (
                    values[col_index] * (points[row_index] - points[col_index])
                )
    derivative[0, 0] = -degree * (degree + 1) / 4.0
    derivative[degree, degree] = degree * (degree + 1) / 4.0
    stiffness = derivative.T @ (weights[:, None] * derivative)
    return weights, derivative, stiffness


def element_tables():
    weights, derivative, stiffness = gll_one_d()
    identity = np.eye(SIDE)
    mass_weights = np.kron(weights, weights)
    return (
        np.kron(np.diag(weights), stiffness),
        np.kron(stiffness, np.diag(weights)),
        mass_weights[:, None] * np.kron(identity, derivative),
        mass_weights[:, None] * np.kron(derivative, identity),
        mass_weights,
    )


def fourier_tables(planes):
    plane_grid = np.arange(planes)
    synthesis = np.zeros((planes, planes))
    forward = np.zeros((planes, planes))
    synthesis[:, 0] = 1.0
    synthesis[:, 1] = np.cos(np.pi * plane_grid)
    forward[0] = 1.0 / planes
    forward[1] = np.cos(np.pi * plane_grid) / planes
    for wavenumber in range(1, planes // 2):
        phase_angle = 2.0 * np.pi * wavenumber * plane_grid / planes
        synthesis[:, 2 * wavenumber] = np.cos(phase_angle)
        synthesis[:, 2 * wavenumber + 1] = np.sin(phase_angle)
        forward[2 * wavenumber] = 2.0 * np.cos(phase_angle) / planes
        forward[2 * wavenumber + 1] = 2.0 * np.sin(phase_angle) / planes
    return synthesis, forward


def span_forward(forward):
    turned = np.zeros_like(forward)
    for wavenumber in range(1, forward.shape[0] // 2):
        turned[2 * wavenumber] = span_wave * wavenumber * forward[2 * wavenumber + 1]
        turned[2 * wavenumber + 1] = -span_wave * wavenumber * forward[2 * wavenumber]
    return turned


def two_parts(table):
    table = np.asarray(table, np.float32)
    high = table.astype(jnp.bfloat16)
    low = (table - high.astype(np.float32)).astype(jnp.bfloat16)
    return high, low


def placement(row, skip_shared):
    table = np.zeros((SIDE * SIDE, LANES))
    for j in range(SIDE):
        if skip_shared and row == 1 and j == 0:
            continue
        for i in range(SIDE):
            table[SIDE * j + i, ROWS * i + 6 * row + j] = 1.0
    return table


def column_tables():
    stiff_along, stiff_across, slope_along, slope_across, mass_weights = element_tables()
    matrices = []
    for table in (slope_along, slope_across, stiff_along, stiff_across):
        for row in range(2):
            place = placement(row, False)
            matrices.append(place.T @ table.T @ place)
    for start in (FIRST, SECOND):
        matrix = np.zeros((LANES, LANES))
        for at in range(SHARE):
            matrix[SPEED + at, start + at] = 1.0
        matrices.append(matrix)
    masses = [mass_weights @ placement(row, False) for row in range(2)]
    return np.stack(matrices).astype(np.float32), np.stack(masses).astype(np.float32)


def split_two(value):
    high = value.astype(jnp.bfloat16)
    low = (value - high.astype(jnp.float32)).astype(jnp.bfloat16)
    return high, low


def split_three(value):
    high = value.astype(jnp.bfloat16)
    rest = value - high.astype(jnp.float32)
    middle = rest.astype(jnp.bfloat16)
    low = (rest - middle.astype(jnp.float32)).astype(jnp.bfloat16)
    return high, middle, low


def dot(left, right):
    return jnp.dot(left, right, preferred_element_type=jnp.float32)


def dot_split(left, right):
    return dot(left[0], right[0]) + (dot(left[0], right[1]) + dot(left[1], right[0]))


def one_hot(ids_row, count):
    rows = lax.broadcasted_iota(jnp.int32, (count, LANES), 0)
    return jnp.where(rows == ids_row, 1.0, 0.0).astype(jnp.bfloat16)


def element_order(element_ids, own_nodes):
    wide = (element_ids.shape[0], LANES)
    first_corner = jnp.broadcast_to(element_ids[:, 0:1], wide)
    last_corner = jnp.broadcast_to(element_ids[:, SIDE - 1 : SIDE], wide)
    picked = [
        jnp.where(first_corner == float(own_nodes + 6 * row), 1.0, 0.0) for row in range(2)
    ]
    order = [picked]
    for _ in range(COLS - 1):
        corners = [jnp.sum(last_corner * mask, axis=0, keepdims=True) for mask in picked]
        picked = [jnp.where(first_corner == corner, 1.0, 0.0) for corner in corners]
        order.append(picked)
    return order


def gather_kernel(
    plane_ref, connect_hbm, place_hbm, velocity_hbm,
    slot_a, slot_b, slot_c, slot_d, ids_ref,
    connect_ref, place_ref, velocity_ref, arrived,
):
    slots = (slot_a, slot_b, slot_c, slot_d)
    sources = (connect_hbm, place_hbm, velocity_hbm)
    targets = (connect_ref, place_ref, velocity_ref)
    copies = [
        pltpu.make_async_copy(source, target, arrived.at[at])
        for at, (source, target) in enumerate(zip(sources, targets))
    ]
    for copy in copies:
        copy.start()
    own_nodes = velocity_ref.shape[1]
    modes = velocity_ref.shape[0] // 3
    lane = lax.broadcasted_iota(jnp.int32, (1, LANES), 1)
    plane = plane_ref[0]
    copies[0].wait()
    element_ids = connect_ref[...].astype(jnp.float32)
    order = element_order(element_ids, own_nodes)
    ids_parts = split_two(element_ids)
    copies[1].wait()
    placed = [dot(ids_parts[0], place_ref[r]) + dot(ids_parts[1], place_ref[r]) for r in range(2)]
    rows = []
    for column in range(COLS):
        picked = order[column]
        ids = jnp.sum(placed[0] * picked[0] + placed[1] * picked[1], axis=0, keepdims=True)
        rows.append(jnp.where(lane < GRID, ids.astype(jnp.int32), -1))
    kept = [jnp.where(lane >= ROWS, ids, -1) for ids in rows]
    ids_ref[...] = jnp.concatenate(kept + [jnp.full((8 - COLS, LANES), -1, jnp.int32)], axis=0)
    last = jnp.broadcast_to(rows[COLS - 1].astype(jnp.float32), (8, LANES))
    for column in range(COLS):
        count = min(SHARE, ROWS - SHARE * column)
        taken = pltpu.roll(last, SPEED - 6 * ROWS - SHARE * column, 1)[0:1, :].astype(jnp.int32)
        rows[column] = jnp.where((lane >= SPEED) & (lane < SPEED + count), taken, rows[column])
    chosen = []
    for slot in range(COLS):
        ids = rows[0]
        for column in range(1, COLS):
            ids = jnp.where((plane ^ slot) == column, rows[column], ids)
        chosen.append(one_hot(ids, own_nodes))
    copies[2].wait()
    both = dot(
        jnp.concatenate(split_two(velocity_ref[...]), axis=0), jnp.concatenate(chosen, axis=1)
    )
    both = both[: 3 * modes, :] + both[3 * modes :, :]
    tile_lane = lax.broadcasted_iota(jnp.int32, (modes, LANES), 1)
    quarter = modes // 4
    for slot in range(COLS):
        values = both[:, slot * LANES : (slot + 1) * LANES]
        last = values[2 * modes :, :]
        for c in range(2):
            slots[slot][c * modes : (c + 1) * modes, :] = jnp.where(
                tile_lane < TAKEN,
                values[c * modes : (c + 1) * modes, :],
                pltpu.roll(last, TAKEN - c * ROOM, 1),
            )
        rest = pltpu.roll(last[:quarter, :], LANES - 2 * ROOM, 1)
        for part in range(1, 4):
            rest = jnp.where(
                tile_lane[:quarter, :] < part * QUARTER,
                rest,
                pltpu.roll(
                    last[part * quarter : (part + 1) * quarter, :],
                    (part * QUARTER - 2 * ROOM) % LANES,
                    1,
                ),
            )
        slots[slot][2 * modes :, :] = rest


def three_of(slot, modes):
    lower, upper, rest = slot[:modes, :], slot[modes : 2 * modes, :], slot[2 * modes :, :]
    lane = lax.broadcasted_iota(jnp.int32, (modes, LANES), 1)
    spread = [pltpu.roll(rest, (2 * ROOM - part * QUARTER) % LANES, 1) for part in range(4)]
    last = jnp.where(
        lane < ROOM,
        pltpu.roll(lower, ROOM, 1),
        jnp.where(
            lane < 2 * ROOM, pltpu.roll(upper, 2 * ROOM, 1), jnp.concatenate(spread, axis=0)
        ),
    )
    return jnp.concatenate([lower, upper, last], axis=1)


def setup_kernel(
    own_nodes, plane_at, connect_hbm, extents_hbm, fourier_hbm, plane_hbm, mass_hbm,
    fourier_ref, in_plane_ref, row_ref,
    connect_ref, extents_ref, plane_ref, mass_ref, arrived,
):
    sources = (connect_hbm, extents_hbm, mass_hbm, plane_hbm, fourier_hbm)
    targets = (connect_ref, extents_ref, mass_ref, plane_ref, fourier_ref)
    copies = [
        pltpu.make_async_copy(source, target, arrived.at[at])
        for at, (source, target) in enumerate(zip(sources, targets))
    ]
    for copy in copies:
        copy.start()
    for copy in copies[:3]:
        copy.wait()
    element_ids = connect_ref[...].astype(jnp.float32)
    elements = element_ids.shape[0]
    order = element_order(element_ids, own_nodes)
    lane = lax.broadcasted_iota(jnp.int32, (1, LANES), 1)
    diagonal = lax.broadcasted_iota(jnp.int32, (elements, elements), 0) == lax.broadcasted_iota(
        jnp.int32, (elements, elements), 1
    )
    held = []
    for axis in range(2):
        lengths = jnp.sum(
            jnp.where(diagonal, extents_ref[axis : axis + 1, :], 0.0), axis=1, keepdims=True
        )
        for row in range(2):
            mask = order[0][row]
            for column in range(1, COLS):
                mask = jnp.where(plane_at[0] == column, order[column][row], mask)
            held.append(jnp.sum(lengths * mask, axis=0, keepdims=True))
    hx, hy = held[:2], held[2:]
    carried = jnp.zeros((1, LANES), jnp.float32)
    for at, value in enumerate(held):
        carried = carried + jnp.where(lane == WHOLE + at, value, 0.0)
    mass = sum((hx[r] * hy[r] / 4.0) * mass_ref[r : r + 1, :] for r in range(2))
    row_ref[...] = jnp.concatenate([mass, carried, jnp.zeros((6, LANES), jnp.float32)], axis=0)
    copies[3].wait()
    along = sum((hy[r] / 2.0) * plane_ref[r] for r in range(2)) + plane_ref[8]
    across = sum((hx[r] / 2.0) * plane_ref[2 + r] for r in range(2)) + plane_ref[9]
    stiff = viscosity * sum(
        (hy[r] / hx[r]) * plane_ref[4 + r] + (hx[r] / hy[r]) * plane_ref[6 + r] for r in range(2)
    )
    high, low = split_two(jnp.concatenate([along, across, stiff], axis=0))
    in_plane_ref[0] = high
    in_plane_ref[1] = low
    copies[4].wait()


def residual_kernel(
    modes, plane_at, slot_a, slot_b, slot_c, slot_d, fourier_ref, in_plane_ref, row_ref,
    out_ref, packed_ref,
):
    planes = PLANES
    groups = planes // modes
    for slot, slot_ref in enumerate((slot_a, slot_b, slot_c, slot_d)):
        start = pl.multiple_of((plane_at[0] ^ slot) * modes, modes)
        packed_ref[pl.ds(start, modes), :] = three_of(slot_ref[...], modes)
    packed = packed_ref[...]
    synthesis = (fourier_ref[0, :, :planes], fourier_ref[1, :, :planes])
    forward = (fourier_ref[0, :, planes:], fourier_ref[1, :, planes:])
    physical = dot_split(synthesis, split_two(packed))
    speeds = [packed[:, c * LANES : (c + 1) * LANES] for c in range(3)]
    fields = [physical[:, c * LANES : (c + 1) * LANES] for c in range(3)]
    mass = row_ref[0:1, :]
    carried = row_ref[1:2, :]
    products = [[fields[a] * fields[c] for a in range(3)] for c in range(3)]
    lane = lax.broadcasted_iota(jnp.int32, (planes, LANES), 1)
    in_plane = (in_plane_ref[0], in_plane_ref[1])
    divergence = [
        dot_split(
            split_two(jnp.concatenate([products[c][0], products[c][1], fields[c]], axis=1)),
            in_plane,
        )
        for c in range(3)
    ]
    divergence[1] = jnp.where(
        (lane >= FIRST) & (lane < SECOND),
        pltpu.roll(products[2][2], FIRST - SPEED, 1),
        divergence[1],
    )
    upper = split_two(jnp.concatenate(divergence, axis=1))
    lower = split_two(jnp.concatenate([mass * products[c][2] for c in range(3)], axis=1))
    result = dot_split((forward[0][:, :planes], forward[1][:, :planes]), upper) + dot_split(
        (forward[0][:, planes:], forward[1][:, planes:]), lower
    )
    mode = lax.broadcasted_iota(jnp.int32, (planes, LANES), 0)
    wave = span_wave * jnp.where(mode == 1, planes // 2, mode // 2).astype(jnp.float32)
    square = wave * wave
    tiles = []
    for c in range(3):
        tile = result[:, c * LANES : (c + 1) * LANES] - square * (mass * speeds[c])
        tiles.append(jnp.where((lane >= SPEED) & (lane < FIRST), speeds[c], tile))
    beside = lane >= KEPT
    tiles[0] = jnp.where(beside, pltpu.roll(tiles[2], KEPT - WHOLE, 1), tiles[0])
    tiles[1] = jnp.where(beside, pltpu.roll(tiles[2], KEPT - WHOLE - SPLIT, 1), tiles[1])
    tiles[2] = jnp.where(lane < WHOLE, tiles[2], carried)
    blocks = planes // 8
    per_group = modes // 8
    left = lax.broadcasted_iota(jnp.int32, (8, LANES), 1) < LANES // 2
    for block in range(blocks):
        start = CHUNK * ((block % per_group) * groups + block // per_group)
        rows = slice(8 * block, 8 * block + 8)
        out_ref[start : start + 8, :] = tiles[0][rows, :]
        out_ref[start + 8 : start + 16, :] = tiles[1][rows, :]
        last = tiles[2][rows, :]
        last = jnp.where(left, last, pltpu.roll(pltpu.roll(last, LANES // 2, 1), 4, 0))
        out_ref[start + 16 : start + 20, :] = last[0:4, :]


def apply_line(stiffness, values):
    even = [values[k] + values[6 - k] for k in range(3)] + [values[3]]
    odd = [values[k] - values[6 - k] for k in range(3)]
    result = [None] * 7
    for i in range(4):
        total = float(stiffness[i, 3]) * even[3]
        for k in range(3):
            total = total + float((stiffness[i, k] + stiffness[i, 6 - k]) / 2) * even[k]
        if i == 3:
            result[3] = total
            continue
        other = float((stiffness[i, 0] - stiffness[i, 6]) / 2) * odd[0]
        for k in range(1, 3):
            other = other + float((stiffness[i, k] - stiffness[i, 6 - k]) / 2) * odd[k]
        result[i] = total + other
        result[6 - i] = total - other
    return result


def cg_kernel(
    columns, first_ref, in_ref,
    out_ref, grid_ref, turn_ref, rest_ref, image_ref, way_ref,
):
    weights, derivative, stiffness = gll_one_d()
    lane = lax.broadcasted_iota(jnp.int32, (8, LANES), 1)
    at = lane % columns

    def node(i, y):
        start = (ROWS * i + y) * 8
        return slice(start, start + 8)

    def from_next(value):
        return jnp.where(
            at == columns - 1,
            pltpu.roll(value, columns - 1, 1),
            pltpu.roll(value, LANES - 1, 1),
        )

    def from_previous(value):
        return jnp.where(
            at == 0,
            pltpu.roll(value, LANES - columns + 1, 1),
            pltpu.roll(value, 1, 1),
        )

    same = (
        lax.broadcasted_iota(jnp.int32, (LANES, LANES), 0) // columns
        == lax.broadcasted_iota(jnp.int32, (LANES, LANES), 1) // columns
    )
    ones = jnp.where(same, 1.0, 0.0).astype(jnp.bfloat16)
    ones = jnp.concatenate([ones, ones, ones], axis=0)

    def tree(values):
        return (values[0] + values[1]) + (values[2] + values[3]) + (values[4] + values[5])

    def over_columns(value):
        value = jnp.where(value == value, value, 0.0)
        return dot(jnp.concatenate(split_three(value), axis=1), ones)

    blank = jnp.zeros((LANES - 3 * columns, LANES), jnp.float32)
    wide = lax.broadcasted_iota(jnp.int32, (columns, LANES), 1)
    for mode in range(8):
        rows = [in_ref[pl.ds(start + mode, columns, stride=CHUNK), :] for start in (0, 8)]
        last = in_ref[pl.ds(16 + mode % 4, columns, stride=CHUNK), :]
        if mode == 0:
            turn_ref[...] = jnp.concatenate([last] * (LANES // columns), axis=0).T
        if mode >= 4:
            last = pltpu.roll(last, LANES // 2, 1)
        beside = jnp.where(
            wide < WHOLE + SPLIT,
            pltpu.roll(rows[0], LANES - KEPT + WHOLE, 1),
            pltpu.roll(rows[1], LANES - KEPT + WHOLE + SPLIT, 1),
        )
        rows.append(jnp.where(wide < WHOLE, last, beside))
        turned = jnp.concatenate(rows + [blank], axis=0).T
        grid_ref[pl.ds(mode, LANES, stride=8), :] = turned

    def extent(which):
        at = WHOLE + which
        return jnp.broadcast_to(turn_ref[at : at + 1, :], (8, LANES))

    hx = [extent(0), extent(1)]
    hy = [extent(2), extent(3)]
    mode = first_ref[0] + lax.broadcasted_iota(jnp.int32, (8, LANES), 0)
    wave = span_wave * jnp.where(mode == 1, PLANES // 2, mode // 2).astype(jnp.float32)
    pair_wave = span_wave * (mode // 2).astype(jnp.float32)
    helmholtz = inverse_step + wave * wave
    ratio_along = [hy[r] / hx[r] for r in range(2)]
    ratio_across = [hx[r] / hy[r] for r in range(2)]
    mass = [helmholtz * (hx[r] * hy[r] / 4.0) for r in range(2)]

    def over_rows(pair, y):
        if y < 6:
            return float(weights[y]) * pair[0]
        if y > 6:
            return float(weights[y - 6]) * pair[1]
        return float(weights[6]) * pair[0] + float(weights[0]) * pair[1]

    def shared(pair):
        return [
            float(weights[0]) * value + float(weights[6]) * from_previous(value) for value in pair
        ]

    mass_shared = shared(mass)
    across_shared = shared(ratio_across)

    group = lane // columns

    def handed(start, y):
        row = (start + y % SHARE) * 8
        value = grid_ref[row : row + 8, :]
        by = COLS - y // SHARE
        return jnp.where(
            at < by, pltpu.roll(value, LANES - columns + by, 1), pltpu.roll(value, by, 1)
        )

    at_first = at % COLS == 0

    def masked(pair):
        return [jnp.where(at_first, value, 0.0) for value in pair]

    first_speed = [handed(SPEED, y) for y in range(ROWS)]
    first = [handed(FIRST, y) for y in range(ROWS)]
    second = [handed(SECOND, y) for y in range(ROWS)]
    half_x = masked([0.5 * value for value in hx])
    half_y = masked([0.5 * value for value in hy])
    area = masked([0.25 * hx[r] * hy[r] for r in range(2)])
    edge_along = masked(ratio_along)
    edge_across = masked(ratio_across)
    sloped = weights[:, None] * derivative
    lines = [jnp.zeros((8, LANES), jnp.float32)] * ROWS
    for r in range(2):
        rows = range(6 * r, 6 * r + SIDE)
        curved = apply_line(stiffness, [first_speed[y] for y in rows])
        for j, y in enumerate(rows):
            slope = sum(float(sloped[j, k]) * second[6 * r + k] for k in range(SIDE))
            lines[y] = lines[y] + float(weights[0]) * (
                half_x[r] * slope - edge_across[r] * curved[j]
            )
    even = mode % 2 == 0
    total = jnp.zeros((8, LANES), jnp.float32)
    for y in range(ROWS):
        along = jnp.where(group == 1, pltpu.roll(second[y], columns, 1), first[y])
        span = jnp.where(
            group == 0,
            pltpu.roll(first[y], 2 * columns, 1),
            jnp.where(
                group == 1,
                pltpu.roll(second[y], LANES - columns, 1),
                pltpu.roll(first[y], columns, 1),
            ),
        )
        span = jnp.where(even, pltpu.roll(span, 7, 0), -pltpu.roll(span, 1, 0))
        across = lines[y] + float(weights[0]) * over_rows(area, y) * (
            pair_wave * span - (wave * wave) * first_speed[y]
        )
        flux = over_rows(half_y, y) * along
        speed = over_rows(edge_along, y) * first_speed[y]
        values = [
            grid_ref[node(i, y), :]
            + float(sloped[i, 0]) * flux
            - float(stiffness[i, 0]) * speed
            for i in range(SIDE)
        ]
        values[0] = values[0] + across + from_previous(values[6])
        for i in range(6):
            value = values[i]
            rest_ref[node(i, y), :] = value
            way_ref[0, node(i, y), :] = value
            total = total + value * value
    rest_norm = over_columns(total)

    def apply(iteration, turn):
        for y in range(ROWS):
            values = []
            for i in range(6):
                value = rest_ref[node(i, y), :]
                if iteration:
                    value = value + turn * way_ref[iteration - 1, node(i, y), :]
                    way_ref[iteration, node(i, y), :] = value
                values.append(value)
            values.append(from_next(values[0]))
            lines = apply_line(stiffness, values)
            along = over_rows(ratio_along, y)
            lines = [along * line for line in lines]
            lines[0] = lines[0] + from_previous(lines[6])
            inner = over_rows(mass, y)
            inner = [None] + [float(weights[i]) * inner for i in range(1, 4)]
            inner = [over_rows(mass_shared, y)] + inner[1:] + [inner[2], inner[1]]
            for i in range(6):
                image_ref[node(i, y), :] = lines[i] + inner[i] * values[i]
        totals = [jnp.zeros((8, LANES), jnp.float32)] * 6
        for i in range(6):
            values = [way_ref[iteration, node(i, y), :] for y in range(ROWS)]
            lower = apply_line(stiffness, values[:7])
            upper = apply_line(stiffness, values[6:])
            if i == 0:
                scale = across_shared
            else:
                scale = [float(weights[i]) * value for value in ratio_across]
            lower = [scale[0] * value for value in lower]
            upper = [scale[1] * value for value in upper]
            lines = lower[:6] + [lower[6] + upper[0]] + upper[1:]
            for y in range(ROWS):
                image = image_ref[node(i, y), :] + lines[y]
                image_ref[node(i, y), :] = image
                totals[y % 6] = totals[y % 6] + values[y] * image
        return over_columns(tree(totals))

    turn = None
    sizes = []
    for iteration in range(ITERS):
        size = rest_norm / apply(iteration, turn)
        sizes.append(size)
        if iteration == ITERS - 1:
            break
        totals = [jnp.zeros((8, LANES), jnp.float32)] * 6
        for y in range(ROWS):
            for i in range(6):
                rest = rest_ref[node(i, y), :] - size * image_ref[node(i, y), :]
                rest_ref[node(i, y), :] = rest
                totals[i] = totals[i] + rest * rest
        following = over_columns(tree(totals))
        turn = following / rest_norm
        rest_norm = following
    zero = jnp.zeros((8, LANES), jnp.float32)
    for y in range(ROWS):
        grid_ref[node(0, y), :] = zero
        for i in range(6):
            value = sizes[0] * way_ref[0, node(i, y), :]
            for step in range(1, ITERS):
                value = value + sizes[step] * way_ref[step, node(i, y), :]
            if i == 0:
                grid_ref[node(6, y), :] = from_next(value)
            else:
                grid_ref[node(i, y), :] = value
    for left in range(GRID, LANES):
        grid_ref[left * 8 : left * 8 + 8, :] = zero
    parts = columns // COLS
    node_lane = lax.broadcasted_iota(jnp.int32, (3 * parts, LANES), 1)
    owned = (node_lane >= ROWS) & (node_lane < GRID)
    rest_from = LANES - ROWS - SPARE
    for mode in range(8):
        turn_ref[...] = grid_ref[pl.ds(mode, LANES, stride=8), :].T
        pieces = [turn_ref[pl.ds(k, 3 * parts, stride=COLS), :] for k in range(COLS)]
        for k in range(2):
            tile = jnp.where(owned, pieces[k], pltpu.roll(pieces[k + 2], OWNED, 1))
            for c in range(3):
                out_ref[pl.ds(24 * k + 8 * c + mode, parts, stride=64), :] = tile[
                    c * parts : (c + 1) * parts, :
                ]
        rest = jnp.where(
            node_lane < REST,
            pltpu.roll(pieces[2], rest_from, 1),
            pltpu.roll(pieces[3], rest_from + REST, 1),
        )
        rest = [rest[c * parts : (c + 1) * parts, :] for c in range(3)]
        both = jnp.where(
            node_lane[:parts, :] < LANES // 2, rest[0], pltpu.roll(rest[1], LANES // 2, 1)
        )
        out_ref[pl.ds(48 + mode, parts, stride=64), :] = both
        out_ref[pl.ds(56 + mode, parts, stride=64), :] = rest[2]


def choice_kernel(ids_ref, out_ref):
    nodes = lax.broadcasted_iota(jnp.int32, (LANES, out_ref.shape[1]), 1)
    for column in range(COLS):
        ids = jnp.broadcast_to(ids_ref[column : column + 1, :].astype(jnp.float32), (LANES, LANES))
        ids = ids.T[:, 0:1].astype(jnp.int32)
        out_ref[column * LANES : (column + 1) * LANES, :] = jnp.where(
            nodes == ids, 1.0, 0.0
        ).astype(jnp.bfloat16)


def scatter_kernel(velocity_ref, change_ref, chosen_ref, out_ref):
    rows = velocity_ref.shape[0]
    sources = change_ref.shape[0]
    def tiles(start):
        return jnp.concatenate(
            [change_ref[m, start : start + 8, :] for m in range(sources)], axis=0
        )

    lane = lax.broadcasted_iota(jnp.int32, (8 * sources, LANES), 1)
    pieces = []
    shared, single = tiles(48), tiles(56)
    for c in range(3):
        held = [tiles(24 * k + 8 * c) for k in range(2)]
        rest, skip = (single, 0) if c == 2 else (shared, c * (LANES // 2))
        for k in range(2):
            moved = pltpu.roll(rest, (ROWS + SPARE - k * REST - skip) % LANES, 1)
            held.append(jnp.where(lane < ROWS + SPARE, pltpu.roll(held[k], SPARE, 1), moved))
        pieces.append(jnp.concatenate(held, axis=1))
    parts = jnp.concatenate(split_two(jnp.concatenate(pieces, axis=0)), axis=0)
    change = dot(parts, chosen_ref[...])
    out_ref[...] = velocity_ref[...] + (change[:rows, :] + change[rows:, :])


def call(kernel, out_shape, scratch=(), spaces="", cost=None):
    place = {
        "s": pl.BlockSpec(memory_space=pltpu.SMEM),
        "v": pl.BlockSpec(memory_space=pltpu.VMEM),
        "h": pl.BlockSpec(memory_space=pltpu.HBM),
    }
    many = isinstance(out_shape, tuple)
    run = pl.pallas_call(
        kernel,
        out_shape=out_shape,
        in_specs=[place[space] for space in spaces],
        out_specs=(place["v"],) * len(out_shape) if many else place["v"],
        scratch_shapes=list(scratch),
        cost_estimate=cost,
        compiler_params=pltpu.CompilerParams(vmem_limit_bytes=16 * 2**20),
    )

    def with_spaces(*operands):
        return run(
            *(
                pltpu.with_memory_space_constraint(operand, pltpu.HBM) if space == "h" else operand
                for space, operand in zip(spaces, operands)
            )
        )

    return with_spaces


def transposed(velocity, connect, right_list, extents):
    components, modes, own_nodes = velocity.shape
    groups = lax.axis_size("planes")
    parts = lax.axis_size("mesh")
    plane = lax.axis_index("planes")
    part = lax.axis_index("mesh")
    rows = components * modes
    columns = parts * COLS
    synthesis, forward = fourier_tables(PLANES)
    forward = np.concatenate([forward, span_forward(forward)], axis=1) * (-1.0 / viscosity)
    fourier = np.stack(two_parts(np.concatenate([synthesis, forward], axis=1)))
    matrices, masses = column_tables()
    place = np.stack([placement(row, True) for row in range(2)])
    flat = velocity.reshape(rows, own_nodes)
    f32 = jnp.float32
    slot_shape = jax.ShapeDtypeStruct((modes * 9 // 4, LANES), f32)
    *slots, ids = call(
        gather_kernel,
        (slot_shape,) * COLS + (jax.ShapeDtypeStruct((8, LANES), jnp.int32),),
        scratch=(
            pltpu.VMEM(connect.shape[::-1], jnp.int32),
            pltpu.VMEM(place.shape, jnp.bfloat16),
            pltpu.VMEM((rows, own_nodes), f32),
            pltpu.SemaphoreType.DMA((3,)),
        ),
        spaces="shhh",
    )(plane.reshape(1), connect.T, jnp.asarray(place, jnp.bfloat16), flat)
    for s in reversed(range(1, groups)):
        slots[s] = lax.ppermute(slots[s], "planes", [(p, p ^ s) for p in range(groups)])
    tables = call(
        functools.partial(setup_kernel, own_nodes),
        (
            jax.ShapeDtypeStruct(fourier.shape, jnp.bfloat16),
            jax.ShapeDtypeStruct((2, 3 * LANES, LANES), jnp.bfloat16),
            jax.ShapeDtypeStruct((8, LANES), f32),
        ),
        scratch=(
            pltpu.VMEM(connect.shape[::-1], jnp.int32),
            pltpu.VMEM(extents.shape, f32),
            pltpu.VMEM(matrices.shape, f32),
            pltpu.VMEM(masses.shape, f32),
            pltpu.SemaphoreType.DMA((5,)),
        ),
        spaces="shhhhh",
        cost=pl.CostEstimate(flops=10**6, bytes_accessed=3 * 10**6, transcendentals=0),
    )(
        plane.reshape(1), connect.T, extents,
        jnp.asarray(fourier), jnp.asarray(matrices), jnp.asarray(masses),
    )
    residual = call(
        functools.partial(residual_kernel, modes),
        jax.ShapeDtypeStruct((columns * CHUNK, LANES), f32),
        scratch=(pltpu.VMEM((PLANES, 3 * LANES), f32),),
        spaces="svvvvvvv",
    )(plane.reshape(1), *slots, *tables)
    residual = lax.all_to_all(
        residual.reshape(columns * CHUNK, 1, LANES),
        ("mesh", "planes"),
        split_axis=0,
        concat_axis=0,
        tiled=True,
    )
    chosen = call(
        choice_kernel,
        jax.ShapeDtypeStruct((COLS * LANES, own_nodes), jnp.bfloat16),
        spaces="v",
        cost=pl.CostEstimate(flops=10**6, bytes_accessed=10**6, transcendentals=0),
    )(ids)
    held = pltpu.VMEM((96 * 8, LANES), f32)
    change = call(
        functools.partial(cg_kernel, columns),
        jax.ShapeDtypeStruct((parts * 64, LANES), f32),
        scratch=(pltpu.VMEM((LANES * 8, LANES), f32), pltpu.VMEM((LANES, LANES), f32))
        + (held, held, pltpu.VMEM((ITERS, 6 * ROWS * 8, LANES), f32)),
        spaces="sv",
    )((plane * modes + part * 8).reshape(1), residual.reshape(columns * CHUNK, LANES))
    change = lax.all_to_all(
        change.reshape(parts, 64, LANES), "mesh", split_axis=0, concat_axis=0, tiled=True
    )
    result = call(scatter_kernel, jax.ShapeDtypeStruct((rows, own_nodes), f32), spaces="vvv")(
        flat, change, chosen
    )
    return result.reshape(velocity.shape)


def from_behind(value, axis, by):
    peers = lax.axis_size(axis)
    return lax.ppermute(value, axis, [(i, (i + by) % peers) for i in range(peers)])


def partitioned(velocity, connect, right_list, extents):
    components, modes, own_nodes = velocity.shape
    edge_count = right_list.shape[0]
    first_mode = lax.axis_index("planes") * modes
    tables = [jnp.asarray(table, jnp.float32) for table in element_tables()]
    stiff_along, stiff_across, slope_along, slope_across, mass_weights = tables
    synthesis, forward = (jnp.asarray(t, jnp.float32) for t in fourier_tables(PLANES))
    hx, hy = extents[0], extents[1]
    mass_full = mass_weights[:, None] * (hx * hy / 4.0)[None, :]
    index_list = first_mode + jnp.arange(modes, dtype=jnp.int32)
    wave = span_wave * jnp.where(index_list == 1, PLANES // 2, index_list // 2).astype(jnp.float32)
    wave = wave[None, :, None, None]
    helmholtz = inverse_step + wave * wave
    locals_ = jnp.arange(own_nodes + edge_count, dtype=jnp.int32)
    chosen = (locals_[:, None, None] == connect[None]).astype(jnp.float32)
    at_edge = (locals_[:own_nodes, None] == right_list[None]).astype(jnp.float32)

    def contract(spec, *operands):
        return jnp.einsum(spec, *operands, precision=highest)

    physical = contract(
        "jq,cqn->cjn",
        synthesis,
        lax.all_to_all(velocity, "planes", split_axis=2, concat_axis=1, tiled=True),
    )
    pairs = ((0, 0), (0, 1), (0, 2), (1, 1), (1, 2), (2, 2))
    products = jnp.stack([physical[a] * physical[b] for a, b in pairs])
    product_hat = lax.all_to_all(
        contract("qj,fjn->fqn", forward, products), "planes", split_axis=1, concat_axis=2, tiled=True
    )

    def spread(fields):
        ghosts = from_behind(contract("cqn,ny->cqy", fields, at_edge), "mesh", 1)
        return contract("cqn,nke->cqke", jnp.concatenate([fields, ghosts], axis=2), chosen)

    def assemble(terms):
        summed = contract("cqke,nke->cqn", terms, chosen)
        returned = from_behind(summed[:, :, own_nodes:], "mesh", -1)
        return summed[:, :, :own_nodes] + contract("cqy,ny->cqn", returned, at_edge)

    def stiffness(values):
        return (hy / hx) * contract("lk,cqke->cqle", stiff_along, values) + (hx / hy) * contract(
            "lk,cqke->cqle", stiff_across, values
        )

    def dots(left, right):
        return lax.psum(jnp.sum(left * right, axis=2), "mesh")

    values = spread(jnp.concatenate([velocity, product_hat], axis=0))
    speeds, along = values[0:3], values[3:6]
    across = jnp.stack([values[4], values[6], values[7]])
    span = jnp.stack([values[5], values[7], values[8]])
    shaped = span.reshape(span.shape[0], modes // 2, 2, *span.shape[2:])
    turned = jnp.stack([shaped[:, :, 1], -shaped[:, :, 0]], axis=2).reshape(span.shape)
    pair_wave = span_wave * (index_list // 2).astype(jnp.float32)[None, :, None, None]
    advection = (hy / 2.0) * contract("lk,cqke->cqle", slope_along, along)
    advection = advection + (hx / 2.0) * contract("lk,cqke->cqle", slope_across, across)
    advection = advection + mass_full * (pair_wave * turned)
    residual = assemble(
        -(wave * wave) * mass_full * speeds - stiffness(speeds) - advection / viscosity
    )
    solution = velocity
    direction = residual
    norm_now = dots(residual, residual)
    for _ in range(ITERS):
        values = spread(direction)
        operated = assemble(stiffness(values) + helmholtz * mass_full * values)
        step_size = (norm_now / dots(direction, operated))[:, :, None]
        solution = solution + step_size * direction
        residual = residual - step_size * operated
        norm_next = dots(residual, residual)
        direction = residual + (norm_next / norm_now)[:, :, None] * direction
        norm_now = norm_next
    return solution


def on_device(velocity, connect, right_list, extents):
    groups = lax.axis_size("planes")
    parts = lax.axis_size("mesh")
    modes = velocity.shape[1]
    fits = groups == COLS and modes == 8 * parts and 3 * parts * COLS <= LANES
    step = transposed if fits else partitioned
    return step(velocity, connect, right_list, extents)


def solution(mesh):
    placed = (P(None, "planes", "mesh"), P(None, "mesh"), P("mesh"), P(None, "mesh"))
    return jax.shard_map(
        on_device, mesh=mesh, in_specs=placed, out_specs=P(None, "planes", "mesh"), check_vma=False
    )
```

```python
import functools

import jax
import jax.numpy as jnp
import numpy as np
from jax import lax
from jax.experimental import pallas as pl
from jax.experimental.pallas import tpu as pltpu
from jax.sharding import PartitionSpec as P

PLANES = 256
ITERS = 4
SIDE = 7
ROWS = 13
COLS = 4
GRID = SIDE * ROWS
LANES = 128
SHARE = 4
SPEED = GRID
FIRST = GRID + SHARE
SECOND = GRID + 2 * SHARE
KEPT = GRID + 3 * SHARE
SPLIT = LANES - KEPT
WHOLE = KEPT - 2 * SPLIT
TAKEN = GRID + SHARE
ROOM = LANES - TAKEN
QUARTER = LANES // 4
CHUNK = 20
OWNED = GRID - ROWS
SPARE = LANES - OWNED
REST = OWNED - SPARE

highest = lax.Precision.HIGHEST
viscosity = 0.002
time_step = 3e-05
span_wave = 4.0
inverse_step = 1.0 / (viscosity * time_step)


def legendre_six(points):
    previous = 0.0 * points + 1.0
    current = 1.0 * points
    for order in range(1, 6):
        following = ((2 * order + 1) * points * current - order * previous) / (order + 1)
        previous = current
        current = following
    return current


def gll_one_d():
    degree = 6
    points = np.array(
        [
            -1.0,
            -0.830223896278567,
            -0.4688487934707142,
            0.0,
            0.4688487934707142,
            0.830223896278567,
            1.0,
        ]
    )
    values = legendre_six(points)
    weights = 2.0 / (degree * (degree + 1) * values**2)
    derivative = np.zeros((degree + 1, degree + 1))
    for row_index in range(degree + 1):
        for col_index in range(degree + 1):
            if row_index != col_index:
                derivative[row_index, col_index] = values[row_index] / (
                    values[col_index] * (points[row_index] - points[col_index])
                )
    derivative[0, 0] = -degree * (degree + 1) / 4.0
    derivative[degree, degree] = degree * (degree + 1) / 4.0
    stiffness = derivative.T @ (weights[:, None] * derivative)
    return weights, derivative, stiffness


def element_tables():
    weights, derivative, stiffness = gll_one_d()
    identity = np.eye(SIDE)
    mass_weights = np.kron(weights, weights)
    return (
        np.kron(np.diag(weights), stiffness),
        np.kron(stiffness, np.diag(weights)),
        mass_weights[:, None] * np.kron(identity, derivative),
        mass_weights[:, None] * np.kron(derivative, identity),
        mass_weights,
    )


def fourier_tables(planes):
    plane_grid = np.arange(planes)
    synthesis = np.zeros((planes, planes))
    forward = np.zeros((planes, planes))
    synthesis[:, 0] = 1.0
    synthesis[:, 1] = np.cos(np.pi * plane_grid)
    forward[0] = 1.0 / planes
    forward[1] = np.cos(np.pi * plane_grid) / planes
    for wavenumber in range(1, planes // 2):
        phase_angle = 2.0 * np.pi * wavenumber * plane_grid / planes
        synthesis[:, 2 * wavenumber] = np.cos(phase_angle)
        synthesis[:, 2 * wavenumber + 1] = np.sin(phase_angle)
        forward[2 * wavenumber] = 2.0 * np.cos(phase_angle) / planes
        forward[2 * wavenumber + 1] = 2.0 * np.sin(phase_angle) / planes
    return synthesis, forward


def span_forward(forward):
    turned = np.zeros_like(forward)
    for wavenumber in range(1, forward.shape[0] // 2):
        turned[2 * wavenumber] = span_wave * wavenumber * forward[2 * wavenumber + 1]
        turned[2 * wavenumber + 1] = -span_wave * wavenumber * forward[2 * wavenumber]
    return turned


def two_parts(table):
    table = np.asarray(table, np.float32)
    high = table.astype(jnp.bfloat16)
    low = (table - high.astype(np.float32)).astype(jnp.bfloat16)
    return high, low


def placement(row, skip_shared):
    table = np.zeros((SIDE * SIDE, LANES))
    for j in range(SIDE):
        if skip_shared and row == 1 and j == 0:
            continue
        for i in range(SIDE):
            table[SIDE * j + i, ROWS * i + 6 * row + j] = 1.0
    return table


def column_tables():
    stiff_along, stiff_across, slope_along, slope_across, mass_weights = element_tables()
    matrices = []
    for table in (slope_along, slope_across, stiff_along, stiff_across):
        for row in range(2):
            place = placement(row, False)
            matrices.append(place.T @ table.T @ place)
    for start in (FIRST, SECOND):
        matrix = np.zeros((LANES, LANES))
        for at in range(SHARE):
            matrix[SPEED + at, start + at] = 1.0
        matrices.append(matrix)
    masses = [mass_weights @ placement(row, False) for row in range(2)]
    return np.stack(matrices).astype(np.float32), np.stack(masses).astype(np.float32)


def split_two(value):
    high = value.astype(jnp.bfloat16)
    low = (value - high.astype(jnp.float32)).astype(jnp.bfloat16)
    return high, low


def split_three(value):
    high = value.astype(jnp.bfloat16)
    rest = value - high.astype(jnp.float32)
    middle = rest.astype(jnp.bfloat16)
    low = (rest - middle.astype(jnp.float32)).astype(jnp.bfloat16)
    return high, middle, low


def dot(left, right):
    return jnp.dot(left, right, preferred_element_type=jnp.float32)


def dot_split(left, right):
    return dot(left[0], right[0]) + (dot(left[0], right[1]) + dot(left[1], right[0]))


def one_hot(ids_row, count):
    rows = lax.broadcasted_iota(jnp.int32, (count, LANES), 0)
    return jnp.where(rows == ids_row, 1.0, 0.0).astype(jnp.bfloat16)


def element_order(element_ids, own_nodes):
    wide = (element_ids.shape[0], LANES)
    first_corner = jnp.broadcast_to(element_ids[:, 0:1], wide)
    last_corner = jnp.broadcast_to(element_ids[:, SIDE - 1 : SIDE], wide)
    picked = [
        jnp.where(first_corner == float(own_nodes + 6 * row), 1.0, 0.0) for row in range(2)
    ]
    order = [picked]
    for _ in range(COLS - 1):
        corners = [jnp.sum(last_corner * mask, axis=0, keepdims=True) for mask in picked]
        picked = [jnp.where(first_corner == corner, 1.0, 0.0) for corner in corners]
        order.append(picked)
    return order


def gather_kernel(
    plane_ref, connect_hbm, place_hbm, velocity_hbm,
    slot_a, slot_b, slot_c, slot_d, ids_ref,
    connect_ref, place_ref, velocity_ref, arrived,
):
    slots = (slot_a, slot_b, slot_c, slot_d)
    sources = (connect_hbm, place_hbm, velocity_hbm)
    targets = (connect_ref, place_ref, velocity_ref)
    copies = [
        pltpu.make_async_copy(source, target, arrived.at[at])
        for at, (source, target) in enumerate(zip(sources, targets))
    ]
    for copy in copies:
        copy.start()
    own_nodes = velocity_ref.shape[1]
    modes = velocity_ref.shape[0] // 3
    lane = lax.broadcasted_iota(jnp.int32, (1, LANES), 1)
    plane = plane_ref[0]
    copies[0].wait()
    element_ids = connect_ref[...].astype(jnp.float32)
    order = element_order(element_ids, own_nodes)
    ids_parts = split_two(element_ids)
    copies[1].wait()
    placed = [dot(ids_parts[0], place_ref[r]) + dot(ids_parts[1], place_ref[r]) for r in range(2)]
    rows = []
    for column in range(COLS):
        picked = order[column]
        ids = jnp.sum(placed[0] * picked[0] + placed[1] * picked[1], axis=0, keepdims=True)
        rows.append(jnp.where(lane < GRID, ids.astype(jnp.int32), -1))
    kept = [jnp.where(lane >= ROWS, ids, -1) for ids in rows]
    ids_ref[...] = jnp.concatenate(kept + [jnp.full((8 - COLS, LANES), -1, jnp.int32)], axis=0)
    last = jnp.broadcast_to(rows[COLS - 1].astype(jnp.float32), (8, LANES))
    for column in range(COLS):
        count = min(SHARE, ROWS - SHARE * column)
        taken = pltpu.roll(last, SPEED - 6 * ROWS - SHARE * column, 1)[0:1, :].astype(jnp.int32)
        rows[column] = jnp.where((lane >= SPEED) & (lane < SPEED + count), taken, rows[column])
    chosen = []
    for slot in range(COLS):
        ids = rows[0]
        for column in range(1, COLS):
            ids = jnp.where((plane ^ slot) == column, rows[column], ids)
        chosen.append(one_hot(ids, own_nodes))
    copies[2].wait()
    both = dot(
        jnp.concatenate(split_two(velocity_ref[...]), axis=0), jnp.concatenate(chosen, axis=1)
    )
    both = both[: 3 * modes, :] + both[3 * modes :, :]
    tile_lane = lax.broadcasted_iota(jnp.int32, (modes, LANES), 1)
    quarter = modes // 4
    for slot in range(COLS):
        values = both[:, slot * LANES : (slot + 1) * LANES]
        last = values[2 * modes :, :]
        for c in range(2):
            slots[slot][c * modes : (c + 1) * modes, :] = jnp.where(
                tile_lane < TAKEN,
                values[c * modes : (c + 1) * modes, :],
                pltpu.roll(last, TAKEN - c * ROOM, 1),
            )
        rest = pltpu.roll(last[:quarter, :], LANES - 2 * ROOM, 1)
        for part in range(1, 4):
            rest = jnp.where(
                tile_lane[:quarter, :] < part * QUARTER,
                rest,
                pltpu.roll(
                    last[part * quarter : (part + 1) * quarter, :],
                    (part * QUARTER - 2 * ROOM) % LANES,
                    1,
                ),
            )
        slots[slot][2 * modes :, :] = rest


def three_of(slot, modes):
    lower, upper, rest = slot[:modes, :], slot[modes : 2 * modes, :], slot[2 * modes :, :]
    lane = lax.broadcasted_iota(jnp.int32, (modes, LANES), 1)
    spread = [pltpu.roll(rest, (2 * ROOM - part * QUARTER) % LANES, 1) for part in range(4)]
    last = jnp.where(
        lane < ROOM,
        pltpu.roll(lower, ROOM, 1),
        jnp.where(
            lane < 2 * ROOM, pltpu.roll(upper, 2 * ROOM, 1), jnp.concatenate(spread, axis=0)
        ),
    )
    return jnp.concatenate([lower, upper, last], axis=1)


def setup_kernel(
    own_nodes, plane_at, connect_hbm, extents_hbm, fourier_hbm, plane_hbm, mass_hbm,
    fourier_ref, in_plane_ref, row_ref,
    connect_ref, extents_ref, plane_ref, mass_ref, arrived,
):
    sources = (connect_hbm, extents_hbm, mass_hbm, plane_hbm, fourier_hbm)
    targets = (connect_ref, extents_ref, mass_ref, plane_ref, fourier_ref)
    copies = [
        pltpu.make_async_copy(source, target, arrived.at[at])
        for at, (source, target) in enumerate(zip(sources, targets))
    ]
    for copy in copies:
        copy.start()
    for copy in copies[:3]:
        copy.wait()
    element_ids = connect_ref[...].astype(jnp.float32)
    elements = element_ids.shape[0]
    order = element_order(element_ids, own_nodes)
    lane = lax.broadcasted_iota(jnp.int32, (1, LANES), 1)
    diagonal = lax.broadcasted_iota(jnp.int32, (elements, elements), 0) == lax.broadcasted_iota(
        jnp.int32, (elements, elements), 1
    )
    held = []
    for axis in range(2):
        lengths = jnp.sum(
            jnp.where(diagonal, extents_ref[axis : axis + 1, :], 0.0), axis=1, keepdims=True
        )
        for row in range(2):
            mask = order[0][row]
            for column in range(1, COLS):
                mask = jnp.where(plane_at[0] == column, order[column][row], mask)
            held.append(jnp.sum(lengths * mask, axis=0, keepdims=True))
    hx, hy = held[:2], held[2:]
    carried = jnp.zeros((1, LANES), jnp.float32)
    for at, value in enumerate(held):
        carried = carried + jnp.where(lane == WHOLE + at, value, 0.0)
    mass = sum((hx[r] * hy[r] / 4.0) * mass_ref[r : r + 1, :] for r in range(2))
    row_ref[...] = jnp.concatenate([mass, carried, jnp.zeros((6, LANES), jnp.float32)], axis=0)
    copies[3].wait()
    along = sum((hy[r] / 2.0) * plane_ref[r] for r in range(2)) + plane_ref[8]
    across = sum((hx[r] / 2.0) * plane_ref[2 + r] for r in range(2)) + plane_ref[9]
    stiff = viscosity * sum(
        (hy[r] / hx[r]) * plane_ref[4 + r] + (hx[r] / hy[r]) * plane_ref[6 + r] for r in range(2)
    )
    high, low = split_two(jnp.concatenate([along, across, stiff], axis=0))
    in_plane_ref[0] = high
    in_plane_ref[1] = low
    copies[4].wait()


def residual_kernel(
    modes, plane_at, slot_a, slot_b, slot_c, slot_d, fourier_ref, in_plane_ref, row_ref,
    out_ref, packed_ref,
):
    planes = PLANES
    groups = planes // modes
    for slot, slot_ref in enumerate((slot_a, slot_b, slot_c, slot_d)):
        start = pl.multiple_of((plane_at[0] ^ slot) * modes, modes)
        packed_ref[pl.ds(start, modes), :] = three_of(slot_ref[...], modes)
    packed = packed_ref[...]
    synthesis = (fourier_ref[0, :, :planes], fourier_ref[1, :, :planes])
    forward = (fourier_ref[0, :, planes:], fourier_ref[1, :, planes:])
    physical = dot_split(synthesis, split_two(packed))
    speeds = [packed[:, c * LANES : (c + 1) * LANES] for c in range(3)]
    fields = [physical[:, c * LANES : (c + 1) * LANES] for c in range(3)]
    mass = row_ref[0:1, :]
    carried = row_ref[1:2, :]
    products = [[fields[a] * fields[c] for a in range(3)] for c in range(3)]
    lane = lax.broadcasted_iota(jnp.int32, (planes, LANES), 1)
    in_plane = (in_plane_ref[0], in_plane_ref[1])
    divergence = [
        dot_split(
            split_two(jnp.concatenate([products[c][0], products[c][1], fields[c]], axis=1)),
            in_plane,
        )
        for c in range(3)
    ]
    divergence[1] = jnp.where(
        (lane >= FIRST) & (lane < SECOND),
        pltpu.roll(products[2][2], FIRST - SPEED, 1),
        divergence[1],
    )
    upper = split_two(jnp.concatenate(divergence, axis=1))
    lower = split_two(jnp.concatenate([mass * products[c][2] for c in range(3)], axis=1))
    result = dot_split((forward[0][:, :planes], forward[1][:, :planes]), upper) + dot_split(
        (forward[0][:, planes:], forward[1][:, planes:]), lower
    )
    mode = lax.broadcasted_iota(jnp.int32, (planes, LANES), 0)
    wave = span_wave * jnp.where(mode == 1, planes // 2, mode // 2).astype(jnp.float32)
    square = wave * wave
    tiles = []
    for c in range(3):
        tile = result[:, c * LANES : (c + 1) * LANES] - square * (mass * speeds[c])
        tiles.append(jnp.where((lane >= SPEED) & (lane < FIRST), speeds[c], tile))
    beside = lane >= KEPT
    tiles[0] = jnp.where(beside, pltpu.roll(tiles[2], KEPT - WHOLE, 1), tiles[0])
    tiles[1] = jnp.where(beside, pltpu.roll(tiles[2], KEPT - WHOLE - SPLIT, 1), tiles[1])
    tiles[2] = jnp.where(lane < WHOLE, tiles[2], carried)
    blocks = planes // 8
    per_group = modes // 8
    left = lax.broadcasted_iota(jnp.int32, (8, LANES), 1) < LANES // 2
    for block in range(blocks):
        start = CHUNK * ((block % per_group) * groups + block // per_group)
        rows = slice(8 * block, 8 * block + 8)
        out_ref[start : start + 8, :] = tiles[0][rows, :]
        out_ref[start + 8 : start + 16, :] = tiles[1][rows, :]
        last = tiles[2][rows, :]
        last = jnp.where(left, last, pltpu.roll(pltpu.roll(last, LANES // 2, 1), 4, 0))
        out_ref[start + 16 : start + 20, :] = last[0:4, :]


def apply_line(stiffness, values):
    even = [values[k] + values[6 - k] for k in range(3)] + [values[3]]
    odd = [values[k] - values[6 - k] for k in range(3)]
    result = [None] * 7
    for i in range(4):
        total = float(stiffness[i, 3]) * even[3]
        for k in range(3):
            total = total + float((stiffness[i, k] + stiffness[i, 6 - k]) / 2) * even[k]
        if i == 3:
            result[3] = total
            continue
        other = float((stiffness[i, 0] - stiffness[i, 6]) / 2) * odd[0]
        for k in range(1, 3):
            other = other + float((stiffness[i, k] - stiffness[i, 6 - k]) / 2) * odd[k]
        result[i] = total + other
        result[6 - i] = total - other
    return result


def cg_kernel(
    columns, first_ref, in_ref,
    out_ref, grid_ref, turn_ref, rest_ref, image_ref, way_ref,
):
    weights, derivative, stiffness = gll_one_d()
    lane = lax.broadcasted_iota(jnp.int32, (8, LANES), 1)
    at = lane % columns

    def node(i, y):
        start = (ROWS * i + y) * 8
        return slice(start, start + 8)

    def from_next(value):
        return jnp.where(
            at == columns - 1,
            pltpu.roll(value, columns - 1, 1),
            pltpu.roll(value, LANES - 1, 1),
        )

    def from_previous(value):
        return jnp.where(
            at == 0,
            pltpu.roll(value, LANES - columns + 1, 1),
            pltpu.roll(value, 1, 1),
        )

    same = (
        lax.broadcasted_iota(jnp.int32, (LANES, LANES), 0) // columns
        == lax.broadcasted_iota(jnp.int32, (LANES, LANES), 1) // columns
    )
    ones = jnp.where(same, 1.0, 0.0).astype(jnp.bfloat16)

    def tree(values):
        return (values[0] + values[1]) + (values[2] + values[3]) + (values[4] + values[5])

    def over_columns(value):
        value = jnp.where(value == value, value, 0.0)
        parts = [part.astype(jnp.float32) for part in split_three(value)]
        sums = dot(jnp.concatenate(parts, axis=0).astype(jnp.bfloat16), ones)
        return sums[0:8, :] + (sums[8:16, :] + sums[16:24, :])

    blank = jnp.zeros((LANES - 3 * columns, LANES), jnp.float32)
    for mode in range(8):
        rows = [in_ref[pl.ds(start + mode, columns, stride=CHUNK), :] for start in (0, 8)]
        last = in_ref[pl.ds(16 + mode % 4, columns, stride=CHUNK), :]
        if mode == 0:
            turn_ref[...] = jnp.concatenate([last] * (LANES // columns), axis=0).T
        if mode >= 4:
            last = pltpu.roll(last, LANES // 2, 1)
        rows.append(last)
        turned = jnp.concatenate(rows + [blank], axis=0).T
        grid_ref[pl.ds(mode, LANES, stride=8), :] = turned

    def extent(which):
        at = WHOLE + which
        return jnp.broadcast_to(turn_ref[at : at + 1, :], (8, LANES))

    hx = [extent(0), extent(1)]
    hy = [extent(2), extent(3)]
    mode = first_ref[0] + lax.broadcasted_iota(jnp.int32, (8, LANES), 0)
    wave = span_wave * jnp.where(mode == 1, PLANES // 2, mode // 2).astype(jnp.float32)
    pair_wave = span_wave * (mode // 2).astype(jnp.float32)
    helmholtz = inverse_step + wave * wave
    ratio_along = [hy[r] / hx[r] for r in range(2)]
    ratio_across = [hx[r] / hy[r] for r in range(2)]
    mass = [helmholtz * (hx[r] * hy[r] / 4.0) for r in range(2)]

    def over_rows(pair, y):
        if y < 6:
            return float(weights[y]) * pair[0]
        if y > 6:
            return float(weights[y - 6]) * pair[1]
        return float(weights[6]) * pair[0] + float(weights[0]) * pair[1]

    def shared(pair):
        return [
            float(weights[0]) * value + float(weights[6]) * from_previous(value) for value in pair
        ]

    mass_shared = shared(mass)
    across_shared = shared(ratio_across)

    group = lane // columns

    def sent(at_lane):
        value = grid_ref[at_lane * 8 : at_lane * 8 + 8, :]
        if at_lane < WHOLE:
            return value
        by = 2 if at_lane < WHOLE + SPLIT else 1
        row = (at_lane + KEPT - WHOLE - (2 - by) * SPLIT) * 8
        beside = pltpu.roll(grid_ref[row : row + 8, :], by * columns, 1)
        return jnp.where(group == 2, beside, value)

    def handed(start, y):
        value = sent(start + y % SHARE)
        by = COLS - y // SHARE
        return jnp.where(
            at < by, pltpu.roll(value, LANES - columns + by, 1), pltpu.roll(value, by, 1)
        )

    at_first = at % COLS == 0

    def masked(pair):
        return [jnp.where(at_first, value, 0.0) for value in pair]

    first_speed = [handed(SPEED, y) for y in range(ROWS)]
    first = [handed(FIRST, y) for y in range(ROWS)]
    second = [handed(SECOND, y) for y in range(ROWS)]
    half_x = masked([0.5 * value for value in hx])
    half_y = masked([0.5 * value for value in hy])
    area = masked([0.25 * hx[r] * hy[r] for r in range(2)])
    edge_along = masked(ratio_along)
    edge_across = masked(ratio_across)
    sloped = weights[:, None] * derivative
    lines = [jnp.zeros((8, LANES), jnp.float32)] * ROWS
    for r in range(2):
        rows = range(6 * r, 6 * r + SIDE)
        curved = apply_line(stiffness, [first_speed[y] for y in rows])
        for j, y in enumerate(rows):
            slope = sum(float(sloped[j, k]) * second[6 * r + k] for k in range(SIDE))
            lines[y] = lines[y] + float(weights[0]) * (
                half_x[r] * slope - edge_across[r] * curved[j]
            )
    even = mode % 2 == 0
    total = jnp.zeros((8, LANES), jnp.float32)
    for y in range(ROWS):
        along = jnp.where(group == 1, pltpu.roll(second[y], columns, 1), first[y])
        span = jnp.where(
            group == 0,
            pltpu.roll(first[y], 2 * columns, 1),
            jnp.where(
                group == 1,
                pltpu.roll(second[y], LANES - columns, 1),
                pltpu.roll(first[y], columns, 1),
            ),
        )
        span = jnp.where(even, pltpu.roll(span, 7, 0), -pltpu.roll(span, 1, 0))
        across = lines[y] + float(weights[0]) * over_rows(area, y) * (
            pair_wave * span - (wave * wave) * first_speed[y]
        )
        flux = over_rows(half_y, y) * along
        speed = over_rows(edge_along, y) * first_speed[y]
        values = [
            sent(ROWS * i + y)
            + float(sloped[i, 0]) * flux
            - float(stiffness[i, 0]) * speed
            for i in range(SIDE)
        ]
        values[0] = values[0] + across + from_previous(values[6])
        for i in range(6):
            value = values[i]
            rest_ref[node(i, y), :] = value
            way_ref[0, node(i, y), :] = value
            total = total + value * value
    rest_norm = over_columns(total)

    def apply(iteration, turn):
        for y in range(ROWS):
            values = []
            for i in range(6):
                value = rest_ref[node(i, y), :]
                if iteration:
                    value = value + turn * way_ref[iteration - 1, node(i, y), :]
                    way_ref[iteration, node(i, y), :] = value
                values.append(value)
            values.append(from_next(values[0]))
            lines = apply_line(stiffness, values)
            along = over_rows(ratio_along, y)
            lines = [along * line for line in lines]
            lines[0] = lines[0] + from_previous(lines[6])
            inner = over_rows(mass, y)
            inner = [None] + [float(weights[i]) * inner for i in range(1, 4)]
            inner = [over_rows(mass_shared, y)] + inner[1:] + [inner[2], inner[1]]
            for i in range(6):
                image_ref[node(i, y), :] = lines[i] + inner[i] * values[i]
        totals = [jnp.zeros((8, LANES), jnp.float32)] * 6
        for i in range(6):
            values = [way_ref[iteration, node(i, y), :] for y in range(ROWS)]
            lower = apply_line(stiffness, values[:7])
            upper = apply_line(stiffness, values[6:])
            if i == 0:
                scale = across_shared
            else:
                scale = [float(weights[i]) * value for value in ratio_across]
            lower = [scale[0] * value for value in lower]
            upper = [scale[1] * value for value in upper]
            lines = lower[:6] + [lower[6] + upper[0]] + upper[1:]
            for y in range(ROWS):
                image = image_ref[node(i, y), :] + lines[y]
                image_ref[node(i, y), :] = image
                totals[y % 6] = totals[y % 6] + values[y] * image
        return over_columns(tree(totals))

    turn = None
    sizes = []
    for iteration in range(ITERS):
        size = rest_norm / apply(iteration, turn)
        sizes.append(size)
        if iteration == ITERS - 1:
            break
        totals = [jnp.zeros((8, LANES), jnp.float32)] * 6
        for y in range(ROWS):
            for i in range(6):
                rest = rest_ref[node(i, y), :] - size * image_ref[node(i, y), :]
                rest_ref[node(i, y), :] = rest
                totals[i] = totals[i] + rest * rest
        following = over_columns(tree(totals))
        turn = following / rest_norm
        rest_norm = following
    zero = jnp.zeros((8, LANES), jnp.float32)
    for y in range(ROWS):
        grid_ref[node(0, y), :] = zero
        for i in range(6):
            value = sizes[0] * way_ref[0, node(i, y), :]
            for step in range(1, ITERS):
                value = value + sizes[step] * way_ref[step, node(i, y), :]
            if i == 0:
                grid_ref[node(6, y), :] = from_next(value)
            else:
                grid_ref[node(i, y), :] = value
    for left in range(GRID, LANES):
        grid_ref[left * 8 : left * 8 + 8, :] = zero
    parts = columns // COLS
    node_lane = lax.broadcasted_iota(jnp.int32, (3 * parts, LANES), 1)
    owned = (node_lane >= ROWS) & (node_lane < GRID)
    rest_from = LANES - ROWS - SPARE
    for mode in range(8):
        turn_ref[...] = grid_ref[pl.ds(mode, LANES, stride=8), :].T
        pieces = [turn_ref[pl.ds(k, 3 * parts, stride=COLS), :] for k in range(COLS)]
        for k in range(2):
            tile = jnp.where(owned, pieces[k], pltpu.roll(pieces[k + 2], OWNED, 1))
            for c in range(3):
                out_ref[pl.ds(24 * k + 8 * c + mode, parts, stride=64), :] = tile[
                    c * parts : (c + 1) * parts, :
                ]
        rest = jnp.where(
            node_lane < REST,
            pltpu.roll(pieces[2], rest_from, 1),
            pltpu.roll(pieces[3], rest_from + REST, 1),
        )
        rest = [rest[c * parts : (c + 1) * parts, :] for c in range(3)]
        both = jnp.where(
            node_lane[:parts, :] < LANES // 2, rest[0], pltpu.roll(rest[1], LANES // 2, 1)
        )
        out_ref[pl.ds(48 + mode, parts, stride=64), :] = both
        out_ref[pl.ds(56 + mode, parts, stride=64), :] = rest[2]


def choice_kernel(ids_ref, out_ref):
    nodes = lax.broadcasted_iota(jnp.int32, (LANES, out_ref.shape[1]), 1)
    for column in range(COLS):
        ids = jnp.broadcast_to(ids_ref[column : column + 1, :].astype(jnp.float32), (LANES, LANES))
        ids = ids.T[:, 0:1].astype(jnp.int32)
        out_ref[column * LANES : (column + 1) * LANES, :] = jnp.where(
            nodes == ids, 1.0, 0.0
        ).astype(jnp.bfloat16)


def scatter_kernel(velocity_ref, change_ref, chosen_ref, out_ref):
    rows = velocity_ref.shape[0]
    sources = change_ref.shape[0]
    def tiles(start):
        return jnp.concatenate(
            [change_ref[m, start : start + 8, :] for m in range(sources)], axis=0
        )

    lane = lax.broadcasted_iota(jnp.int32, (8 * sources, LANES), 1)
    pieces = []
    shared, single = tiles(48), tiles(56)
    for c in range(3):
        held = [tiles(24 * k + 8 * c) for k in range(2)]
        rest, skip = (single, 0) if c == 2 else (shared, c * (LANES // 2))
        for k in range(2):
            moved = pltpu.roll(rest, (ROWS + SPARE - k * REST - skip) % LANES, 1)
            held.append(jnp.where(lane < ROWS + SPARE, pltpu.roll(held[k], SPARE, 1), moved))
        pieces.append(jnp.concatenate(held, axis=1))
    parts = jnp.concatenate(split_two(jnp.concatenate(pieces, axis=0)), axis=0)
    change = dot(parts, chosen_ref[...])
    out_ref[...] = velocity_ref[...] + (change[:rows, :] + change[rows:, :])


def call(kernel, out_shape, scratch=(), spaces="", cost=None):
    place = {
        "s": pl.BlockSpec(memory_space=pltpu.SMEM),
        "v": pl.BlockSpec(memory_space=pltpu.VMEM),
        "h": pl.BlockSpec(memory_space=pltpu.HBM),
    }
    many = isinstance(out_shape, tuple)
    run = pl.pallas_call(
        kernel,
        out_shape=out_shape,
        in_specs=[place[space] for space in spaces],
        out_specs=(place["v"],) * len(out_shape) if many else place["v"],
        scratch_shapes=list(scratch),
        cost_estimate=cost,
        compiler_params=pltpu.CompilerParams(vmem_limit_bytes=16 * 2**20),
    )

    def with_spaces(*operands):
        return run(
            *(
                pltpu.with_memory_space_constraint(operand, pltpu.HBM) if space == "h" else operand
                for space, operand in zip(spaces, operands)
            )
        )

    return with_spaces


def transposed(velocity, connect, right_list, extents):
    components, modes, own_nodes = velocity.shape
    groups = lax.axis_size("planes")
    parts = lax.axis_size("mesh")
    plane = lax.axis_index("planes")
    part = lax.axis_index("mesh")
    rows = components * modes
    columns = parts * COLS
    synthesis, forward = fourier_tables(PLANES)
    forward = np.concatenate([forward, span_forward(forward)], axis=1) * (-1.0 / viscosity)
    fourier = np.stack(two_parts(np.concatenate([synthesis, forward], axis=1)))
    matrices, masses = column_tables()
    place = np.stack([placement(row, True) for row in range(2)])
    flat = velocity.reshape(rows, own_nodes)
    f32 = jnp.float32
    slot_shape = jax.ShapeDtypeStruct((modes * 9 // 4, LANES), f32)
    *slots, ids = call(
        gather_kernel,
        (slot_shape,) * COLS + (jax.ShapeDtypeStruct((8, LANES), jnp.int32),),
        scratch=(
            pltpu.VMEM(connect.shape[::-1], jnp.int32),
            pltpu.VMEM(place.shape, jnp.bfloat16),
            pltpu.VMEM((rows, own_nodes), f32),
            pltpu.SemaphoreType.DMA((3,)),
        ),
        spaces="shhh",
    )(plane.reshape(1), connect.T, jnp.asarray(place, jnp.bfloat16), flat)
    for s in reversed(range(1, groups)):
        slots[s] = lax.ppermute(slots[s], "planes", [(p, p ^ s) for p in range(groups)])
    tables = call(
        functools.partial(setup_kernel, own_nodes),
        (
            jax.ShapeDtypeStruct(fourier.shape, jnp.bfloat16),
            jax.ShapeDtypeStruct((2, 3 * LANES, LANES), jnp.bfloat16),
            jax.ShapeDtypeStruct((8, LANES), f32),
        ),
        scratch=(
            pltpu.VMEM(connect.shape[::-1], jnp.int32),
            pltpu.VMEM(extents.shape, f32),
            pltpu.VMEM(matrices.shape, f32),
            pltpu.VMEM(masses.shape, f32),
            pltpu.SemaphoreType.DMA((5,)),
        ),
        spaces="shhhhh",
        cost=pl.CostEstimate(flops=10**6, bytes_accessed=3 * 10**6, transcendentals=0),
    )(
        plane.reshape(1), connect.T, extents,
        jnp.asarray(fourier), jnp.asarray(matrices), jnp.asarray(masses),
    )
    residual = call(
        functools.partial(residual_kernel, modes),
        jax.ShapeDtypeStruct((columns * CHUNK, LANES), f32),
        scratch=(pltpu.VMEM((PLANES, 3 * LANES), f32),),
        spaces="svvvvvvv",
    )(plane.reshape(1), *slots, *tables)
    residual = lax.all_to_all(
        residual.reshape(columns * CHUNK, 1, LANES),
        ("mesh", "planes"),
        split_axis=0,
        concat_axis=0,
        tiled=True,
    )
    chosen = call(
        choice_kernel,
        jax.ShapeDtypeStruct((COLS * LANES, own_nodes), jnp.bfloat16),
        spaces="v",
        cost=pl.CostEstimate(flops=10**6, bytes_accessed=10**6, transcendentals=0),
    )(ids)
    held = pltpu.VMEM((96 * 8, LANES), f32)
    change = call(
        functools.partial(cg_kernel, columns),
        jax.ShapeDtypeStruct((parts * 64, LANES), f32),
        scratch=(pltpu.VMEM((LANES * 8, LANES), f32), pltpu.VMEM((LANES, LANES), f32))
        + (held, held, pltpu.VMEM((ITERS, 6 * ROWS * 8, LANES), f32)),
        spaces="sv",
    )((plane * modes + part * 8).reshape(1), residual.reshape(columns * CHUNK, LANES))
    change = lax.all_to_all(
        change.reshape(parts, 64, LANES), "mesh", split_axis=0, concat_axis=0, tiled=True
    )
    result = call(scatter_kernel, jax.ShapeDtypeStruct((rows, own_nodes), f32), spaces="vvv")(
        flat, change, chosen
    )
    return result.reshape(velocity.shape)


def from_behind(value, axis, by):
    peers = lax.axis_size(axis)
    return lax.ppermute(value, axis, [(i, (i + by) % peers) for i in range(peers)])


def partitioned(velocity, connect, right_list, extents):
    components, modes, own_nodes = velocity.shape
    edge_count = right_list.shape[0]
    first_mode = lax.axis_index("planes") * modes
    tables = [jnp.asarray(table, jnp.float32) for table in element_tables()]
    stiff_along, stiff_across, slope_along, slope_across, mass_weights = tables
    synthesis, forward = (jnp.asarray(t, jnp.float32) for t in fourier_tables(PLANES))
    hx, hy = extents[0], extents[1]
    mass_full = mass_weights[:, None] * (hx * hy / 4.0)[None, :]
    index_list = first_mode + jnp.arange(modes, dtype=jnp.int32)
    wave = span_wave * jnp.where(index_list == 1, PLANES // 2, index_list // 2).astype(jnp.float32)
    wave = wave[None, :, None, None]
    helmholtz = inverse_step + wave * wave
    locals_ = jnp.arange(own_nodes + edge_count, dtype=jnp.int32)
    chosen = (locals_[:, None, None] == connect[None]).astype(jnp.float32)
    at_edge = (locals_[:own_nodes, None] == right_list[None]).astype(jnp.float32)

    def contract(spec, *operands):
        return jnp.einsum(spec, *operands, precision=highest)

    physical = contract(
        "jq,cqn->cjn",
        synthesis,
        lax.all_to_all(velocity, "planes", split_axis=2, concat_axis=1, tiled=True),
    )
    pairs = ((0, 0), (0, 1), (0, 2), (1, 1), (1, 2), (2, 2))
    products = jnp.stack([physical[a] * physical[b] for a, b in pairs])
    product_hat = lax.all_to_all(
        contract("qj,fjn->fqn", forward, products), "planes", split_axis=1, concat_axis=2, tiled=True
    )

    def spread(fields):
        ghosts = from_behind(contract("cqn,ny->cqy", fields, at_edge), "mesh", 1)
        return contract("cqn,nke->cqke", jnp.concatenate([fields, ghosts], axis=2), chosen)

    def assemble(terms):
        summed = contract("cqke,nke->cqn", terms, chosen)
        returned = from_behind(summed[:, :, own_nodes:], "mesh", -1)
        return summed[:, :, :own_nodes] + contract("cqy,ny->cqn", returned, at_edge)

    def stiffness(values):
        return (hy / hx) * contract("lk,cqke->cqle", stiff_along, values) + (hx / hy) * contract(
            "lk,cqke->cqle", stiff_across, values
        )

    def dots(left, right):
        return lax.psum(jnp.sum(left * right, axis=2), "mesh")

    values = spread(jnp.concatenate([velocity, product_hat], axis=0))
    speeds, along = values[0:3], values[3:6]
    across = jnp.stack([values[4], values[6], values[7]])
    span = jnp.stack([values[5], values[7], values[8]])
    shaped = span.reshape(span.shape[0], modes // 2, 2, *span.shape[2:])
    turned = jnp.stack([shaped[:, :, 1], -shaped[:, :, 0]], axis=2).reshape(span.shape)
    pair_wave = span_wave * (index_list // 2).astype(jnp.float32)[None, :, None, None]
    advection = (hy / 2.0) * contract("lk,cqke->cqle", slope_along, along)
    advection = advection + (hx / 2.0) * contract("lk,cqke->cqle", slope_across, across)
    advection = advection + mass_full * (pair_wave * turned)
    residual = assemble(
        -(wave * wave) * mass_full * speeds - stiffness(speeds) - advection / viscosity
    )
    solution = velocity
    direction = residual
    norm_now = dots(residual, residual)
    for _ in range(ITERS):
        values = spread(direction)
        operated = assemble(stiffness(values) + helmholtz * mass_full * values)
        step_size = (norm_now / dots(direction, operated))[:, :, None]
        solution = solution + step_size * direction
        residual = residual - step_size * operated
        norm_next = dots(residual, residual)
        direction = residual + (norm_next / norm_now)[:, :, None] * direction
        norm_now = norm_next
    return solution


def on_device(velocity, connect, right_list, extents):
    groups = lax.axis_size("planes")
    parts = lax.axis_size("mesh")
    modes = velocity.shape[1]
    fits = groups == COLS and modes == 8 * parts and 3 * parts * COLS <= LANES
    step = transposed if fits else partitioned
    return step(velocity, connect, right_list, extents)


def solution(mesh):
    placed = (P(None, "planes", "mesh"), P(None, "mesh"), P("mesh"), P(None, "mesh"))
    return jax.shard_map(
        on_device, mesh=mesh, in_specs=placed, out_specs=P(None, "planes", "mesh"), check_vma=False
    )
```

```python
import functools

import jax
import jax.numpy as jnp
import numpy as np
from jax import lax
from jax.experimental import pallas as pl
from jax.experimental.pallas import tpu as pltpu
from jax.sharding import PartitionSpec as P

PLANES = 256
ITERS = 4
SIDE = 7
ROWS = 13
COLS = 4
GRID = SIDE * ROWS
LANES = 128
SHARE = 4
SPEED = GRID
FIRST = GRID + SHARE
SECOND = GRID + 2 * SHARE
KEPT = GRID + 3 * SHARE
SPLIT = LANES - KEPT
WHOLE = KEPT - 2 * SPLIT
TAKEN = GRID + SHARE
ROOM = LANES - TAKEN
QUARTER = LANES // 4
CHUNK = 20
OWNED = GRID - ROWS
SPARE = LANES - OWNED
REST = OWNED - SPARE

highest = lax.Precision.HIGHEST
viscosity = 0.002
time_step = 3e-05
span_wave = 4.0
inverse_step = 1.0 / (viscosity * time_step)


def legendre_six(points):
    previous = 0.0 * points + 1.0
    current = 1.0 * points
    for order in range(1, 6):
        following = ((2 * order + 1) * points * current - order * previous) / (order + 1)
        previous = current
        current = following
    return current


def gll_one_d():
    degree = 6
    points = np.array(
        [
            -1.0,
            -0.830223896278567,
            -0.4688487934707142,
            0.0,
            0.4688487934707142,
            0.830223896278567,
            1.0,
        ]
    )
    values = legendre_six(points)
    weights = 2.0 / (degree * (degree + 1) * values**2)
    derivative = np.zeros((degree + 1, degree + 1))
    for row_index in range(degree + 1):
        for col_index in range(degree + 1):
            if row_index != col_index:
                derivative[row_index, col_index] = values[row_index] / (
                    values[col_index] * (points[row_index] - points[col_index])
                )
    derivative[0, 0] = -degree * (degree + 1) / 4.0
    derivative[degree, degree] = degree * (degree + 1) / 4.0
    stiffness = derivative.T @ (weights[:, None] * derivative)
    return weights, derivative, stiffness


def element_tables():
    weights, derivative, stiffness = gll_one_d()
    identity = np.eye(SIDE)
    mass_weights = np.kron(weights, weights)
    return (
        np.kron(np.diag(weights), stiffness),
        np.kron(stiffness, np.diag(weights)),
        mass_weights[:, None] * np.kron(identity, derivative),
        mass_weights[:, None] * np.kron(derivative, identity),
        mass_weights,
    )


def fourier_tables(planes):
    plane_grid = np.arange(planes)
    synthesis = np.zeros((planes, planes))
    forward = np.zeros((planes, planes))
    synthesis[:, 0] = 1.0
    synthesis[:, 1] = np.cos(np.pi * plane_grid)
    forward[0] = 1.0 / planes
    forward[1] = np.cos(np.pi * plane_grid) / planes
    for wavenumber in range(1, planes // 2):
        phase_angle = 2.0 * np.pi * wavenumber * plane_grid / planes
        synthesis[:, 2 * wavenumber] = np.cos(phase_angle)
        synthesis[:, 2 * wavenumber + 1] = np.sin(phase_angle)
        forward[2 * wavenumber] = 2.0 * np.cos(phase_angle) / planes
        forward[2 * wavenumber + 1] = 2.0 * np.sin(phase_angle) / planes
    return synthesis, forward


def span_forward(forward):
    turned = np.zeros_like(forward)
    for wavenumber in range(1, forward.shape[0] // 2):
        turned[2 * wavenumber] = span_wave * wavenumber * forward[2 * wavenumber + 1]
        turned[2 * wavenumber + 1] = -span_wave * wavenumber * forward[2 * wavenumber]
    return turned


def two_parts(table):
    table = np.asarray(table, np.float32)
    high = table.astype(jnp.bfloat16)
    low = (table - high.astype(np.float32)).astype(jnp.bfloat16)
    return high, low


def placement(row, skip_shared):
    table = np.zeros((SIDE * SIDE, LANES))
    for j in range(SIDE):
        if skip_shared and row == 1 and j == 0:
            continue
        for i in range(SIDE):
            table[SIDE * j + i, ROWS * i + 6 * row + j] = 1.0
    return table


def column_tables():
    stiff_along, stiff_across, slope_along, slope_across, mass_weights = element_tables()
    matrices = []
    for table in (slope_along, slope_across, stiff_along, stiff_across):
        for row in range(2):
            place = placement(row, False)
            matrices.append(place.T @ table.T @ place)
    for start in (FIRST, SECOND):
        matrix = np.zeros((LANES, LANES))
        for at in range(SHARE):
            matrix[SPEED + at, start + at] = 1.0
        matrices.append(matrix)
    masses = [mass_weights @ placement(row, False) for row in range(2)]
    return np.stack(matrices).astype(np.float32), np.stack(masses).astype(np.float32)


def split_two(value):
    high = value.astype(jnp.bfloat16)
    low = (value - high.astype(jnp.float32)).astype(jnp.bfloat16)
    return high, low


def split_three(value):
    high = value.astype(jnp.bfloat16)
    rest = value - high.astype(jnp.float32)
    middle = rest.astype(jnp.bfloat16)
    low = (rest - middle.astype(jnp.float32)).astype(jnp.bfloat16)
    return high, middle, low


def dot(left, right):
    return jnp.dot(left, right, preferred_element_type=jnp.float32)


def dot_split(left, right):
    return dot(left[0], right[0]) + (dot(left[0], right[1]) + dot(left[1], right[0]))


def one_hot(ids_row, count):
    rows = lax.broadcasted_iota(jnp.int32, (count, LANES), 0)
    return jnp.where(rows == ids_row, 1.0, 0.0).astype(jnp.bfloat16)


def element_order(element_ids, own_nodes):
    wide = (element_ids.shape[0], LANES)
    first_corner = jnp.broadcast_to(element_ids[:, 0:1], wide)
    last_corner = jnp.broadcast_to(element_ids[:, SIDE - 1 : SIDE], wide)
    picked = [
        jnp.where(first_corner == float(own_nodes + 6 * row), 1.0, 0.0) for row in range(2)
    ]
    order = [picked]
    for _ in range(COLS - 1):
        corners = [jnp.sum(last_corner * mask, axis=0, keepdims=True) for mask in picked]
        picked = [jnp.where(first_corner == corner, 1.0, 0.0) for corner in corners]
        order.append(picked)
    return order


def gather_kernel(
    plane_ref, connect_hbm, place_hbm, velocity_hbm,
    slot_a, slot_b, slot_c, slot_d, ids_ref,
    connect_ref, place_ref, velocity_ref, arrived,
):
    slots = (slot_a, slot_b, slot_c, slot_d)
    sources = (connect_hbm, place_hbm, velocity_hbm)
    targets = (connect_ref, place_ref, velocity_ref)
    copies = [
        pltpu.make_async_copy(source, target, arrived.at[at])
        for at, (source, target) in enumerate(zip(sources, targets))
    ]
    for copy in copies:
        copy.start()
    own_nodes = velocity_ref.shape[1]
    modes = velocity_ref.shape[0] // 3
    lane = lax.broadcasted_iota(jnp.int32, (1, LANES), 1)
    plane = plane_ref[0]
    copies[0].wait()
    element_ids = connect_ref[...].astype(jnp.float32)
    order = element_order(element_ids, own_nodes)
    ids_parts = split_two(element_ids)
    copies[1].wait()
    placed = [dot(ids_parts[0], place_ref[r]) + dot(ids_parts[1], place_ref[r]) for r in range(2)]
    rows = []
    for column in range(COLS):
        picked = order[column]
        ids = jnp.sum(placed[0] * picked[0] + placed[1] * picked[1], axis=0, keepdims=True)
        rows.append(jnp.where(lane < GRID, ids.astype(jnp.int32), -1))
    kept = [jnp.where(lane >= ROWS, ids, -1) for ids in rows]
    ids_ref[...] = jnp.concatenate(kept + [jnp.full((8 - COLS, LANES), -1, jnp.int32)], axis=0)
    last = jnp.broadcast_to(rows[COLS - 1].astype(jnp.float32), (8, LANES))
    for column in range(COLS):
        count = min(SHARE, ROWS - SHARE * column)
        taken = pltpu.roll(last, SPEED - 6 * ROWS - SHARE * column, 1)[0:1, :].astype(jnp.int32)
        rows[column] = jnp.where((lane >= SPEED) & (lane < SPEED + count), taken, rows[column])
    chosen = []
    for slot in range(COLS):
        ids = rows[0]
        for column in range(1, COLS):
            ids = jnp.where((plane ^ slot) == column, rows[column], ids)
        chosen.append(one_hot(ids, own_nodes))
    copies[2].wait()
    both = dot(
        jnp.concatenate(split_two(velocity_ref[...]), axis=0), jnp.concatenate(chosen, axis=1)
    )
    both = both[: 3 * modes, :] + both[3 * modes :, :]
    tile_lane = lax.broadcasted_iota(jnp.int32, (modes, LANES), 1)
    quarter = modes // 4
    for slot in range(COLS):
        values = both[:, slot * LANES : (slot + 1) * LANES]
        last = values[2 * modes :, :]
        for c in range(2):
            slots[slot][c * modes : (c + 1) * modes, :] = jnp.where(
                tile_lane < TAKEN,
                values[c * modes : (c + 1) * modes, :],
                pltpu.roll(last, TAKEN - c * ROOM, 1),
            )
        rest = pltpu.roll(last[:quarter, :], LANES - 2 * ROOM, 1)
        for part in range(1, 4):
            rest = jnp.where(
                tile_lane[:quarter, :] < part * QUARTER,
                rest,
                pltpu.roll(
                    last[part * quarter : (part + 1) * quarter, :],
                    (part * QUARTER - 2 * ROOM) % LANES,
                    1,
                ),
            )
        slots[slot][2 * modes :, :] = rest


def three_of(slot, modes):
    lower, upper, rest = slot[:modes, :], slot[modes : 2 * modes, :], slot[2 * modes :, :]
    lane = lax.broadcasted_iota(jnp.int32, (modes, LANES), 1)
    spread = [pltpu.roll(rest, (2 * ROOM - part * QUARTER) % LANES, 1) for part in range(4)]
    last = jnp.where(
        lane < ROOM,
        pltpu.roll(lower, ROOM, 1),
        jnp.where(
            lane < 2 * ROOM, pltpu.roll(upper, 2 * ROOM, 1), jnp.concatenate(spread, axis=0)
        ),
    )
    return jnp.concatenate([lower, upper, last], axis=1)


def setup_kernel(
    own_nodes, plane_at, connect_hbm, extents_hbm, fourier_hbm, plane_hbm, mass_hbm,
    fourier_ref, in_plane_ref, row_ref,
    connect_ref, extents_ref, plane_ref, mass_ref, arrived,
):
    sources = (connect_hbm, extents_hbm, mass_hbm, plane_hbm, fourier_hbm)
    targets = (connect_ref, extents_ref, mass_ref, plane_ref, fourier_ref)
    copies = [
        pltpu.make_async_copy(source, target, arrived.at[at])
        for at, (source, target) in enumerate(zip(sources, targets))
    ]
    for copy in copies:
        copy.start()
    for copy in copies[:3]:
        copy.wait()
    element_ids = connect_ref[...].astype(jnp.float32)
    elements = element_ids.shape[0]
    order = element_order(element_ids, own_nodes)
    lane = lax.broadcasted_iota(jnp.int32, (1, LANES), 1)
    diagonal = lax.broadcasted_iota(jnp.int32, (elements, elements), 0) == lax.broadcasted_iota(
        jnp.int32, (elements, elements), 1
    )
    held = []
    for axis in range(2):
        lengths = jnp.sum(
            jnp.where(diagonal, extents_ref[axis : axis + 1, :], 0.0), axis=1, keepdims=True
        )
        for row in range(2):
            mask = order[0][row]
            for column in range(1, COLS):
                mask = jnp.where(plane_at[0] == column, order[column][row], mask)
            held.append(jnp.sum(lengths * mask, axis=0, keepdims=True))
    hx, hy = held[:2], held[2:]
    carried = jnp.zeros((1, LANES), jnp.float32)
    for at, value in enumerate(held):
        carried = carried + jnp.where(lane == WHOLE + at, value, 0.0)
    mass = sum((hx[r] * hy[r] / 4.0) * mass_ref[r : r + 1, :] for r in range(2))
    row_ref[...] = jnp.concatenate([mass, carried, jnp.zeros((6, LANES), jnp.float32)], axis=0)
    copies[3].wait()
    along = sum((hy[r] / 2.0) * plane_ref[r] for r in range(2)) + plane_ref[8]
    across = sum((hx[r] / 2.0) * plane_ref[2 + r] for r in range(2)) + plane_ref[9]
    stiff = viscosity * sum(
        (hy[r] / hx[r]) * plane_ref[4 + r] + (hx[r] / hy[r]) * plane_ref[6 + r] for r in range(2)
    )
    high, low = split_two(jnp.concatenate([along, across, stiff], axis=0))
    in_plane_ref[0] = high
    in_plane_ref[1] = low
    copies[4].wait()


def residual_kernel(
    modes, plane_at, slot_a, slot_b, slot_c, slot_d, fourier_ref, in_plane_ref, row_ref,
    out_ref, packed_ref,
):
    planes = PLANES
    groups = planes // modes
    for slot, slot_ref in enumerate((slot_a, slot_b, slot_c, slot_d)):
        start = pl.multiple_of((plane_at[0] ^ slot) * modes, modes)
        packed_ref[pl.ds(start, modes), :] = three_of(slot_ref[...], modes)
    packed = packed_ref[...]
    synthesis = (fourier_ref[0, :, :planes], fourier_ref[1, :, :planes])
    forward = (fourier_ref[0, :, planes:], fourier_ref[1, :, planes:])
    physical = dot_split(synthesis, split_two(packed))
    speeds = [packed[:, c * LANES : (c + 1) * LANES] for c in range(3)]
    fields = [physical[:, c * LANES : (c + 1) * LANES] for c in range(3)]
    mass = row_ref[0:1, :]
    carried = row_ref[1:2, :]
    products = [[fields[a] * fields[c] for a in range(3)] for c in range(3)]
    lane = lax.broadcasted_iota(jnp.int32, (planes, LANES), 1)
    in_plane = (in_plane_ref[0], in_plane_ref[1])
    divergence = [
        dot_split(
            split_two(jnp.concatenate([products[c][0], products[c][1], fields[c]], axis=1)),
            in_plane,
        )
        for c in range(3)
    ]
    divergence[1] = jnp.where(
        (lane >= FIRST) & (lane < SECOND),
        pltpu.roll(products[2][2], FIRST - SPEED, 1),
        divergence[1],
    )
    upper = split_two(jnp.concatenate(divergence, axis=1))
    lower = split_two(jnp.concatenate([mass * products[c][2] for c in range(3)], axis=1))
    result = dot_split((forward[0][:, :planes], forward[1][:, :planes]), upper) + dot_split(
        (forward[0][:, planes:], forward[1][:, planes:]), lower
    )
    mode = lax.broadcasted_iota(jnp.int32, (planes, LANES), 0)
    wave = span_wave * jnp.where(mode == 1, planes // 2, mode // 2).astype(jnp.float32)
    square = wave * wave
    tiles = []
    for c in range(3):
        tile = result[:, c * LANES : (c + 1) * LANES] - square * (mass * speeds[c])
        tiles.append(jnp.where((lane >= SPEED) & (lane < FIRST), speeds[c], tile))
    beside = lane >= KEPT
    tiles[0] = jnp.where(beside, pltpu.roll(tiles[2], KEPT - WHOLE, 1), tiles[0])
    tiles[1] = jnp.where(beside, pltpu.roll(tiles[2], KEPT - WHOLE - SPLIT, 1), tiles[1])
    tiles[2] = jnp.where(lane < WHOLE, tiles[2], carried)
    blocks = planes // 8
    per_group = modes // 8
    left = lax.broadcasted_iota(jnp.int32, (8, LANES), 1) < LANES // 2
    for block in range(blocks):
        start = CHUNK * ((block % per_group) * groups + block // per_group)
        rows = slice(8 * block, 8 * block + 8)
        out_ref[start : start + 8, :] = tiles[0][rows, :]
        out_ref[start + 8 : start + 16, :] = tiles[1][rows, :]
        last = tiles[2][rows, :]
        last = jnp.where(left, last, pltpu.roll(pltpu.roll(last, LANES // 2, 1), 4, 0))
        out_ref[start + 16 : start + 20, :] = last[0:4, :]


def apply_line(stiffness, values):
    even = [values[k] + values[6 - k] for k in range(3)] + [values[3]]
    odd = [values[k] - values[6 - k] for k in range(3)]
    result = [None] * 7
    for i in range(4):
        total = float(stiffness[i, 3]) * even[3]
        for k in range(3):
            total = total + float((stiffness[i, k] + stiffness[i, 6 - k]) / 2) * even[k]
        if i == 3:
            result[3] = total
            continue
        other = float((stiffness[i, 0] - stiffness[i, 6]) / 2) * odd[0]
        for k in range(1, 3):
            other = other + float((stiffness[i, k] - stiffness[i, 6 - k]) / 2) * odd[k]
        result[i] = total + other
        result[6 - i] = total - other
    return result


def cg_kernel(
    columns, first_ref, in_ref,
    out_ref, grid_ref, turn_ref, rest_ref, image_ref, way_ref,
):
    weights, derivative, stiffness = gll_one_d()
    lane = lax.broadcasted_iota(jnp.int32, (8, LANES), 1)
    at = lane % columns

    def node(i, y):
        start = (ROWS * i + y) * 8
        return slice(start, start + 8)

    def from_next(value):
        return jnp.where(
            at == columns - 1,
            pltpu.roll(value, columns - 1, 1),
            pltpu.roll(value, LANES - 1, 1),
        )

    def from_previous(value):
        return jnp.where(
            at == 0,
            pltpu.roll(value, LANES - columns + 1, 1),
            pltpu.roll(value, 1, 1),
        )

    same = (
        lax.broadcasted_iota(jnp.int32, (LANES, LANES), 0) // columns
        == lax.broadcasted_iota(jnp.int32, (LANES, LANES), 1) // columns
    )
    ones = jnp.where(same, 1.0, 0.0).astype(jnp.bfloat16)

    def tree(values):
        return (values[0] + values[1]) + (values[2] + values[3]) + (values[4] + values[5])

    def over_columns(value):
        value = jnp.where(value == value, value, 0.0)
        parts = [part.astype(jnp.float32) for part in split_three(value)]
        sums = dot(jnp.concatenate(parts, axis=0).astype(jnp.bfloat16), ones)
        return sums[0:8, :] + (sums[8:16, :] + sums[16:24, :])

    blank = jnp.zeros((LANES - 3 * columns, LANES), jnp.float32)
    for mode in range(8):
        rows = [in_ref[pl.ds(start + mode, columns, stride=CHUNK), :] for start in (0, 8)]
        last = in_ref[pl.ds(16 + mode % 4, columns, stride=CHUNK), :]
        if mode == 0:
            turn_ref[...] = jnp.concatenate([last] * (LANES // columns), axis=0).T
        if mode >= 4:
            last = pltpu.roll(last, LANES // 2, 1)
        rows.append(last)
        turned = jnp.concatenate(rows + [blank], axis=0).T
        grid_ref[pl.ds(mode, LANES, stride=8), :] = turned

    def extent(which):
        at = WHOLE + which
        return jnp.broadcast_to(turn_ref[at : at + 1, :], (8, LANES))

    hx = [extent(0), extent(1)]
    hy = [extent(2), extent(3)]
    mode = first_ref[0] + lax.broadcasted_iota(jnp.int32, (8, LANES), 0)
    wave = span_wave * jnp.where(mode == 1, PLANES // 2, mode // 2).astype(jnp.float32)
    pair_wave = span_wave * (mode // 2).astype(jnp.float32)
    helmholtz = inverse_step + wave * wave
    ratio_along = [hy[r] / hx[r] for r in range(2)]
    ratio_across = [hx[r] / hy[r] for r in range(2)]
    mass = [helmholtz * (hx[r] * hy[r] / 4.0) for r in range(2)]

    def over_rows(pair, y):
        if y < 6:
            return float(weights[y]) * pair[0]
        if y > 6:
            return float(weights[y - 6]) * pair[1]
        return float(weights[6]) * pair[0] + float(weights[0]) * pair[1]

    def shared(pair):
        return [
            float(weights[0]) * value + float(weights[6]) * from_previous(value) for value in pair
        ]

    mass_shared = shared(mass)
    across_shared = shared(ratio_across)

    group = lane // columns

    def sent(at_lane):
        value = grid_ref[at_lane * 8 : at_lane * 8 + 8, :]
        if at_lane < WHOLE:
            return value
        by = 2 if at_lane < WHOLE + SPLIT else 1
        row = (at_lane + KEPT - WHOLE - (2 - by) * SPLIT) * 8
        beside = pltpu.roll(grid_ref[row : row + 8, :], by * columns, 1)
        return jnp.where(group == 2, beside, value)

    def handed(start, y):
        value = sent(start + y % SHARE)
        by = COLS - y // SHARE
        return jnp.where(
            at < by, pltpu.roll(value, LANES - columns + by, 1), pltpu.roll(value, by, 1)
        )

    at_first = at % COLS == 0

    def masked(pair):
        return [jnp.where(at_first, value, 0.0) for value in pair]

    first_speed = [handed(SPEED, y) for y in range(ROWS)]
    first = [handed(FIRST, y) for y in range(ROWS)]
    second = [handed(SECOND, y) for y in range(ROWS)]
    half_x = masked([0.5 * value for value in hx])
    half_y = masked([0.5 * value for value in hy])
    area = masked([0.25 * hx[r] * hy[r] for r in range(2)])
    edge_along = masked(ratio_along)
    edge_across = masked(ratio_across)
    sloped = weights[:, None] * derivative
    lines = [jnp.zeros((8, LANES), jnp.float32)] * ROWS
    for r in range(2):
        rows = range(6 * r, 6 * r + SIDE)
        curved = apply_line(stiffness, [first_speed[y] for y in rows])
        for j, y in enumerate(rows):
            slope = sum(float(sloped[j, k]) * second[6 * r + k] for k in range(SIDE))
            lines[y] = lines[y] + float(weights[0]) * (
                half_x[r] * slope - edge_across[r] * curved[j]
            )
    even = mode % 2 == 0
    total = jnp.zeros((8, LANES), jnp.float32)
    for y in range(ROWS):
        along = jnp.where(group == 1, pltpu.roll(second[y], columns, 1), first[y])
        span = jnp.where(
            group == 0,
            pltpu.roll(first[y], 2 * columns, 1),
            jnp.where(
                group == 1,
                pltpu.roll(second[y], LANES - columns, 1),
                pltpu.roll(first[y], columns, 1),
            ),
        )
        span = jnp.where(even, pltpu.roll(span, 7, 0), -pltpu.roll(span, 1, 0))
        across = lines[y] + float(weights[0]) * over_rows(area, y) * (
            pair_wave * span - (wave * wave) * first_speed[y]
        )
        flux = over_rows(half_y, y) * along
        speed = over_rows(edge_along, y) * first_speed[y]
        values = [
            sent(ROWS * i + y)
            + float(sloped[i, 0]) * flux
            - float(stiffness[i, 0]) * speed
            for i in range(SIDE)
        ]
        values[0] = values[0] + across + from_previous(values[6])
        for i in range(6):
            value = values[i]
            rest_ref[node(i, y), :] = value
            way_ref[0, node(i, y), :] = value
            total = total + value * value
    rest_norm = over_columns(total)

    def apply(iteration, turn):
        for y in range(ROWS):
            values = []
            for i in range(6):
                value = rest_ref[node(i, y), :]
                if iteration:
                    value = value + turn * way_ref[iteration - 1, node(i, y), :]
                    way_ref[iteration, node(i, y), :] = value
                values.append(value)
            values.append(from_next(values[0]))
            lines = apply_line(stiffness, values)
            along = over_rows(ratio_along, y)
            lines = [along * line for line in lines]
            lines[0] = lines[0] + from_previous(lines[6])
            inner = over_rows(mass, y)
            inner = [None] + [float(weights[i]) * inner for i in range(1, 4)]
            inner = [over_rows(mass_shared, y)] + inner[1:] + [inner[2], inner[1]]
            for i in range(6):
                image_ref[node(i, y), :] = lines[i] + inner[i] * values[i]
        totals = [jnp.zeros((8, LANES), jnp.float32)] * 6
        for i in range(6):
            values = [way_ref[iteration, node(i, y), :] for y in range(ROWS)]
            lower = apply_line(stiffness, values[:7])
            upper = apply_line(stiffness, values[6:])
            if i == 0:
                scale = across_shared
            else:
                scale = [float(weights[i]) * value for value in ratio_across]
            lower = [scale[0] * value for value in lower]
            upper = [scale[1] * value for value in upper]
            lines = lower[:6] + [lower[6] + upper[0]] + upper[1:]
            for y in range(ROWS):
                image = image_ref[node(i, y), :] + lines[y]
                image_ref[node(i, y), :] = image
                totals[y % 6] = totals[y % 6] + values[y] * image
        return over_columns(tree(totals))

    turn = None
    sizes = []
    for iteration in range(ITERS):
        size = rest_norm / apply(iteration, turn)
        sizes.append(size)
        if iteration == ITERS - 1:
            break
        totals = [jnp.zeros((8, LANES), jnp.float32)] * 6
        for y in range(ROWS):
            for i in range(6):
                rest = rest_ref[node(i, y), :] - size * image_ref[node(i, y), :]
                rest_ref[node(i, y), :] = rest
                totals[i] = totals[i] + rest * rest
        following = over_columns(tree(totals))
        turn = following / rest_norm
        rest_norm = following
    zero = jnp.zeros((8, LANES), jnp.float32)
    for y in range(ROWS):
        grid_ref[node(0, y), :] = zero
        for i in range(6):
            value = sizes[0] * way_ref[0, node(i, y), :]
            for step in range(1, ITERS):
                value = value + sizes[step] * way_ref[step, node(i, y), :]
            if i == 0:
                grid_ref[node(6, y), :] = from_next(value)
            else:
                grid_ref[node(i, y), :] = value
    for left in range(GRID, LANES):
        grid_ref[left * 8 : left * 8 + 8, :] = zero
    parts = columns // COLS
    node_lane = lax.broadcasted_iota(jnp.int32, (3 * parts, LANES), 1)
    owned = (node_lane >= ROWS) & (node_lane < GRID)
    rest_from = LANES - ROWS - SPARE
    for mode in range(8):
        turn_ref[...] = grid_ref[pl.ds(mode, LANES, stride=8), :].T
        pieces = [turn_ref[pl.ds(k, 3 * parts, stride=COLS), :] for k in range(COLS)]
        for k in range(2):
            tile = jnp.where(owned, pieces[k], pltpu.roll(pieces[k + 2], OWNED, 1))
            for c in range(3):
                out_ref[pl.ds(24 * k + 8 * c + mode, parts, stride=64), :] = tile[
                    c * parts : (c + 1) * parts, :
                ]
        rest = jnp.where(
            node_lane < REST,
            pltpu.roll(pieces[2], rest_from, 1),
            pltpu.roll(pieces[3], rest_from + REST, 1),
        )
        rest = [rest[c * parts : (c + 1) * parts, :] for c in range(3)]
        both = jnp.where(
            node_lane[:parts, :] < LANES // 2, rest[0], pltpu.roll(rest[1], LANES // 2, 1)
        )
        out_ref[pl.ds(48 + mode, parts, stride=64), :] = both
        out_ref[pl.ds(56 + mode, parts, stride=64), :] = rest[2]


def choice_kernel(ids_ref, out_ref):
    nodes = lax.broadcasted_iota(jnp.int32, (LANES, out_ref.shape[1]), 1)
    for column in range(COLS):
        ids = jnp.broadcast_to(ids_ref[column : column + 1, :].astype(jnp.float32), (LANES, LANES))
        ids = ids.T[:, 0:1].astype(jnp.int32)
        out_ref[column * LANES : (column + 1) * LANES, :] = jnp.where(
            nodes == ids, 1.0, 0.0
        ).astype(jnp.bfloat16)


def scatter_kernel(velocity_ref, change_ref, chosen_ref, out_ref):
    rows = velocity_ref.shape[0]
    sources = change_ref.shape[0]
    def tiles(start):
        return jnp.concatenate(
            [change_ref[m, start : start + 8, :] for m in range(sources)], axis=0
        )

    lane = lax.broadcasted_iota(jnp.int32, (8 * sources, LANES), 1)
    pieces = []
    shared, single = tiles(48), tiles(56)
    for c in range(3):
        held = [tiles(24 * k + 8 * c) for k in range(2)]
        rest, skip = (single, 0) if c == 2 else (shared, c * (LANES // 2))
        for k in range(2):
            moved = pltpu.roll(rest, (ROWS + SPARE - k * REST - skip) % LANES, 1)
            held.append(jnp.where(lane < ROWS + SPARE, pltpu.roll(held[k], SPARE, 1), moved))
        pieces.append(jnp.concatenate(held, axis=1))
    parts = jnp.concatenate(split_two(jnp.concatenate(pieces, axis=0)), axis=0)
    change = dot(parts, chosen_ref[...])
    out_ref[...] = velocity_ref[...] + (change[:rows, :] + change[rows:, :])


def call(kernel, out_shape, scratch=(), spaces="", cost=None):
    place = {
        "s": pl.BlockSpec(memory_space=pltpu.SMEM),
        "v": pl.BlockSpec(memory_space=pltpu.VMEM),
        "h": pl.BlockSpec(memory_space=pltpu.HBM),
    }
    many = isinstance(out_shape, tuple)
    run = pl.pallas_call(
        kernel,
        out_shape=out_shape,
        in_specs=[place[space] for space in spaces],
        out_specs=(place["v"],) * len(out_shape) if many else place["v"],
        scratch_shapes=list(scratch),
        cost_estimate=cost,
        compiler_params=pltpu.CompilerParams(vmem_limit_bytes=16 * 2**20),
    )

    def with_spaces(*operands):
        return run(
            *(
                pltpu.with_memory_space_constraint(operand, pltpu.HBM) if space == "h" else operand
                for space, operand in zip(spaces, operands)
            )
        )

    return with_spaces


def transposed(velocity, connect, right_list, extents):
    components, modes, own_nodes = velocity.shape
    groups = lax.axis_size("planes")
    parts = lax.axis_size("mesh")
    plane = lax.axis_index("planes")
    part = lax.axis_index("mesh")
    rows = components * modes
    columns = parts * COLS
    synthesis, forward = fourier_tables(PLANES)
    forward = np.concatenate([forward, span_forward(forward)], axis=1) * (-1.0 / viscosity)
    fourier = np.stack(two_parts(np.concatenate([synthesis, forward], axis=1)))
    matrices, masses = column_tables()
    place = np.stack([placement(row, True) for row in range(2)])
    flat = velocity.reshape(rows, own_nodes)
    f32 = jnp.float32
    slot_shape = jax.ShapeDtypeStruct((modes * 9 // 4, LANES), f32)
    *slots, ids = call(
        gather_kernel,
        (slot_shape,) * COLS + (jax.ShapeDtypeStruct((8, LANES), jnp.int32),),
        scratch=(
            pltpu.VMEM(connect.shape[::-1], jnp.int32),
            pltpu.VMEM(place.shape, jnp.bfloat16),
            pltpu.VMEM((rows, own_nodes), f32),
            pltpu.SemaphoreType.DMA((3,)),
        ),
        spaces="shhh",
    )(plane.reshape(1), connect.T, jnp.asarray(place, jnp.bfloat16), flat)
    for s in reversed(range(1, groups)):
        slots[s] = lax.ppermute(slots[s], "planes", [(p, p ^ s) for p in range(groups)])
    tables = call(
        functools.partial(setup_kernel, own_nodes),
        (
            jax.ShapeDtypeStruct(fourier.shape, jnp.bfloat16),
            jax.ShapeDtypeStruct((2, 3 * LANES, LANES), jnp.bfloat16),
            jax.ShapeDtypeStruct((8, LANES), f32),
        ),
        scratch=(
            pltpu.VMEM(connect.shape[::-1], jnp.int32),
            pltpu.VMEM(extents.shape, f32),
            pltpu.VMEM(matrices.shape, f32),
            pltpu.VMEM(masses.shape, f32),
            pltpu.SemaphoreType.DMA((5,)),
        ),
        spaces="shhhhh",
        cost=pl.CostEstimate(flops=10**6, bytes_accessed=3 * 10**6, transcendentals=0),
    )(
        plane.reshape(1), connect.T, extents,
        jnp.asarray(fourier), jnp.asarray(matrices), jnp.asarray(masses),
    )
    chosen = call(
        choice_kernel,
        jax.ShapeDtypeStruct((COLS * LANES, own_nodes), jnp.bfloat16),
        spaces="v",
        cost=pl.CostEstimate(flops=10**6, bytes_accessed=10**6, transcendentals=0),
    )(ids)
    tables, chosen = lax.optimization_barrier((tables, chosen))
    residual = call(
        functools.partial(residual_kernel, modes),
        jax.ShapeDtypeStruct((columns * CHUNK, LANES), f32),
        scratch=(pltpu.VMEM((PLANES, 3 * LANES), f32),),
        spaces="svvvvvvv",
    )(plane.reshape(1), *slots, *tables)
    residual = lax.all_to_all(
        residual.reshape(columns * CHUNK, 1, LANES),
        ("mesh", "planes"),
        split_axis=0,
        concat_axis=0,
        tiled=True,
    )
    held = pltpu.VMEM((96 * 8, LANES), f32)
    change = call(
        functools.partial(cg_kernel, columns),
        jax.ShapeDtypeStruct((parts * 64, LANES), f32),
        scratch=(pltpu.VMEM((LANES * 8, LANES), f32), pltpu.VMEM((LANES, LANES), f32))
        + (held, held, pltpu.VMEM((ITERS, 6 * ROWS * 8, LANES), f32)),
        spaces="sv",
    )((plane * modes + part * 8).reshape(1), residual.reshape(columns * CHUNK, LANES))
    change = lax.all_to_all(
        change.reshape(parts, 64, LANES), "mesh", split_axis=0, concat_axis=0, tiled=True
    )
    result = call(scatter_kernel, jax.ShapeDtypeStruct((rows, own_nodes), f32), spaces="vvv")(
        flat, change, chosen
    )
    return result.reshape(velocity.shape)


def from_behind(value, axis, by):
    peers = lax.axis_size(axis)
    return lax.ppermute(value, axis, [(i, (i + by) % peers) for i in range(peers)])


def partitioned(velocity, connect, right_list, extents):
    components, modes, own_nodes = velocity.shape
    edge_count = right_list.shape[0]
    first_mode = lax.axis_index("planes") * modes
    tables = [jnp.asarray(table, jnp.float32) for table in element_tables()]
    stiff_along, stiff_across, slope_along, slope_across, mass_weights = tables
    synthesis, forward = (jnp.asarray(t, jnp.float32) for t in fourier_tables(PLANES))
    hx, hy = extents[0], extents[1]
    mass_full = mass_weights[:, None] * (hx * hy / 4.0)[None, :]
    index_list = first_mode + jnp.arange(modes, dtype=jnp.int32)
    wave = span_wave * jnp.where(index_list == 1, PLANES // 2, index_list // 2).astype(jnp.float32)
    wave = wave[None, :, None, None]
    helmholtz = inverse_step + wave * wave
    locals_ = jnp.arange(own_nodes + edge_count, dtype=jnp.int32)
    chosen = (locals_[:, None, None] == connect[None]).astype(jnp.float32)
    at_edge = (locals_[:own_nodes, None] == right_list[None]).astype(jnp.float32)

    def contract(spec, *operands):
        return jnp.einsum(spec, *operands, precision=highest)

    physical = contract(
        "jq,cqn->cjn",
        synthesis,
        lax.all_to_all(velocity, "planes", split_axis=2, concat_axis=1, tiled=True),
    )
    pairs = ((0, 0), (0, 1), (0, 2), (1, 1), (1, 2), (2, 2))
    products = jnp.stack([physical[a] * physical[b] for a, b in pairs])
    product_hat = lax.all_to_all(
        contract("qj,fjn->fqn", forward, products), "planes", split_axis=1, concat_axis=2, tiled=True
    )

    def spread(fields):
        ghosts = from_behind(contract("cqn,ny->cqy", fields, at_edge), "mesh", 1)
        return contract("cqn,nke->cqke", jnp.concatenate([fields, ghosts], axis=2), chosen)

    def assemble(terms):
        summed = contract("cqke,nke->cqn", terms, chosen)
        returned = from_behind(summed[:, :, own_nodes:], "mesh", -1)
        return summed[:, :, :own_nodes] + contract("cqy,ny->cqn", returned, at_edge)

    def stiffness(values):
        return (hy / hx) * contract("lk,cqke->cqle", stiff_along, values) + (hx / hy) * contract(
            "lk,cqke->cqle", stiff_across, values
        )

    def dots(left, right):
        return lax.psum(jnp.sum(left * right, axis=2), "mesh")

    values = spread(jnp.concatenate([velocity, product_hat], axis=0))
    speeds, along = values[0:3], values[3:6]
    across = jnp.stack([values[4], values[6], values[7]])
    span = jnp.stack([values[5], values[7], values[8]])
    shaped = span.reshape(span.shape[0], modes // 2, 2, *span.shape[2:])
    turned = jnp.stack([shaped[:, :, 1], -shaped[:, :, 0]], axis=2).reshape(span.shape)
    pair_wave = span_wave * (index_list // 2).astype(jnp.float32)[None, :, None, None]
    advection = (hy / 2.0) * contract("lk,cqke->cqle", slope_along, along)
    advection = advection + (hx / 2.0) * contract("lk,cqke->cqle", slope_across, across)
    advection = advection + mass_full * (pair_wave * turned)
    residual = assemble(
        -(wave * wave) * mass_full * speeds - stiffness(speeds) - advection / viscosity
    )
    solution = velocity
    direction = residual
    norm_now = dots(residual, residual)
    for _ in range(ITERS):
        values = spread(direction)
        operated = assemble(stiffness(values) + helmholtz * mass_full * values)
        step_size = (norm_now / dots(direction, operated))[:, :, None]
        solution = solution + step_size * direction
        residual = residual - step_size * operated
        norm_next = dots(residual, residual)
        direction = residual + (norm_next / norm_now)[:, :, None] * direction
        norm_now = norm_next
    return solution


def on_device(velocity, connect, right_list, extents):
    groups = lax.axis_size("planes")
    parts = lax.axis_size("mesh")
    modes = velocity.shape[1]
    fits = groups == COLS and modes == 8 * parts and 3 * parts * COLS <= LANES
    step = transposed if fits else partitioned
    return step(velocity, connect, right_list, extents)


def solution(mesh):
    placed = (P(None, "planes", "mesh"), P(None, "mesh"), P("mesh"), P(None, "mesh"))
    return jax.shard_map(
        on_device, mesh=mesh, in_specs=placed, out_specs=P(None, "planes", "mesh"), check_vma=False
    )
```
